32 devices in a mesh: blk: 8 (over z, y), uly: 4 (over x, core).
Axes of the slice: x: 2, y: 2, z: 4, core: 2. Of those that a mesh axis runs over, the one named last changes fastest.
Arguments:
- tokens: bfloat16 [6400, 1024], P(('blk', 'uly')), may hold values from -6 to 6
- cotangent: bfloat16 [6400, 1024], P(('blk', 'uly')), may hold values from -6 to 6
- noise_embed: bfloat16 [64, 1024], P(('blk', 'uly')), may hold values from -6 to 6
- frame_clip: int32 [64], replicated, may hold values from 0 to 8, as said below
- frame_index: int32 [64], replicated, may hold values from 0 to 31, as said below
- mod_weight: bfloat16 [1024, 6144], replicated, may hold values from -0.1875 to 0.1875
- mod_bias: bfloat16 [6144], replicated, may hold values from -3 to 3
- attn_weight: bfloat16 [1024, 3072], replicated, may hold values from -0.1875 to 0.1875
- attn_bias: bfloat16 [3072], replicated, may hold values from -3 to 3
- proj_weight: bfloat16 [1024, 1024], replicated, may hold values from -3 to 3
- proj_bias: bfloat16 [1024], replicated, may hold values from -3 to 3
- up_weight: bfloat16 [1024, 4096], replicated, may hold values from -0.1875 to 0.1875
- up_bias: bfloat16 [4096], replicated, may hold values from -3 to 3
- down_weight: bfloat16 [4096, 1024], replicated, may hold values from -0.09375 to 0.09375
- down_bias: bfloat16 [1024], replicated, may hold values from -3 to 3
Outputs:
- output: bfloat16 [6400, 1024], P(('blk', 'uly'))
- token_grad: float32 [6400, 1024], P(('blk', 'uly'))
- grad_mod_weight: float32 [1024, 6144], P(('blk', 'uly'))
- grad_mod_bias: float32 [6144], P(('blk', 'uly'))
- grad_attn_weight: float32 [1024, 3072], P(('blk', 'uly'))
- grad_attn_bias: float32 [3072], P(('blk', 'uly'))
- grad_proj_weight: float32 [1024, 1024], P(('blk', 'uly'))
- grad_proj_bias: float32 [1024], P(('blk', 'uly'))
- grad_up_weight: float32 [1024, 4096], P(('blk', 'uly'))
- grad_up_bias: float32 [4096], P(('blk', 'uly'))
- grad_down_weight: float32 [4096, 1024], P(('blk', 'uly'))
- grad_down_bias: float32 [1024], P(('blk', 'uly'))
The draws below stay inside these ranges and needn't reach their ends.
Inputs may be any that keep to these rules, and one draw needn't show every extreme that they name: `frame_clip`: block b holds frames b * 8 to (b + 1) * 8 - 1. Of these, 4 consecutive frames, either the first or the last ones of the block, form one short clip with id b, and the other 4 frames belong to the one long clip, whose id is the number of blocks and which has frames in every block, 32 in all. `frame_index`: the frame's place within its clip, counting from 0 at the clip's first frame; the long clip's places rise with the frame number.
All inputs are finite; a program needn't handle non-finite values.
Results may differ from the reference program's by a relative error of at most 0.015.
The reference program's roundings to bfloat16 on the way count: a program that leaves them out, or rounds other values in their place, can miss the bound.
Values may be sent and summed in bfloat16 or wider, within the bound.
No kernel may reach another device: no remote copies, remote signals or barrier semaphores. Data moves between devices by JAX's collectives and lax.ppermute only.
A program may use at most 320 MiB of HBM per device.

```python
import math
import jax
import jax.numpy as jnp
from jax import lax

D = 1024
H = 16
DH = 64
FF = 4096
GRID = 10
SHORT_FR = 4
FB = 8
PATCH = 100
BT = 800
FRAMES = 64
TOKENS = 6400
N_BLK = 8


def clip_layout(key):
    flips = jax.random.randint(key, (N_BLK,), 0, 2)
    frame = jnp.arange(FRAMES, dtype=jnp.int32)
    block = frame // FB
    inner = frame % FB
    short_first = flips[block] == 1
    in_short = jnp.where(short_first, inner < SHORT_FR, inner >= SHORT_FR)
    clip = jnp.where(in_short, block, N_BLK)
    place = jnp.where(in_short, inner % SHORT_FR, block * SHORT_FR + inner % SHORT_FR)
    return (clip.astype(jnp.int32), place.astype(jnp.int32))


def draw_frame_clip(key, part):
    return clip_layout(jax.random.fold_in(key, 7))[0]


def draw_frame_index(key, part):
    return clip_layout(jax.random.fold_in(key, 7))[1]


def steps_of(own_key, shape, split, low, top_value):
    def one(axis_at, parts):
        draws = jax.random.uniform(jax.random.fold_in(jax.random.fold_in(own_key, 6), axis_at), (parts,), jnp.float32, low / len(split), top_value / len(split))
        return jnp.repeat(jnp.exp(draws), shape[axis_at] // parts).reshape((-1,) + (1,) * (len(shape) - axis_at - 1))

    loudness = one(*split[0])
    for cut in split[1:]:
        loudness = loudness * one(*cut)
    return loudness


def bell_draw(own_key, dims, width, bound, split=(), kind=jnp.bfloat16):
    loudness = steps_of(own_key, dims, split, -0.22, 0.18) if split else 1.0
    array = jax.random.normal(own_key, dims, jnp.float32) * width * loudness
    return jnp.minimum(jnp.maximum(array, -bound), bound).astype(kind)


def setup_inputs(seed: int = 0) -> dict:
    streams_of = jax.random.split(jax.random.key(seed), 16)
    return {
        "tokens": bell_draw(streams_of[0], (TOKENS, D), 1.0, 6.0, ((0, 32),)),
        "cotangent": bell_draw(streams_of[1], (TOKENS, D), 1.0, 6.0, ((0, 32),)),
        "noise_embed": bell_draw(streams_of[2], (FRAMES, D), 1.0, 6.0, ((0, 32),)),
        "frame_clip": draw_frame_clip(jax.random.fold_in(streams_of[15], 71), 0),
        "frame_index": draw_frame_index(jax.random.fold_in(streams_of[15], 71), 0),
        "mod_weight": bell_draw(streams_of[5], (D, 6 * D), D ** -0.5, 0.1875),
        "mod_bias": bell_draw(streams_of[6], (6 * D,), 0.5, 3.0),
        "attn_weight": bell_draw(streams_of[7], (D, 3 * D), D ** -0.5, 0.1875),
        "attn_bias": bell_draw(streams_of[8], (3 * D,), 0.5, 3.0),
        "proj_weight": bell_draw(streams_of[9], (D, D), (max(1, D // 256)) ** -0.5, 3.0),
        "proj_bias": bell_draw(streams_of[10], (D,), 0.5, 3.0),
        "up_weight": bell_draw(streams_of[11], (D, FF), D ** -0.5, 0.1875),
        "up_bias": bell_draw(streams_of[12], (FF,), 0.5, 3.0),
        "down_weight": bell_draw(streams_of[13], (FF, D), FF ** -0.5, 0.09375),
        "down_bias": bell_draw(streams_of[14], (D,), 0.5, 3.0),
    }


@jax.custom_vjp
def low(v):
    return lax.optimization_barrier(v.astype(jnp.bfloat16)).astype(jnp.float32)

@jax.custom_vjp
def low_back(v):
    return v

def low_keep(v):
    return (low(v), None)

def low_pass(kept, grad):
    return (grad,)

def back_keep(v):
    return (v, None)

def back_low(kept, grad):
    return (low(grad),)
low.defvjp(low_keep, low_pass)
low_back.defvjp(back_keep, back_low)
GELU_C = 0.7978845608028654
GELU_K = 0.044715
NEG_BIG = -1e+30

def layer_norm(values):
    center = values - lax.optimization_barrier(jnp.mean(values, axis=-1, keepdims=True))
    return center * lax.rsqrt(lax.optimization_barrier(jnp.mean(center * center, axis=-1, keepdims=True)) + 1e-06)

def exact_dot(left, right):
    return jnp.dot(left, right, precision=lax.Precision.HIGHEST, preferred_element_type=jnp.float32)

def rope_table(time_pos, row_pos, col_pos):
    half = DH // 2
    n_time = DH // 8
    n_row = 3 * DH // 16
    pair = jnp.arange(half, dtype=jnp.int32)
    in_time = pair < n_time
    in_row = (pair >= n_time) & (pair < n_time + n_row)
    local = jnp.where(in_time, pair, jnp.where(in_row, pair - n_time, pair - n_time - n_row))
    total = jnp.where(in_time, n_time, n_row)
    frequency = jnp.exp(-math.log(10000.0) * local.astype(jnp.float32) / total.astype(jnp.float32))
    place = jnp.where(in_time[None, :], time_pos[:, None], jnp.where(in_row[None, :], row_pos[:, None], col_pos[:, None]))
    angle = place.astype(jnp.float32) * frequency[None, :]
    return (jnp.cos(angle), jnp.sin(angle))

def rotate(values, cosine, sine, sign):
    rows = values.shape[0]
    pairs = values.reshape(rows, -1, DH // 2, 2)
    first = pairs[..., 0]
    second = pairs[..., 1]
    cos_part = cosine[:, None, :]
    sin_part = sign * sine[:, None, :]
    turned = jnp.stack([first * cos_part - second * sin_part, first * sin_part + second * cos_part], axis=-1)
    return turned.reshape(values.shape)

def gelu_tanh(values):
    return 0.5 * values * (1.0 + jnp.tanh(GELU_C * (values + GELU_K * values * values * values)))

def reference(tokens, cotangent, noise_embed, frame_clip, frame_index, mod_weight, mod_bias, attn_weight, attn_bias, proj_weight, proj_bias, up_weight, up_bias, down_weight, down_bias):
    scale = 1.0 / math.sqrt(DH)
    silu_noise = low(jax.nn.silu(noise_embed.astype(jnp.float32)))
    clip_tok = jnp.repeat(frame_clip, PATCH)
    time_tok = jnp.repeat(frame_index, PATCH)
    patch = jnp.arange(TOKENS, dtype=jnp.int32) % PATCH
    cosine, sine = rope_table(time_tok, patch // GRID, patch % GRID)

    def attend(queries, keys, values):
        k_rows = keys.reshape(TOKENS, H, DH)
        v_rows = values.reshape(TOKENS, H, DH)

        def rows_of(which):
            first = which * BT
            q_rows = lax.dynamic_slice_in_dim(queries, first, BT, 0).reshape(BT, H, DH)
            clip_q = lax.dynamic_slice_in_dim(clip_tok, first, BT, 0)
            time_q = lax.dynamic_slice_in_dim(time_tok, first, BT, 0)
            allowed = (clip_q[:, None] == clip_tok[None, :]) & (time_tok[None, :] <= time_q[:, None])
            score = low_back(jnp.einsum('qhd,khd->hqk', q_rows, k_rows, precision=lax.Precision.HIGHEST) * scale)
            score = jnp.where(allowed[None], score, NEG_BIG)
            top = lax.optimization_barrier(jnp.max(score, axis=-1, keepdims=True))
            expo = jnp.exp(score - top)
            prob = expo / lax.optimization_barrier(jnp.sum(expo, axis=-1, keepdims=True))
            mixed = jnp.einsum('hqk,khd->qhd', low(prob), v_rows, precision=lax.Precision.HIGHEST)
            return mixed.reshape(BT, D)
        mixed = lax.map(jax.checkpoint(rows_of), jnp.arange(N_BLK, dtype=jnp.int32))
        return mixed.reshape(TOKENS, D)

    def forward(inputs, w_mod, b_mod, w_attn, b_attn, w_proj, b_proj, w_up, b_up, w_down, b_down):
        mod = exact_dot(silu_noise, w_mod) + b_mod
        pieces = [mod[:, None, j * D:(j + 1) * D] for j in range(6)]
        shift1, scale1, gate1, shift2, scale2, gate2 = pieces
        framed = inputs.reshape(FRAMES, PATCH, D)
        hidden1 = low(layer_norm(framed) * (1.0 + scale1) + shift1).reshape(TOKENS, D)
        qkv = low_back(exact_dot(hidden1, w_attn) + b_attn)
        query = low(rotate(qkv[:, :D], cosine, sine, 1.0))
        key = low(rotate(qkv[:, D:2 * D], cosine, sine, 1.0))
        value = low(qkv[:, 2 * D:])
        attn = low(low_back(attend(query, key, value)))
        branch = low_back(exact_dot(attn, w_proj) + b_proj).reshape(FRAMES, PATCH, D)
        resid = framed + gate1 * branch
        hidden2 = low(layer_norm(resid) * (1.0 + scale2) + shift2).reshape(TOKENS, D)
        pre = low_back(exact_dot(hidden2, w_up) + b_up)
        act = low(gelu_tanh(pre))
        mlp = low_back(exact_dot(act, w_down) + b_down).reshape(FRAMES, PATCH, D)
        return (resid + gate2 * mlp).reshape(TOKENS, D)
    params = (tokens, mod_weight, mod_bias, attn_weight, attn_bias, proj_weight, proj_bias, up_weight, up_bias, down_weight, down_bias)
    params = tuple((p.astype(jnp.float32) for p in params))
    output, pullback = jax.vjp(forward, *params)
    grads = pullback(cotangent.astype(jnp.float32))
    return (output.astype(jnp.bfloat16), grads[0], grads[1], grads[2], grads[3], grads[4], grads[5], grads[6], grads[7], grads[8], grads[9], grads[10])
```

```python
import functools
import math

import jax
import jax.numpy as jnp
import numpy as np
from jax import lax
from jax.experimental import pallas as pl
from jax.experimental.pallas import tpu as pltpu
from jax.sharding import PartitionSpec as P

DH = 64
GRID = 10
FB = 8
PATCH = 100
HALF = 64
LANES = 128

GELU_C = 0.7978845608028654
GELU_K = 0.044715
NEG_BIG = -1e30
MIB = 1 << 20

BF = jnp.bfloat16
F32 = jnp.float32


def round_up(value, step):
    return -(-value // step) * step


def lane_low(shape):
    return lax.broadcasted_iota(jnp.int32, shape, len(shape) - 1) < HALF


def first_frame(shape):
    return lax.broadcasted_iota(jnp.int32, shape, 0) < PATCH


def swap_halves(value):
    return pltpu.roll(value, HALF, 1)


def swap_pairs(value):
    even = lax.broadcasted_iota(jnp.int32, value.shape, 1) % 2 == 0
    return jnp.where(even, pltpu.roll(value, LANES - 1, 1), pltpu.roll(value, 1, 1))


def per_frame(shape, first, second):
    return jnp.where(first_frame(shape), jnp.broadcast_to(first, shape), jnp.broadcast_to(second, shape))


def frame_sums(value):
    head = first_frame(value.shape)
    one = jnp.sum(jnp.where(head, value, 0.0), axis=0, keepdims=True)
    two = jnp.sum(jnp.where(head, 0.0, value), axis=0, keepdims=True)
    return one, two


def norm_rows(values):
    center = values - jnp.mean(values, axis=-1, keepdims=True)
    inv_std = lax.rsqrt(jnp.mean(center * center, axis=-1, keepdims=True) + 1e-06)
    return center * inv_std, inv_std


def norm_back(grad, normed, inv_std):
    return inv_std * (
        grad
        - jnp.mean(grad, axis=-1, keepdims=True)
        - normed * jnp.mean(grad * normed, axis=-1, keepdims=True)
    )


def dot(left, right):
    return jnp.dot(left, right, preferred_element_type=F32)


def dot_lanes(left, right):
    return lax.dot_general(left, right, (((1,), (1,)), ((), ())), preferred_element_type=F32)


def dot_rows(left, right):
    return lax.dot_general(left, right, (((0,), (0,)), ((), ())), preferred_element_type=F32)


def split_pair(value, rows_top):
    rows = value.shape[0]
    top = value[:rows_top]
    bottom = jnp.concatenate(
        [value[rows_top:], jnp.zeros((2 * rows_top - rows, LANES), value.dtype)], axis=0
    )
    low = lane_low(top.shape)
    return jnp.where(low, top, swap_halves(bottom)), jnp.where(low, swap_halves(top), bottom)


def join_pair(one, two, rows):
    rows_top = one.shape[0]
    low = lane_low(one.shape)
    top = jnp.where(low, one, swap_halves(two))
    bottom = jnp.where(low, swap_halves(one), two)
    return jnp.concatenate([top, bottom[: rows - rows_top]], axis=0)


def smem():
    return pl.BlockSpec(memory_space=pltpu.SMEM)


def whole(shape):
    return pl.BlockSpec(shape, lambda *_: (0,) * len(shape))


def tokens_to_qkv(flags, tok_own, tok_oth, mods, weight, bias, tab_cos, tab_sin, time_cos, time_sin, lay):
    rows, width = tok_own.shape
    cols = lay.heads * DH

    def body(flag_ref, own_ref, oth_ref, mod_ref, w_ref, b_ref, tc_ref, ts_ref, qc_ref, qs_ref, hid_ref, long_ref, short_ref):
        step = pl.program_id(0)
        own_long = flag_ref[0]

        @pl.when(step == 0)
        def _():
            for src, base, slot in ((own_ref, 0, 1 - own_long), (oth_ref, 2, own_long)):
                normed, _ = norm_rows(src[...].astype(F32))
                shift = per_frame(normed.shape, mod_ref[base : base + 1, :width], mod_ref[base + 1 : base + 2, :width])
                scale = per_frame(
                    normed.shape, mod_ref[base : base + 1, width : 2 * width], mod_ref[base + 1 : base + 2, width : 2 * width]
                )
                hid_ref[slot] = (normed * (1.0 + scale) + shift).astype(BF)

        for slot, out_ref in ((0, long_ref), (1, short_ref)):
            acc = dot(hid_ref[slot], w_ref[...]) + b_ref[...]

            def rotated(pair):
                value = acc[:, pair * LANES : (pair + 1) * LANES]
                cosine = tc_ref[...] + per_frame(value.shape, qc_ref[2 * slot : 2 * slot + 1], qc_ref[2 * slot + 1 : 2 * slot + 2])
                sine = ts_ref[...] + per_frame(value.shape, qs_ref[2 * slot : 2 * slot + 1], qs_ref[2 * slot + 1 : 2 * slot + 2])
                return value * cosine + swap_pairs(value) * sine

            @pl.when(step == 0)
            def _():
                for pair in range(cols // LANES):
                    turned = rotated(pair)
                    out_ref[2 * pair, :rows, :HALF] = turned[:, :HALF].astype(BF)
                    out_ref[2 * pair + 1, :rows, :HALF] = swap_halves(turned)[:, :HALF].astype(BF)

            @pl.when(step == 1)
            def _():
                for pair in range(cols // LANES):
                    turned = rotated(pair)
                    out_ref[2 * pair, :rows, HALF:] = swap_halves(turned)[:, HALF:].astype(BF)
                    out_ref[2 * pair + 1, :rows, HALF:] = turned[:, HALF:].astype(BF)

            @pl.when(step == 2)
            def _():
                for pair in range(cols // LANES):
                    one, two = split_pair(acc[:, pair * LANES : (pair + 1) * LANES], lay.top)
                    out_ref[2 * pair, lay.vrow :, :] = one.astype(BF)
                    out_ref[2 * pair + 1, lay.vrow :, :] = two.astype(BF)

    packed = (lay.heads, lay.vrow + lay.top, LANES)
    return pl.pallas_call(
        body,
        grid_spec=pltpu.PrefetchScalarGridSpec(
            num_scalar_prefetch=1,
            grid=(3,),
            in_specs=[
                whole((rows, width)),
                whole((rows, width)),
                whole(mods.shape),
                pl.BlockSpec((width, cols), lambda j, f: (0, 2 * j + f[1])),
                pl.BlockSpec((1, cols), lambda j, f: (0, 2 * j + f[1])),
                whole(tab_cos.shape),
                whole(tab_sin.shape),
                whole(time_cos.shape),
                whole(time_sin.shape),
            ],
            out_specs=[whole((2, rows, width)), whole(packed), whole(packed)],
        ),
        out_shape=[
            jax.ShapeDtypeStruct((2, rows, width), BF),
            jax.ShapeDtypeStruct(packed, BF),
            jax.ShapeDtypeStruct(packed, BF),
        ],
        compiler_params=pltpu.CompilerParams(vmem_limit_bytes=40 * MIB),
        cost_estimate=pl.CostEstimate(flops=12 * rows * width * cols, bytes_accessed=12 * MIB, transcendentals=0),
        name="tokens_to_qkv",
    )(flags, tok_own, tok_oth, mods, weight, bias, tab_cos, tab_sin, time_cos, time_sin)


def unpack_values(ref, at, lay):
    part = ref[at, lay.vrow :, :].astype(F32)
    return jnp.concatenate([part, swap_halves(part)[: lay.rows - lay.top]], axis=0)


def diag_mask(shape, lay, core):
    key_row = lax.broadcasted_iota(jnp.int32, shape, 0)
    query = lax.broadcasted_iota(jnp.int32, shape, 1)
    own = (key_row < lay.rows) & ((key_row < PATCH) | (query >= PATCH))
    return own | ((key_row >= lay.rows) & (core == 1))


def load_keys(own_ref, oth_ref, group, lay):
    low = lane_low((lay.rows, LANES))
    halves = [
        jnp.where(low, unpack_values(ref, group, lay), ref[group, : lay.rows, :].astype(F32))
        for ref in (own_ref, oth_ref)
    ]
    return jnp.concatenate(halves, axis=0)


def load_query(own_ref, at, lay):
    value = swap_halves(own_ref[at, : lay.rows, :].astype(F32)) * (1.0 / math.sqrt(DH))
    return jnp.where(lane_low(value.shape), 0.0, value).astype(BF)


def fold_rows(value, op):
    return op(value.reshape(value.shape[0] // 8, 8, value.shape[1]), axis=0)


def attend(flags, own, oth, lay, long_clip):
    groups = own.shape[0]
    parts = lay.parts if long_clip else 1
    tile = 2 * lay.rows
    depth = groups if long_clip else 1

    def body(flag_ref, own_ref, oth_ref, o_ref, ot_ref, lse_ref, kv_ref, vt_ref, st_ref):
        core = flag_ref[2]
        part = flag_ref[3]

        def prepare(group, _):
            keys = load_keys(own_ref, oth_ref, group, lay)
            kv_ref[group] = keys.astype(BF)
            vt_ref[group] = keys.T[:HALF].astype(BF)
            return 0

        lax.fori_loop(0, groups, prepare, 0)
        if parts > 1:
            o_ref[...] = jnp.zeros_like(o_ref)

        def block(step, _):
            at = step * parts + part if parts > 1 else step
            slot = at if long_clip else 0
            query = load_query(own_ref, at, lay)

            def scores(kt, top):
                score = dot_lanes(kv_ref[kt], query)
                st_ref[kt] = score
                return jnp.maximum(top, fold_rows(score, jnp.max))

            top = jnp.full((8, lay.rows), NEG_BIG, F32)
            if long_clip:
                top = lax.fori_loop(0, at, scores, top)
            score = dot_lanes(kv_ref[at], query)
            score = jnp.where(diag_mask(score.shape, lay, core), score, NEG_BIG)
            st_ref[slot] = score
            top = jnp.max(jnp.maximum(top, fold_rows(score, jnp.max)), axis=0, keepdims=True)

            def mix(kt, carry):
                total, acc = carry
                expo = jnp.exp(st_ref[kt if long_clip else 0] - top)
                total = total + fold_rows(expo, jnp.sum)
                return total, acc + dot(vt_ref[kt], expo.astype(BF))

            zero = (jnp.zeros((8, lay.rows), F32), jnp.zeros((HALF, lay.rows), F32))
            if long_clip:
                total, acc = lax.fori_loop(0, at + 1, mix, zero)
            else:
                total, acc = mix(at, zero)
            total = jnp.sum(total, axis=0, keepdims=True)
            acc = acc / total
            ot_ref[at] = acc
            lse_ref[at] = jnp.broadcast_to(top + jnp.log(total), (8, lay.rows))
            out = jnp.concatenate([acc, jnp.zeros_like(acc)], axis=0).T
            o_ref[at] = split_pair(out, lay.top)[0].astype(BF)
            return 0

        lax.fori_loop(0, groups // parts, block, 0)

    vm = pl.BlockSpec(memory_space=pltpu.VMEM)
    pairs = groups * (groups + 1) // 2 if long_clip else groups
    return pl.pallas_call(
        body,
        in_specs=[smem(), vm, vm],
        out_specs=[vm, vm, vm],
        out_shape=[
            jax.ShapeDtypeStruct((groups, lay.top, LANES), BF),
            jax.ShapeDtypeStruct((groups, HALF, lay.rows), F32),
            jax.ShapeDtypeStruct((groups, 8, lay.rows), F32),
        ],
        scratch_shapes=[
            pltpu.VMEM((groups, tile, LANES), BF),
            pltpu.VMEM((groups, HALF, tile), BF),
            pltpu.VMEM((depth, tile, lay.rows), F32),
        ],
        compiler_params=pltpu.CompilerParams(vmem_limit_bytes=48 * MIB),
        cost_estimate=pl.CostEstimate(
            flops=pairs * 16 * tile * lay.rows * DH // parts, bytes_accessed=4 * MIB, transcendentals=pairs * tile * lay.rows
        ),
        name="attend_long" if long_clip else "attend_short",
    )(flags, own, oth)


def attend_back(flags, own, oth, d_out, ot, lse, tab_cos, tab_sin, time_cos, time_sin, lay, long_clip):
    groups = own.shape[0]
    parts = lay.parts if long_clip else 1
    tile = 2 * lay.rows

    def body(flag_ref, own_ref, oth_ref, do_ref, ot_ref, lse_ref, tc_ref, ts_ref, qc_ref, qs_ref, dq_ref, down_ref, doth_ref, kv_ref, kt_ref, acc_ref):
        core = flag_ref[2]
        part = flag_ref[3]

        def prepare(group, _):
            keys = load_keys(own_ref, oth_ref, group, lay)
            kv_ref[group] = keys.astype(BF)
            kt_ref[group] = keys.T[HALF:].astype(BF)
            acc_ref[group] = jnp.zeros((tile, LANES), F32)
            return 0

        lax.fori_loop(0, groups, prepare, 0)
        if parts > 1:
            dq_ref[...] = jnp.zeros_like(dq_ref)

        def block(step, _):
            at = step * parts + part if parts > 1 else step
            query = load_query(own_ref, at, lay)
            packed = do_ref[at].astype(F32)
            grad = jnp.concatenate([packed, swap_halves(packed)[: lay.rows - lay.top]], axis=0)
            grad = jnp.where(lane_low(grad.shape), grad, 0.0)
            delta = jnp.sum(grad.T[:HALF] * ot_ref[at], axis=0, keepdims=True)
            grad = grad.astype(BF)
            lse_row = lse_ref[at][0:1]

            def tile_back(kt, acc, mask):
                keys = kv_ref[kt]
                prob = jnp.exp(dot_lanes(keys, query) - lse_row)
                if mask is not None:
                    prob = jnp.where(mask, prob, 0.0)
                score_grad = (prob * (dot_lanes(keys, grad) - delta)).astype(BF)
                acc_ref[kt] += dot(score_grad, query) + dot(prob.astype(BF), grad)
                return acc + dot(kt_ref[kt], score_grad)

            acc = tile_back(at, jnp.zeros((HALF, lay.rows), F32), diag_mask((tile, lay.rows), lay, core))
            if long_clip:
                acc = lax.fori_loop(0, at, lambda kt, a: tile_back(kt, a, None), acc)
            acc = acc * (1.0 / math.sqrt(DH))
            dq = jnp.concatenate([acc, jnp.zeros_like(acc)], axis=0).T
            tab = at if long_clip else 0
            cosine = tc_ref[...] + per_frame(dq.shape, qc_ref[2 * tab], qc_ref[2 * tab + 1])
            sine = ts_ref[...] + per_frame(dq.shape, qs_ref[2 * tab], qs_ref[2 * tab + 1])
            dq_ref[at] = (dq * cosine - swap_pairs(dq) * sine).astype(BF)
            return 0

        lax.fori_loop(0, groups // parts, block, 0)

        def flush(group, _):
            down_ref[group] = acc_ref[group, : lay.rows]
            doth_ref[group] = acc_ref[group, lay.rows :].astype(BF)
            return 0

        lax.fori_loop(0, groups, flush, 0)

    vm = pl.BlockSpec(memory_space=pltpu.VMEM)
    pairs = groups * (groups + 1) // 2 if long_clip else groups
    return pl.pallas_call(
        body,
        in_specs=[smem()] + [vm] * 9,
        out_specs=[vm, vm, vm],
        out_shape=[
            jax.ShapeDtypeStruct((groups, lay.rows, LANES), BF),
            jax.ShapeDtypeStruct((groups, lay.rows, LANES), F32),
            jax.ShapeDtypeStruct((groups, lay.rows, LANES), BF),
        ],
        scratch_shapes=[
            pltpu.VMEM((groups, tile, LANES), BF),
            pltpu.VMEM((groups, HALF, tile), BF),
            pltpu.VMEM((groups, tile, LANES), F32),
        ],
        compiler_params=pltpu.CompilerParams(vmem_limit_bytes=48 * MIB),
        cost_estimate=pl.CostEstimate(
            flops=pairs * 40 * tile * lay.rows * DH // parts, bytes_accessed=6 * MIB, transcendentals=pairs * tile * lay.rows
        ),
        name="attend_back_long" if long_clip else "attend_back_short",
    )(flags, own, oth, d_out, ot, lse, tab_cos, tab_sin, time_cos, time_sin)


def finish_keys(dq, mine, theirs, tab_cos, tab_sin, time_cos, time_sin, lay, long_clip):
    groups = dq.shape[0]

    def body(dq_ref, a_ref, b_ref, tc_ref, ts_ref, qc_ref, qs_ref, out_ref):
        def one(group, _):
            both = a_ref[group] + b_ref[group].astype(F32)
            tab = group if long_clip else 0
            cosine = tc_ref[...] + per_frame(both.shape, qc_ref[2 * tab], qc_ref[2 * tab + 1])
            sine = ts_ref[...] + per_frame(both.shape, qs_ref[2 * tab], qs_ref[2 * tab + 1])
            keys = both * cosine - swap_pairs(both) * sine
            out_ref[group, : lay.rows, :] = jnp.where(lane_low(keys.shape), dq_ref[group].astype(F32), keys).astype(BF)
            out_ref[group, lay.vrow :, :] = split_pair(both, lay.top)[0].astype(BF)
            return 0

        lax.fori_loop(0, groups, one, 0)

    vm = pl.BlockSpec(memory_space=pltpu.VMEM)
    return pl.pallas_call(
        body,
        in_specs=[vm] * 7,
        out_specs=vm,
        out_shape=jax.ShapeDtypeStruct((groups, lay.vrow + lay.top, LANES), BF),
        compiler_params=pltpu.CompilerParams(vmem_limit_bytes=40 * MIB),
        cost_estimate=pl.CostEstimate(flops=groups * lay.rows * LANES * 10, bytes_accessed=3 * MIB, transcendentals=0),
        name="finish_keys",
    )(dq, mine, theirs, tab_cos, tab_sin, time_cos, time_sin)


def project_and_norm(flags, long_out, short_out, recv, weight, bias, tokens, mods, lay):
    rows, width = tokens.shape
    half = lay.heads * DH

    def body(flag_ref, long_ref, short_ref, recv_ref, w_ref, b_ref, tok_ref, mod_ref, branch_ref, resid_ref, normed_ref, inv_ref, hid_ref, att_ref):
        own_long = flag_ref[0]
        side = flag_ref[1]
        for pair in range(lay.heads // 2):
            kept = [
                jnp.where(own_long == 1, long_ref[2 * pair + k].astype(F32), short_ref[2 * pair + k].astype(F32)) for k in (0, 1)
            ]
            got = [recv_ref[2 * pair + k].astype(F32) for k in (0, 1)]
            lanes = slice(pair * LANES, (pair + 1) * LANES)
            att_ref[side, :, lanes] = join_pair(kept[0], kept[1], rows).astype(BF)
            att_ref[1 - side, :, lanes] = join_pair(got[0], got[1], rows).astype(BF)
        branch = dot(att_ref[0], w_ref[:half]) + dot(att_ref[1], w_ref[half:]) + b_ref[...]
        branch_ref[...] = branch
        gate = per_frame(branch.shape, mod_ref[0:1], mod_ref[1:2])
        resid = tok_ref[...].astype(F32) + gate * branch
        resid_ref[...] = resid
        normed, inv_std = norm_rows(resid)
        normed_ref[...] = normed
        inv_ref[...] = jnp.broadcast_to(inv_std, inv_ref.shape)
        shift = per_frame(branch.shape, mod_ref[2:3], mod_ref[3:4])
        scale = per_frame(branch.shape, mod_ref[4:5], mod_ref[5:6])
        hid_ref[...] = (normed * (1.0 + scale) + shift).astype(BF)

    vm = pl.BlockSpec(memory_space=pltpu.VMEM)
    full = jax.ShapeDtypeStruct((rows, width), F32)
    return pl.pallas_call(
        body,
        in_specs=[smem()] + [vm] * 7,
        out_specs=[vm] * 5,
        out_shape=[full, full, full, jax.ShapeDtypeStruct((rows, LANES), F32), jax.ShapeDtypeStruct((rows, width), BF)],
        scratch_shapes=[pltpu.VMEM((2, rows, half), BF)],
        compiler_params=pltpu.CompilerParams(vmem_limit_bytes=32 * MIB),
        cost_estimate=pl.CostEstimate(flops=2 * rows * width * width, bytes_accessed=6 * MIB, transcendentals=0),
        name="project_and_norm",
    )(flags, long_out, short_out, recv, weight, bias, tokens, mods)


def mlp_both(flags, hidden, mlp_grad, up_weight, up_bias, down_weight, lay, out_dtype, name):
    rows, width = hidden.shape
    ff = up_weight.shape[1]
    wide = 2 * LANES
    steps = ff // (2 * wide)

    def body(flag_ref, hid_ref, mg_ref, up_ref, ub_ref, dn_ref, actm_ref, actt_ref, pgm_ref, pgt_ref, bm_ref, bt_ref, mlp_ref, hg_ref, macc, hacc):
        step = pl.program_id(0)
        core = flag_ref[2]
        pre = dot(hid_ref[...], up_ref[...]) + ub_ref[...]
        tanh = jnp.tanh(GELU_C * (pre + GELU_K * pre * pre * pre))
        act = (0.5 * pre * (1.0 + tanh)).astype(BF)
        slope = 0.5 * (1.0 + tanh) + 0.5 * pre * (1.0 - tanh * tanh) * GELU_C * (1.0 + 3.0 * GELU_K * pre * pre)
        pre_low = (dot_lanes(mg_ref[...], dn_ref[...]) * slope).astype(BF)
        mlp = dot(act, dn_ref[...])
        back = dot_lanes(pre_low, up_ref[...])

        @pl.when(step == 0)
        def _():
            macc[...] = mlp
            hacc[...] = back

        @pl.when(step > 0)
        def _():
            macc[...] += mlp
            hacc[...] += back

        @pl.when(step == steps - 1)
        def _():
            mlp_ref[...] = macc[...].astype(mlp_ref.dtype)
            hg_ref[...] = hacc[...].astype(hg_ref.dtype)

        first = core == 0
        actm_ref[...] = jnp.where(first, act[:, :LANES], act[:, LANES:])
        actt_ref[...] = jnp.where(first, act[:, LANES:], act[:, :LANES])
        pgm_ref[...] = jnp.where(first, pre_low[:, :LANES], pre_low[:, LANES:])
        pgt_ref[...] = jnp.where(first, pre_low[:, LANES:], pre_low[:, :LANES])
        sums = jnp.sum(pre_low.astype(F32), axis=0, keepdims=True)
        bm_ref[...] = jnp.broadcast_to(jnp.where(first, sums[:, :LANES], sums[:, LANES:]), bm_ref.shape)
        bt_ref[...] = jnp.broadcast_to(jnp.where(first, sums[:, LANES:], sums[:, :LANES]), bt_ref.shape)

    quarter = ff // 4
    chunk = pl.BlockSpec((rows, LANES), lambda i, f: (0, i))
    bchunk = pl.BlockSpec((8, LANES), lambda i, f: (0, i))
    return pl.pallas_call(
        body,
        grid_spec=pltpu.PrefetchScalarGridSpec(
            num_scalar_prefetch=1,
            grid=(steps,),
            in_specs=[
                whole((rows, width)),
                whole((rows, width)),
                pl.BlockSpec((width, wide), lambda i, f: (0, 2 * i + f[1])),
                pl.BlockSpec((1, wide), lambda i, f: (0, 2 * i + f[1])),
                pl.BlockSpec((wide, width), lambda i, f: (2 * i + f[1], 0)),
            ],
            out_specs=[chunk, chunk, chunk, chunk, bchunk, bchunk, whole((rows, width)), whole((rows, width))],
            scratch_shapes=[pltpu.VMEM((rows, width), F32), pltpu.VMEM((rows, width), F32)],
        ),
        out_shape=[jax.ShapeDtypeStruct((rows, quarter), BF)] * 4
        + [jax.ShapeDtypeStruct((8, quarter), F32)] * 2
        + [jax.ShapeDtypeStruct((rows, width), out_dtype)] * 2,
        compiler_params=pltpu.CompilerParams(vmem_limit_bytes=32 * MIB),
        cost_estimate=pl.CostEstimate(flops=4 * rows * width * ff, bytes_accessed=12 * MIB, transcendentals=rows * ff // 2),
        name=name,
    )(flags, hidden, mlp_grad, up_weight, up_bias, down_weight)


def branch_back(flags, hid_own, hid_recv, cotangent, normed, inv_std, branch, mods, weight, lay):
    rows, width = normed.shape
    half = lay.heads * DH

    def body(flag_ref, a_ref, b_ref, dy_ref, n_ref, inv_ref, br_ref, mod_ref, w_ref, rg_ref, bg_ref, keep_ref, send_ref, sums_ref):
        side = flag_ref[1]
        hid = a_ref[...] + b_ref[...].astype(F32)
        norm = n_ref[...]
        scale = per_frame(hid.shape, mod_ref[4:5], mod_ref[5:6])
        resid = dy_ref[...].astype(F32) + norm_back(hid * (1.0 + scale), norm, inv_ref[:, 0:1])
        rg_ref[...] = resid
        gate = per_frame(hid.shape, mod_ref[0:1], mod_ref[1:2])
        low = (gate * resid).astype(BF)
        bg_ref[...] = low
        for out_ref, which in ((keep_ref, side), (send_ref, 1 - side)):
            grad = dot_lanes(low, w_ref[pl.ds(pl.multiple_of(which * half, half), half), :])
            for pair in range(lay.heads // 2):
                one, two = split_pair(grad[:, pair * LANES : (pair + 1) * LANES], lay.top)
                out_ref[2 * pair] = one.astype(BF)
                out_ref[2 * pair + 1] = two.astype(BF)
        sums_ref[0:1], sums_ref[1:2] = frame_sums(resid * br_ref[...])
        sums_ref[2:3], sums_ref[3:4] = frame_sums(hid)
        sums_ref[4:5], sums_ref[5:6] = frame_sums(hid * norm)
        sums_ref[6:7] = jnp.sum(low.astype(F32), axis=0, keepdims=True)
        sums_ref[7:8] = jnp.zeros((1, width), F32)

    vm = pl.BlockSpec(memory_space=pltpu.VMEM)
    packed = jax.ShapeDtypeStruct((lay.heads, lay.top, LANES), BF)
    return pl.pallas_call(
        body,
        in_specs=[smem()] + [vm] * 8,
        out_specs=[vm] * 5,
        out_shape=[
            jax.ShapeDtypeStruct((rows, width), F32),
            jax.ShapeDtypeStruct((rows, width), BF),
            packed,
            packed,
            jax.ShapeDtypeStruct((8, width), F32),
        ],
        compiler_params=pltpu.CompilerParams(vmem_limit_bytes=32 * MIB),
        cost_estimate=pl.CostEstimate(flops=2 * rows * width * width, bytes_accessed=8 * MIB, transcendentals=0),
        name="branch_back",
    )(flags, hid_own, hid_recv, cotangent, normed, inv_std, branch, mods, weight)


def qkv_back(flags, grads, tok_own, tok_oth, weight, lay, is_long):
    rows, width = tok_own.shape
    cols = lay.heads * DH
    half = cols // 2

    def body(flag_ref, g_ref, own_ref, oth_ref, w_ref, hid_ref, low_ref, gm_ref, gt_ref, bias_ref, sums_ref, q_ref, acc_ref):
        step = pl.program_id(0)
        core = flag_ref[2]

        @pl.when(step == 0)
        def _():
            for pair in range(lay.heads // 2):
                one, two = g_ref[2 * pair, :rows, :].astype(F32), g_ref[2 * pair + 1, :rows, :].astype(F32)
                low = lane_low(one.shape)
                lanes = slice(pair * LANES, (pair + 1) * LANES)
                q_ref[0, :, lanes] = jnp.where(low, one, swap_halves(two)).astype(BF)
                q_ref[1, :, lanes] = jnp.where(low, swap_halves(one), two).astype(BF)
                one, two = g_ref[2 * pair, lay.vrow :, :].astype(F32), g_ref[2 * pair + 1, lay.vrow :, :].astype(F32)
                q_ref[2, :, lanes] = join_pair(one, two, rows).astype(BF)

        value = q_ref[step]
        part = dot_lanes(value, w_ref[...])

        @pl.when(step == 0)
        def _():
            acc_ref[...] = part

        @pl.when(step > 0)
        def _():
            acc_ref[...] += part

        first = core == 0
        gm_ref[...] = jnp.where(first, value[:, :half], value[:, half:])
        gt_ref[...] = jnp.where(first, value[:, half:], value[:, :half])
        bias_ref[...] = jnp.broadcast_to(jnp.sum(value.astype(F32), axis=0, keepdims=True), bias_ref.shape)

        @pl.when(step == 2)
        def _():
            hid = acc_ref[...]
            hid_ref[...] = hid
            low_ref[...] = hid.astype(BF)
            mine = (flag_ref[0] == 1) if is_long else (flag_ref[0] == 0)
            normed, _ = norm_rows(jnp.where(mine, own_ref[...].astype(F32), oth_ref[...].astype(F32)))
            sums_ref[0:1], sums_ref[1:2] = frame_sums(hid)
            sums_ref[2:3], sums_ref[3:4] = frame_sums(hid * normed)
            sums_ref[4:8] = jnp.zeros((4, width), F32)

    return pl.pallas_call(
        body,
        grid_spec=pltpu.PrefetchScalarGridSpec(
            num_scalar_prefetch=1,
            grid=(3,),
            in_specs=[
                whole(grads.shape),
                whole((rows, width)),
                whole((rows, width)),
                pl.BlockSpec((width, cols), lambda j, f: (0, 2 * j + f[1])),
            ],
            out_specs=[
                whole((rows, width)),
                whole((rows, width)),
                pl.BlockSpec((rows, half), lambda j, f: (0, j)),
                pl.BlockSpec((rows, half), lambda j, f: (0, j)),
                pl.BlockSpec((8, cols), lambda j, f: (0, j)),
                whole((8, width)),
            ],
            scratch_shapes=[pltpu.VMEM((3, rows, cols), BF), pltpu.VMEM((rows, width), F32)],
        ),
        out_shape=[
            jax.ShapeDtypeStruct((rows, width), F32),
            jax.ShapeDtypeStruct((rows, width), BF),
            jax.ShapeDtypeStruct((rows, 3 * half), BF),
            jax.ShapeDtypeStruct((rows, 3 * half), BF),
            jax.ShapeDtypeStruct((8, 3 * cols), F32),
            jax.ShapeDtypeStruct((8, width), F32),
        ],
        compiler_params=pltpu.CompilerParams(vmem_limit_bytes=40 * MIB),
        cost_estimate=pl.CostEstimate(flops=6 * rows * width * cols, bytes_accessed=8 * MIB, transcendentals=0),
        name="qkv_back_long" if is_long else "qkv_back_short",
    )(flags, grads, tok_own, tok_oth, weight)


def token_back(flags, hid_long, hid_short, recv, tokens, resid_grad, mods, lay):
    rows, width = tokens.shape

    def body(flag_ref, l_ref, s_ref, r_ref, tok_ref, rg_ref, mod_ref, out_ref):
        hid = jnp.where(flag_ref[0] == 1, l_ref[...], s_ref[...]) + r_ref[...].astype(F32)
        normed, inv_std = norm_rows(tok_ref[...].astype(F32))
        scale = per_frame(hid.shape, mod_ref[0:1, width : 2 * width], mod_ref[1:2, width : 2 * width])
        out_ref[...] = rg_ref[...] + norm_back(hid * (1.0 + scale), normed, inv_std)

    vm = pl.BlockSpec(memory_space=pltpu.VMEM)
    return pl.pallas_call(
        body,
        in_specs=[smem()] + [vm] * 6,
        out_specs=vm,
        out_shape=jax.ShapeDtypeStruct((rows, width), F32),
        compiler_params=pltpu.CompilerParams(vmem_limit_bytes=32 * MIB),
        cost_estimate=pl.CostEstimate(flops=rows * width * 20, bytes_accessed=5 * MIB, transcendentals=0),
        name="token_back",
    )(flags, hid_long, hid_short, recv, tokens, resid_grad, mods)


def weight_grads(lefts, rights, n_blk, name):
    count = len(lefts)
    rows, depth = lefts[0].shape
    cols = rights[0].shape[1]
    tall = max(depth // n_blk, LANES)
    steps = depth // tall
    per = tall // (depth // n_blk)

    def body(*refs):
        out_ref = refs[-1]
        acc = dot_rows(refs[0][...], refs[count][...])
        for k in range(1, count):
            acc += dot_rows(refs[k][...], refs[count + k][...])
        out_ref[...] = acc.astype(BF).reshape(out_ref.shape)

    return pl.pallas_call(
        body,
        grid=(steps,),
        in_specs=[pl.BlockSpec((rows, tall), lambda i: (0, i))] * count + [whole((rows, cols))] * count,
        out_specs=pl.BlockSpec((per, tall // per, cols), lambda i: (i, 0, 0)),
        out_shape=jax.ShapeDtypeStruct((n_blk, depth // n_blk, cols), BF),
        compiler_params=pltpu.CompilerParams(vmem_limit_bytes=32 * MIB),
        cost_estimate=pl.CostEstimate(flops=2 * count * rows * depth * cols, bytes_accessed=6 * MIB, transcendentals=0),
        name=name,
    )(*lefts, *rights)


def head_weight_grads(longs, shorts, grad_long, grad_short, lay):
    rows, width = grad_long.shape
    pairs = lay.heads // 2

    def body(l_ref, s_ref, gl_ref, gs_ref, out_ref):
        for pair in range(pairs):
            acc = 0.0
            for ref, g_ref in ((l_ref, gl_ref), (s_ref, gs_ref)):
                left = join_pair(ref[2 * pair].astype(F32), ref[2 * pair + 1].astype(F32), rows).astype(BF)
                acc = acc + dot_rows(left, g_ref[...])
            out_ref[pair * LANES : (pair + 1) * LANES, :] = acc.astype(BF)

    vm = pl.BlockSpec(memory_space=pltpu.VMEM)
    return pl.pallas_call(
        body,
        in_specs=[vm] * 4,
        out_specs=vm,
        out_shape=jax.ShapeDtypeStruct((lay.heads * DH, width), BF),
        compiler_params=pltpu.CompilerParams(vmem_limit_bytes=32 * MIB),
        cost_estimate=pl.CostEstimate(flops=4 * rows * width * lay.heads * DH, bytes_accessed=3 * MIB, transcendentals=0),
        name="head_weight_grads",
    )(longs, shorts, grad_long, grad_short)


def rotary_static(frames):
    n_time, n_row = DH // 8, 3 * DH // 16
    cosine = np.zeros((frames * PATCH, LANES), np.float32)
    sine = np.zeros((frames * PATCH, LANES), np.float32)
    patch = np.arange(frames * PATCH) % PATCH
    for group, place in ((0, patch // GRID), (1, patch % GRID)):
        for j in range(n_row):
            freq = np.exp(np.float32(-math.log(10000.0)) * np.float32(j) / np.float32(n_row)).astype(np.float32)
            angle = (place.astype(np.float32) * freq).astype(np.float64)
            pair = n_time + group * n_row + j
            for head in (0, HALF):
                cosine[:, head + 2 * pair] = np.cos(angle)
                cosine[:, head + 2 * pair + 1] = np.cos(angle)
                sine[:, head + 2 * pair] = -np.sin(angle)
                sine[:, head + 2 * pair + 1] = np.sin(angle)
    return cosine, sine


def rotary_time(times):
    n_time = DH // 8
    lane = jnp.arange(LANES, dtype=jnp.int32)
    pair = (lane % HALF) // 2
    freq = jnp.exp(-math.log(10000.0) * pair.astype(F32) / float(n_time))
    angle = times.astype(F32)[:, None] * freq[None, :]
    live = (pair < n_time)[None, :]
    sign = jnp.where(lane % 2 == 0, -1.0, 1.0)[None, :]
    return jnp.where(live, jnp.cos(angle), 0.0), jnp.where(live, sign * jnp.sin(angle), 0.0)


class Layout:
    def __init__(self, rows, heads, parts):
        self.rows = rows
        self.heads = heads
        self.parts = parts
        self.top = round_up(-(-rows // 2), 16)
        self.vrow = round_up(rows, 16)


def on_device(
    tokens, cotangent, noise_embed, frame_clip, frame_index, mod_weight, mod_bias, attn_weight, attn_bias,
    proj_weight, proj_bias, up_weight, up_bias, down_weight, down_bias,
):
    n_uly = lax.axis_size("uly")
    n_blk = lax.axis_size("blk")
    blk = lax.axis_index("blk")
    uly = lax.axis_index("uly")
    rows, width = tokens.shape
    frames = noise_embed.shape[0]
    side, core = uly // 2, uly % 2
    heads = width // DH // 2
    parts = n_blk // heads
    lay = Layout(rows, heads, parts)
    dev = blk * n_uly + uly

    def swap_side(value):
        return lax.ppermute(value, "uly", [(i, i ^ 2) for i in range(n_uly)])

    def swap_core(value):
        return lax.ppermute(value, "uly", [(i, i ^ 1) for i in range(n_uly)])

    def spread(value):
        return lax.all_to_all(value, "blk", split_axis=0, concat_axis=0, tiled=True)

    def gather_all(value):
        many = lax.all_to_all(jnp.broadcast_to(value[None], (n_blk,) + value.shape), "blk", 0, 0, tiled=True)
        return lax.all_to_all(jnp.broadcast_to(many[None], (n_uly,) + many.shape), "uly", 0, 0, tiled=True)

    long_first = frame_clip[::FB] == n_blk
    own_long_b = lax.dynamic_index_in_dim(long_first, blk, 0, False) == (side == 0)
    own_long = own_long_b.astype(jnp.int32)
    flags = jnp.stack([own_long, side, core, blk // heads]).astype(jnp.int32)

    noise_oth = swap_side(noise_embed)
    tok_oth = swap_side(tokens)

    block_time = frame_index.reshape(n_blk, FB)
    head_time, tail_time = block_time[:, : FB // 2], block_time[:, FB // 2 :]
    long_times = lax.dynamic_slice_in_dim(jnp.where(long_first[:, None], head_time, tail_time), core * frames, frames, 1)
    short_times = lax.dynamic_slice_in_dim(jnp.where(long_first[:, None], tail_time, head_time), core * frames, frames, 1)
    short_times = lax.dynamic_index_in_dim(short_times, blk, 0, False)
    time_cos, time_sin = rotary_time(jnp.concatenate([lax.dynamic_index_in_dim(long_times, blk, 0, False), short_times]))
    long_cos, long_sin = rotary_time(long_times.reshape(-1))
    short_cos, short_sin = time_cos[frames:, None], time_sin[frames:, None]
    long_cos, long_sin = long_cos[:, None], long_sin[:, None]
    tab_cos, tab_sin = (jnp.asarray(t) for t in rotary_static(frames))

    noise = jnp.concatenate([noise_embed, noise_oth], axis=0).astype(F32)
    silu = jax.nn.silu(noise).astype(BF)
    mod = dot(silu, mod_weight) + mod_bias.astype(F32)
    own_mod = mod[:frames]
    gate2 = own_mod[:, 5 * width :]
    mid_mods = jnp.concatenate(
        [own_mod[:, 2 * width : 3 * width], own_mod[:, 3 * width : 4 * width], own_mod[:, 4 * width : 5 * width]], axis=0
    )
    mid_mods = jnp.concatenate([mid_mods, jnp.zeros((2, width), F32)], axis=0)
    gate2_rows = jnp.repeat(gate2, PATCH, axis=0)
    dy_grad = cotangent.astype(F32)
    mlp_grad = (gate2_rows * dy_grad).astype(BF)

    hidden1, qkv_long, qkv_short = tokens_to_qkv(
        flags, tokens, tok_oth, mod[:, : 2 * width], attn_weight, attn_bias.astype(F32)[None], tab_cos, tab_sin, time_cos, time_sin, lay
    )
    sent = jnp.concatenate([qkv_long] * parts, axis=0) if parts > 1 else qkv_long
    long_own = spread(sent)
    short_oth = swap_core(qkv_short)
    mlp_grad_oth = swap_side(mlp_grad)
    out_short, ot_short, lse_short = attend(flags, qkv_short, short_oth, lay, False)
    long_oth = swap_core(long_own)
    out_long_all, ot_long, lse_long = attend(flags, long_own, long_oth, lay, True)

    def own_part(value):
        if parts == 1:
            return value
        return lax.dynamic_slice_in_dim(value, (blk % parts) * heads, heads, 0)

    out_long = own_part(spread(out_long_all))
    out_recv = swap_side(jnp.where(own_long_b, out_short, out_long))
    branch, resid, normed2, inv2, hidden2 = project_and_norm(
        flags, out_long, out_short, out_recv, proj_weight, proj_bias.astype(F32)[None], tokens, mid_mods, lay
    )

    hidden2_oth = swap_side(hidden2)
    up_b = up_bias.astype(F32)[None]
    actm, actt, pgm, pgt, bm, bt, mlp_own, hid_own = mlp_both(
        flags, hidden2, mlp_grad, up_weight, up_b, down_weight, lay, F32, "mlp_own"
    )
    actm2, actt2, pgm2, pgt2, bm2, bt2, mlp_oth, hid_oth = mlp_both(
        flags, hidden2_oth, mlp_grad_oth, up_weight, up_b, down_weight, lay, BF, "mlp_other"
    )
    hid_recv = swap_side(hid_oth)

    resid_grad, branch_grad, do_keep, do_send, mid_sums = branch_back(
        flags, hid_own, hid_recv, cotangent, normed2, inv2, branch, mid_mods, proj_weight, lay
    )
    do_recv = swap_side(do_send)
    do_long = jnp.where(own_long_b, do_keep, do_recv)
    do_short = jnp.where(own_long_b, do_recv, do_keep)
    if parts > 1:
        hot = (jnp.arange(parts) == blk % parts)[:, None, None, None]
        do_sent = jnp.where(hot, do_long[None], 0).reshape((n_blk,) + do_long.shape[1:])
    else:
        do_sent = do_long
    do_all = spread(do_sent)

    dq_s, mine_s, theirs_s = attend_back(
        flags, qkv_short, short_oth, do_short, ot_short, lse_short, tab_cos, tab_sin, short_cos, short_sin, lay, False
    )
    grads_short = finish_keys(dq_s, mine_s, swap_core(theirs_s), tab_cos, tab_sin, short_cos, short_sin, lay, False)

    dq_l, mine_l, theirs_l = attend_back(
        flags, long_own, long_oth, do_all, ot_long, lse_long, tab_cos, tab_sin, long_cos, long_sin, lay, True
    )
    grads_all = spread(finish_keys(dq_l, mine_l, swap_core(theirs_l), tab_cos, tab_sin, long_cos, long_sin, lay, True))
    if parts > 1:
        grads_long = jnp.sum(grads_all.astype(F32).reshape((parts, heads) + grads_all.shape[1:]), axis=0).astype(BF)
    else:
        grads_long = grads_all

    hidS, hidS_low, gmS, gtS, abS, sumS = qkv_back(flags, grads_short, tokens, tok_oth, attn_weight, lay, False)
    hidL, hidL_low, gmL, gtL, abL, sumL = qkv_back(flags, grads_long, tokens, tok_oth, attn_weight, lay, True)
    hid1_recv = swap_side(jnp.where(own_long_b, hidS_low, hidL_low))
    token_grad = token_back(flags, hidL, hidS, hid1_recv, tokens, resid_grad, mod[:, : 2 * width], lay)

    mlp_recv = swap_side(mlp_oth)
    mlp = mlp_own + mlp_recv.astype(F32) + down_bias.astype(F32)[None]
    output = (resid + gate2_rows * mlp).astype(BF)
    gate2_grad = jnp.sum((dy_grad * mlp).reshape(frames, PATCH, width), axis=1)

    act_got, pg_got, act_got2, pg_got2 = (swap_core(v) for v in (actt, pgt, actt2, pgt2))
    hid_c, hid_c2, mg_c, mg_c2 = (swap_core(v) for v in (hidden2, hidden2_oth, mlp_grad, mlp_grad_oth))
    up_part = weight_grads([hidden2, hidden2_oth, hid_c, hid_c2], [pgm, pgm2, pg_got, pg_got2], n_blk, "up_grads")
    down_part = weight_grads([actm, actm2, act_got, act_got2], [mlp_grad, mlp_grad_oth, mg_c, mg_c2], n_blk, "down_grads")
    mlp_total = lax.psum_scatter(
        jnp.concatenate([up_part, down_part], axis=1), "blk", scatter_dimension=0, tiled=False
    )
    up_rows = up_part.shape[1]
    up_mine = mlp_total[:up_rows]
    down_mine = mlp_total[up_rows:].astype(F32)

    def to_rows(value):
        return lax.all_to_all(value.reshape((n_uly, value.shape[0] // n_uly) + value.shape[1:]), "uly", 0, 0, tiled=True)

    up_all = to_rows(up_mine)
    row_out = up_all.shape[1]
    ff = up_weight.shape[1]
    g_up_weight = jnp.swapaxes(up_all, 0, 1).reshape(row_out, n_uly, ff // (n_uly * LANES), LANES)
    g_up_weight = jnp.swapaxes(g_up_weight, 1, 2).reshape(row_out, ff).astype(F32)

    g = ff // (n_blk * n_uly)
    def down_home(index):
        b, u = divmod(index, n_uly)
        start = ((b * g // LANES) * n_uly + u) * LANES + (b * g) % LANES
        return start // g

    down_map = [(i, down_home(i)) for i in range(n_blk * n_uly)]
    if all(a == b for a, b in down_map):
        g_down_weight = down_mine
    else:
        g_down_weight = lax.ppermute(down_mine, ("blk", "uly"), down_map)

    branch_grad_oth = swap_side(branch_grad)
    bg_long = jnp.where(own_long_b, branch_grad, branch_grad_oth)
    bg_short = jnp.where(own_long_b, branch_grad_oth, branch_grad)
    proj_part = head_weight_grads(out_long, out_short, bg_long, bg_short, lay).reshape(2, -1, width)
    proj_got = swap_core(jnp.where(core == 0, proj_part[1], proj_part[0]))
    proj_half = jnp.where(core == 0, proj_part[0], proj_part[1]).astype(F32) + proj_got.astype(F32)
    proj_sum = jnp.sum(spread(proj_half.astype(BF).reshape(n_blk, -1, width)).astype(F32), axis=0)
    proj_map = [(b * n_uly + u, u * n_blk + b) for b in range(n_blk) for u in range(n_uly)]
    g_proj_weight = lax.ppermute(proj_sum, ("blk", "uly"), proj_map)

    h1_core = swap_core(hidden1)
    attn_part = weight_grads(
        [hidden1[0], hidden1[1], h1_core[0], h1_core[1]], [gmL, gmS, swap_core(gtL), swap_core(gtS)], n_blk, "attn_grads"
    )
    attn_sum = jnp.sum(spread(attn_part).astype(F32), axis=0)
    attn_all = to_rows(attn_sum)
    g_attn_weight = jnp.transpose(attn_all.reshape(n_uly, row_out, 3, -1), (1, 2, 0, 3)).reshape(row_out, 3 * width)

    down_b = jnp.sum(mlp_grad.astype(F32), axis=0, keepdims=True)
    early = jnp.concatenate(
        [mid_sums[0:2], mid_sums[2:6], gate2_grad, silu[:frames].astype(F32), down_b, mid_sums[6:7],
         (bm + bm2)[0:1], (bt + bt2)[0:1], jnp.zeros((2, width), F32)], axis=0,
    ).astype(BF)
    early_all = gather_all(early).astype(F32)
    late = jnp.concatenate(
        [sumL[:4], sumS[:4], jnp.pad((abL + abS)[0], (0, width // 2)).reshape(2, width), jnp.zeros((6, width), F32)], axis=0
    ).astype(BF)
    late_all = gather_all(late).astype(F32)

    own_long_all = (long_first[None, :] == (jnp.arange(n_uly) // 2 == 0)[:, None])[:, :, None, None]
    part_l, part_s = late_all[:, :, 0:4], late_all[:, :, 4:8]
    part_own = jnp.where(own_long_all, part_l, part_s)
    part_oth = jnp.where(own_long_all, part_s, part_l)
    first_all = part_own + jnp.concatenate([part_oth[2:], part_oth[:2]], axis=0)
    silu_all = early_all[:, :, 8:10].reshape(-1, width).astype(BF)
    silu_cols = lax.dynamic_slice_in_dim(silu_all, dev * (width // (n_blk * n_uly)), width // (n_blk * n_uly), 1)
    mod_all = jnp.concatenate(
        [first_all[:, :, 0:2], first_all[:, :, 2:4], early_all[:, :, 0:2], early_all[:, :, 2:4], early_all[:, :, 4:6], early_all[:, :, 6:8]],
        axis=-1,
    ).reshape(-1, 6 * width)
    g_mod_weight = dot_rows(silu_cols, mod_all.astype(BF))

    def cut(vector, start, size):
        return lax.dynamic_slice_in_dim(vector, start, size, 0)

    total_dev = n_blk * n_uly
    g_mod_bias = cut(jnp.sum(mod_all, axis=0), dev * (6 * width // total_dev), 6 * width // total_dev)
    early_sum = jnp.sum(early_all, axis=(0, 1))
    g_down_bias = cut(early_sum[10], dev * (width // total_dev), width // total_dev)
    g_proj_bias = cut(early_sum[11], dev * (width // total_dev), width // total_dev)
    up_by_uly = jnp.sum(early_all[:, :, 12:14], axis=1)
    up_quarter = up_by_uly[:, 0] + up_by_uly[:, 1].reshape(n_uly // 2, 2, width)[:, ::-1].reshape(n_uly, width)
    up_line = jnp.swapaxes(up_quarter.reshape(n_uly, -1, LANES), 0, 1).reshape(-1)
    g_up_bias = cut(up_line, dev * g, g)
    late_bias = jnp.sum(late_all[:, :, 8:10], axis=1).reshape(n_uly // 2, 2, 2 * width).sum(axis=1)[:, : 3 * width // 2]
    attn_line = jnp.swapaxes(late_bias.reshape(n_uly // 2, 3, width // 2), 0, 1).reshape(-1)
    g_attn_bias = cut(attn_line, dev * (3 * width // total_dev), 3 * width // total_dev)
    return (
        output, token_grad, g_mod_weight, g_mod_bias, g_attn_weight, g_attn_bias,
        g_proj_weight, g_proj_bias, g_up_weight, g_up_bias, g_down_weight, g_down_bias,
    )


def solution(mesh):
    row = P(("blk", "uly"), None)
    flat = P(("blk", "uly"))
    in_specs = (row, row, row) + (P(),) * 12
    out_specs = (row, row, row, flat, row, flat, row, flat, row, flat, row, flat)
    return jax.shard_map(on_device, mesh=mesh, in_specs=in_specs, out_specs=out_specs, check_vma=False)
```

```python
import functools
import math

import jax
import jax.numpy as jnp
import numpy as np
from jax import lax
from jax.experimental import pallas as pl
from jax.experimental.pallas import tpu as pltpu
from jax.sharding import PartitionSpec as P

DH = 64
GRID = 10
FB = 8
PATCH = 100
HALF = 64
LANES = 128

GELU_C = 0.7978845608028654
GELU_K = 0.044715
NEG_BIG = -1e30
MIB = 1 << 20
UNROLL = 2
PACK = 24

BF = jnp.bfloat16
F32 = jnp.float32


def round_up(value, step):
    return -(-value // step) * step


def lane_low(shape):
    return lax.broadcasted_iota(jnp.int32, shape, len(shape) - 1) < HALF


def first_frame(shape):
    return lax.broadcasted_iota(jnp.int32, shape, 0) < PATCH


def swap_halves(value):
    return pltpu.roll(value, HALF, 1)


def swap_pairs(value):
    even = lax.broadcasted_iota(jnp.int32, value.shape, 1) % 2 == 0
    return jnp.where(even, pltpu.roll(value, LANES - 1, 1), pltpu.roll(value, 1, 1))


def per_frame(shape, first, second):
    return jnp.where(first_frame(shape), jnp.broadcast_to(first, shape), jnp.broadcast_to(second, shape))


def frame_sums(value):
    head = first_frame(value.shape)
    one = jnp.sum(jnp.where(head, value, 0.0), axis=0, keepdims=True)
    two = jnp.sum(jnp.where(head, 0.0, value), axis=0, keepdims=True)
    return one, two


def norm_rows(values):
    center = values - jnp.mean(values, axis=-1, keepdims=True)
    inv_std = lax.rsqrt(jnp.mean(center * center, axis=-1, keepdims=True) + 1e-06)
    return center * inv_std, inv_std


def norm_back(grad, normed, inv_std):
    return inv_std * (
        grad
        - jnp.mean(grad, axis=-1, keepdims=True)
        - normed * jnp.mean(grad * normed, axis=-1, keepdims=True)
    )


def dot(left, right):
    return jnp.dot(left, right, preferred_element_type=F32)


def dot_lanes(left, right):
    return lax.dot_general(left, right, (((1,), (1,)), ((), ())), preferred_element_type=F32)


def dot_rows(left, right):
    return lax.dot_general(left, right, (((0,), (0,)), ((), ())), preferred_element_type=F32)


def split_pair(value, rows_top):
    rows = value.shape[0]
    top = value[:rows_top]
    bottom = jnp.concatenate(
        [value[rows_top:], jnp.zeros((2 * rows_top - rows, LANES), value.dtype)], axis=0
    )
    low = lane_low(top.shape)
    return jnp.where(low, top, swap_halves(bottom)), jnp.where(low, swap_halves(top), bottom)


def join_pair(one, two, rows):
    rows_top = one.shape[0]
    low = lane_low(one.shape)
    top = jnp.where(low, one, swap_halves(two))
    bottom = jnp.where(low, swap_halves(one), two)
    return jnp.concatenate([top, bottom[: rows - rows_top]], axis=0)


def smem():
    return pl.BlockSpec(memory_space=pltpu.SMEM)


def whole(shape):
    return pl.BlockSpec(shape, lambda *_: (0,) * len(shape))


def kernel_call(body, flags, args, outs, *, specs=None, out_specs=None, grid=(1,), scratch=(), vmem=16, pins=(), out_pins=(), aliases=None, flops, name):
    specs = specs or [None] * len(args)
    out_specs = out_specs or [None] * len(outs)
    return pl.pallas_call(
        body,
        grid_spec=pltpu.PrefetchScalarGridSpec(
            num_scalar_prefetch=1,
            grid=grid,
            in_specs=[spec or whole(a.shape) for spec, a in zip(specs, args)],
            out_specs=[spec or whole(o.shape) for spec, o in zip(out_specs, outs)],
            scratch_shapes=list(scratch),
        ),
        out_shape=[pltpu.HBM(o.shape, o.dtype) if k in out_pins else o for k, o in enumerate(outs)],
        input_output_aliases=aliases or {},
        compiler_params=pltpu.CompilerParams(vmem_limit_bytes=vmem * MIB),
        cost_estimate=pl.CostEstimate(flops=flops // 4096, bytes_accessed=4096, transcendentals=0),
        name=name,
    )(flags, *[pltpu.with_memory_space_constraint(a, pltpu.HBM) if a.size >= MIB or k in pins else a for k, a in enumerate(args)])


def shape_of(dims, dtype):
    return jax.ShapeDtypeStruct(dims, dtype)


def tokens_to_qkv(flags, tok_own, tok_oth, mods, weight, bias, tab_cos, tab_sin, time_cos, time_sin, lay):
    rows, width = tok_own.shape
    cols = lay.heads * DH

    def body(flag_ref, own_ref, oth_ref, mod_ref, w_ref, b_ref, tc_ref, ts_ref, qc_ref, qs_ref, hid_ref, long_ref, short_ref):
        step = pl.program_id(0)
        own_long = flag_ref[0]

        @pl.when(step == 0)
        def _():
            for src, base, slot in ((own_ref, 0, 1 - own_long), (oth_ref, 2, own_long)):
                normed, _ = norm_rows(src[...].astype(F32))
                shift = per_frame(normed.shape, mod_ref[base : base + 1, :width], mod_ref[base + 1 : base + 2, :width])
                scale = per_frame(
                    normed.shape, mod_ref[base : base + 1, width : 2 * width], mod_ref[base + 1 : base + 2, width : 2 * width]
                )
                hid_ref[slot] = (normed * (1.0 + scale) + shift).astype(BF)

        for slot, out_ref in ((0, long_ref), (1, short_ref)):
            acc = dot(hid_ref[slot], w_ref[...]) + b_ref[...]

            def rotated(pair):
                value = acc[:, pair * LANES : (pair + 1) * LANES]
                cosine = tc_ref[...] + per_frame(value.shape, qc_ref[2 * slot : 2 * slot + 1], qc_ref[2 * slot + 1 : 2 * slot + 2])
                sine = ts_ref[...] + per_frame(value.shape, qs_ref[2 * slot : 2 * slot + 1], qs_ref[2 * slot + 1 : 2 * slot + 2])
                return value * cosine + swap_pairs(value) * sine

            @pl.when(step == 0)
            def _():
                for pair in range(cols // LANES):
                    turned = rotated(pair)
                    out_ref[2 * pair, :rows, :HALF] = turned[:, :HALF].astype(BF)
                    out_ref[2 * pair + 1, :rows, :HALF] = swap_halves(turned)[:, :HALF].astype(BF)

            @pl.when(step == 1)
            def _():
                for pair in range(cols // LANES):
                    turned = rotated(pair)
                    out_ref[2 * pair, :rows, HALF:] = swap_halves(turned)[:, HALF:].astype(BF)
                    out_ref[2 * pair + 1, :rows, HALF:] = turned[:, HALF:].astype(BF)

            @pl.when(step == 2)
            def _():
                for pair in range(cols // LANES):
                    one, two = split_pair(acc[:, pair * LANES : (pair + 1) * LANES], lay.top)
                    out_ref[2 * pair, lay.vrow :, :] = one.astype(BF)
                    out_ref[2 * pair + 1, lay.vrow :, :] = two.astype(BF)

    packed = (lay.heads, lay.vrow + lay.top, LANES)
    return kernel_call(
        body,
        flags,
        [tok_own, tok_oth, mods, weight, bias, tab_cos, tab_sin, time_cos, time_sin],
        [shape_of((2, rows, width), BF), shape_of(packed, BF), shape_of(packed, BF)],
        specs=[
            None, None, None,
            pl.BlockSpec((width, cols), lambda j, f: (0, 2 * j + f[1])),
            pl.BlockSpec((1, cols), lambda j, f: (0, 2 * j + f[1])),
            None, None, None, None,
        ],
        out_pins=(0,),
        grid=(3,),
        flops=12 * rows * width * cols,
        name="tokens_to_qkv",
    )


def unpack_values(ref, at, lay):
    part = ref[at, lay.vrow :, :].astype(F32)
    return jnp.concatenate([part, swap_halves(part)[: lay.rows - lay.top]], axis=0)


def hundreds(value):
    return (value * 1311) >> 17


def diag_mask(keys, queries, core):
    key = hundreds(lax.broadcasted_iota(jnp.int32, (keys, 1), 0)) ^ (2 * core)
    query = hundreds(lax.broadcasted_iota(jnp.int32, (1, queries), 1))
    query = ((query & 2) << 1) + (query & 1) + 2 * core
    return key <= query


def load_keys(own_ref, oth_ref, group, lay):
    low = lane_low((lay.rows, LANES))
    halves = [
        jnp.where(low, unpack_values(ref, group, lay), ref[group, : lay.rows, :].astype(F32))
        for ref in (own_ref, oth_ref)
    ]
    return jnp.concatenate(halves, axis=0)


def load_query(own_ref, at, lay):
    value = swap_halves(own_ref[at, : lay.rows, :].astype(F32)) * (1.0 / math.sqrt(DH))
    return jnp.where(lane_low(value.shape), 0.0, value)


def load_rows(load, groups):
    return jnp.concatenate([load(g) for g in groups], axis=0)


def fold_rows(value, op):
    return op(value.reshape(value.shape[0] // 8, 8, value.shape[1]), axis=0)


def unpack_rows(ref, at, lay):
    packed = ref[at].astype(F32)
    grad = jnp.concatenate([packed, swap_halves(packed)[: lay.rows - lay.top]], axis=0)
    return jnp.where(lane_low(grad.shape), grad, 0.0)


def attend(flags, own, oth, lay, long_clip):
    groups = own.shape[0]
    parts = lay.parts if long_clip else 1
    per = 2 if long_clip else 1
    count = groups // per
    keys, queries = 2 * lay.rows * per, lay.rows * per
    depth = count if long_clip else UNROLL

    def body(flag_ref, own_ref, oth_ref, o_ref, ot_ref, lse_ref, kv_ref, vt_ref, st_ref):
        core = flag_ref[2]
        part = flag_ref[3]

        def prepare(tile, slot):
            rows = jnp.concatenate([load_keys(own_ref, oth_ref, per * tile + k, lay) for k in range(per)], axis=0)
            kv_ref[slot] = rows.astype(BF)
            vt_ref[slot] = rows.T[:HALF].astype(BF)

        def block(at, slot):
            query = load_rows(lambda g: load_query(own_ref, g, lay), [per * at + k for k in range(per)]).astype(BF)

            def scores(kt, top):
                score = dot_lanes(kv_ref[kt], query)
                st_ref[kt] = score
                return jnp.maximum(top, fold_rows(score, jnp.max))

            top = jnp.full((8, queries), NEG_BIG, F32)
            if long_clip:
                top = lax.fori_loop(0, at, scores, top)
            score = dot_lanes(kv_ref[slot], query)
            score = jnp.where(diag_mask(keys, queries, core), score, NEG_BIG)
            st_ref[slot] = score
            top = jnp.max(jnp.maximum(top, fold_rows(score, jnp.max)), axis=0, keepdims=True)

            def mix(kt, carry):
                total, acc = carry
                expo = jnp.exp(st_ref[kt] - top)
                total = total + fold_rows(expo, jnp.sum)
                return total, acc + dot(vt_ref[kt], expo.astype(BF))

            zero = (jnp.zeros((8, queries), F32), jnp.zeros((HALF, queries), F32))
            if long_clip:
                total, acc = lax.fori_loop(0, at + 1, mix, zero)
            else:
                total, acc = mix(slot, zero)
            total = jnp.sum(total, axis=0, keepdims=True)
            acc = acc / total
            ot_ref[at] = acc
            lse_ref[at] = jnp.broadcast_to(top + jnp.log(total), (8, queries))
            out = jnp.concatenate([acc, jnp.zeros_like(acc)], axis=0).T
            for k in range(per):
                o_ref[per * at + k] = split_pair(out[k * lay.rows : (k + 1) * lay.rows], lay.top)[0].astype(BF)

        if long_clip:
            def prepare_loop(tile, _):
                prepare(tile, tile)
                return 0

            lax.fori_loop(0, count, prepare_loop, 0)
            if parts > 1:
                o_ref[...] = jnp.zeros_like(o_ref)

            def block_loop(step, _):
                at = step * parts + part if parts > 1 else step
                block(at, at)
                return 0

            lax.fori_loop(0, count // parts, block_loop, 0)
        else:
            def head_loop(step, _):
                for k in range(UNROLL):
                    prepare(UNROLL * step + k, k)
                for k in range(UNROLL):
                    block(UNROLL * step + k, k)
                return 0

            lax.fori_loop(0, count // UNROLL, head_loop, 0)

    pairs = count * (count + 1) // 2 if long_clip else count
    return kernel_call(
        body,
        flags,
        [own, oth],
        [
            shape_of((groups, lay.top, LANES), BF),
            shape_of((count, HALF, queries), F32),
            shape_of((count, 8, queries), F32),
        ],
        scratch=[
            pltpu.VMEM((depth, keys, LANES), BF),
            pltpu.VMEM((depth, HALF, keys), BF),
            pltpu.VMEM((depth, keys, queries), F32),
        ],
        out_pins=(1, 2),
        vmem=max(24, 3 * groups) if long_clip else 16,
        flops=pairs * 16 * keys * queries * DH // parts,
        name="attend_long" if long_clip else "attend_short",
    )


def attend_back(flags, own, oth, d_outs, ot, lse, tab_cos, tab_sin, time_cos, time_sin, lay, long_clip):
    groups = own.shape[0]
    parts = lay.parts if long_clip else 1
    per = 2 if long_clip else 1
    count = groups // per
    keys, queries = 2 * lay.rows * per, lay.rows * per
    depth = count if long_clip else UNROLL

    def body(flag_ref, own_ref, oth_ref, *refs):
        do_refs, refs = refs[: len(d_outs)], refs[len(d_outs) :]
        ot_ref, lse_ref, tc_ref, ts_ref, qc_ref, qs_ref, dq_ref, down_ref, doth_ref, kv_ref, kt_ref, acc_ref = refs
        own_long = flag_ref[0]
        core = flag_ref[2]
        part = flag_ref[3]

        def prepare(tile, slot):
            rows = jnp.concatenate([load_keys(own_ref, oth_ref, per * tile + k, lay) for k in range(per)], axis=0)
            kv_ref[slot] = rows.astype(BF)
            kt_ref[slot] = rows.T[HALF:].astype(BF)
            if long_clip:
                acc_ref[slot] = jnp.zeros((keys, LANES), F32)

        def block(at, slot):
            members = [per * at + k for k in range(per)]
            query = load_rows(lambda g: load_query(own_ref, g, lay), members).astype(BF)
            if long_clip:
                grad = load_rows(lambda g: unpack_rows(do_refs[0], g, lay), members)
            else:
                grad = load_rows(
                    lambda g: jnp.where(own_long == 1, unpack_rows(do_refs[1], g, lay), unpack_rows(do_refs[0], g, lay)), members
                )
            delta = jnp.sum(grad.T[:HALF] * ot_ref[at], axis=0, keepdims=True)
            grad = grad.astype(BF)
            lse_row = lse_ref[at][0:1]

            def tile_back(kt, acc, diag):
                tile = kv_ref[kt]
                prob = jnp.exp(dot_lanes(tile, query) - lse_row)
                if diag:
                    prob = jnp.where(diag_mask(keys, queries, core), prob, 0.0)
                score_grad = (prob * (dot_lanes(tile, grad) - delta)).astype(BF)
                both = dot(score_grad, query) + dot(prob.astype(BF), grad)
                if long_clip:
                    acc_ref[kt] += both
                else:
                    acc_ref[kt] = both
                return acc + dot(kt_ref[kt], score_grad)

            acc = tile_back(slot, jnp.zeros((HALF, queries), F32), True)
            if long_clip:
                acc = lax.fori_loop(0, at, lambda kt, a: tile_back(kt, a, False), acc)
            acc = acc * (1.0 / math.sqrt(DH))
            turned = jnp.concatenate([acc, jnp.zeros_like(acc)], axis=0).T
            for k, group in enumerate(members):
                dq = turned[k * lay.rows : (k + 1) * lay.rows]
                tab = group if long_clip else 0
                cosine = tc_ref[...] + per_frame(dq.shape, qc_ref[2 * tab], qc_ref[2 * tab + 1])
                sine = ts_ref[...] + per_frame(dq.shape, qs_ref[2 * tab], qs_ref[2 * tab + 1])
                dq_ref[group] = (dq * cosine - swap_pairs(dq) * sine).astype(BF)

        def flush(tile, slot):
            for k in range(per):
                down_ref[per * tile + k] = acc_ref[slot, 2 * k * lay.rows : (2 * k + 1) * lay.rows]
                doth_ref[per * tile + k] = acc_ref[slot, (2 * k + 1) * lay.rows : (2 * k + 2) * lay.rows].astype(BF)

        if long_clip:
            def prepare_loop(tile, _):
                prepare(tile, tile)
                return 0

            lax.fori_loop(0, count, prepare_loop, 0)
            if parts > 1:
                dq_ref[...] = jnp.zeros_like(dq_ref)

            def block_loop(step, _):
                at = step * parts + part if parts > 1 else step
                block(at, at)
                return 0

            lax.fori_loop(0, count // parts, block_loop, 0)

            def flush_loop(tile, _):
                flush(tile, tile)
                return 0

            lax.fori_loop(0, count, flush_loop, 0)
        else:
            def head_loop(step, _):
                for k in range(UNROLL):
                    prepare(UNROLL * step + k, k)
                for k in range(UNROLL):
                    block(UNROLL * step + k, k)
                for k in range(UNROLL):
                    flush(UNROLL * step + k, k)
                return 0

            lax.fori_loop(0, count // UNROLL, head_loop, 0)

    pairs = count * (count + 1) // 2 if long_clip else count
    return kernel_call(
        body,
        flags,
        [own, oth, *d_outs, ot, lse, tab_cos, tab_sin, time_cos, time_sin],
        [
            shape_of((groups, lay.rows, LANES), BF),
            shape_of((groups, lay.rows, LANES), F32),
            shape_of((groups, lay.rows, LANES), BF),
        ],
        scratch=[
            pltpu.VMEM((depth, keys, LANES), BF),
            pltpu.VMEM((depth, HALF, keys), BF),
            pltpu.VMEM((depth, keys, LANES), F32),
        ],
        out_pins=(0, 1),
        vmem=max(24, 3 * groups) if long_clip else 20,
        pins=(0, 1) + tuple(range(2 + len(d_outs), 8 + len(d_outs))),
        flops=pairs * 40 * keys * queries * DH // parts,
        name="attend_back_long" if long_clip else "attend_back_short",
    )


def finish_keys(flags, dq, mine, theirs, tab_cos, tab_sin, time_cos, time_sin, lay, long_clip):
    groups = dq.shape[0]

    def body(flag_ref, dq_ref, a_ref, b_ref, tc_ref, ts_ref, qc_ref, qs_ref, out_ref):
        def one(group, _):
            both = a_ref[group] + b_ref[group].astype(F32)
            tab = group if long_clip else 0
            cosine = tc_ref[...] + per_frame(both.shape, qc_ref[2 * tab], qc_ref[2 * tab + 1])
            sine = ts_ref[...] + per_frame(both.shape, qs_ref[2 * tab], qs_ref[2 * tab + 1])
            keys = both * cosine - swap_pairs(both) * sine
            out_ref[group, : lay.rows, :] = jnp.where(lane_low(keys.shape), dq_ref[group].astype(F32), keys).astype(BF)
            out_ref[group, lay.vrow :, :] = split_pair(both, lay.top)[0].astype(BF)
            return 0

        lax.fori_loop(0, groups, one, 0)

    return kernel_call(
        body,
        flags,
        [dq, mine, theirs, tab_cos, tab_sin, time_cos, time_sin],
        [shape_of((groups, lay.vrow + lay.top, LANES), BF)],
        pins=(0, 1),
        vmem=max(16, groups),
        flops=groups * lay.rows * LANES * 10,
        name="finish_keys",
    )[0]


def project_and_norm(flags, long_out, short_out, recv, weight, bias, tokens, mods, lay):
    rows, width = tokens.shape
    half = lay.heads * DH

    def body(flag_ref, long_ref, short_ref, recv_ref, w_ref, b_ref, tok_ref, mod_ref, branch_ref, resid_ref, normed_ref, inv_ref, hid_ref, att_ref):
        own_long = flag_ref[0]
        side = flag_ref[1]
        for pair in range(lay.heads // 2):
            kept = [
                jnp.where(own_long == 1, long_ref[2 * pair + k].astype(F32), short_ref[2 * pair + k].astype(F32)) for k in (0, 1)
            ]
            got = [recv_ref[2 * pair + k].astype(F32) for k in (0, 1)]
            lanes = slice(pair * LANES, (pair + 1) * LANES)
            att_ref[side, :, lanes] = join_pair(kept[0], kept[1], rows).astype(BF)
            att_ref[1 - side, :, lanes] = join_pair(got[0], got[1], rows).astype(BF)
        branch = dot(att_ref[0], w_ref[:half]) + dot(att_ref[1], w_ref[half:]) + b_ref[...]
        branch_ref[...] = branch
        gate = per_frame(branch.shape, mod_ref[0:1], mod_ref[1:2])
        resid = tok_ref[...].astype(F32) + gate * branch
        resid_ref[...] = resid
        normed, inv_std = norm_rows(resid)
        normed_ref[...] = normed
        inv_ref[...] = jnp.broadcast_to(inv_std, inv_ref.shape)
        shift = per_frame(branch.shape, mod_ref[2:3], mod_ref[3:4])
        scale = per_frame(branch.shape, mod_ref[4:5], mod_ref[5:6])
        hid_ref[...] = (normed * (1.0 + scale) + shift).astype(BF)

    full = shape_of((rows, width), F32)
    return kernel_call(
        body,
        flags,
        [long_out, short_out, recv, weight, bias, tokens, mods],
        [full, full, full, shape_of((rows, LANES), F32), shape_of((rows, width), BF)],
        scratch=[pltpu.VMEM((2, rows, half), BF)],
        out_pins=(0, 1, 2, 3),
        vmem=24,
        flops=2 * rows * width * width,
        name="project_and_norm",
    )


def mlp_both(flags, hidden, mlp_grad, up_weight, up_bias, down_weight, lay, out_dtype, name):
    rows, width = hidden.shape
    ff = up_weight.shape[1]
    wide = 2 * LANES
    chunks = 2
    steps = ff // (2 * wide * chunks)
    quarter = ff // 4

    def body(flag_ref, hid_ref, mg_ref, *refs):
        weights, outs = refs[: 3 * chunks], refs[3 * chunks :]
        mine_ref, send_ref, bm_ref, bt_ref, mlp_ref, hg_ref, macc, hacc = outs
        step = pl.program_id(0)
        first = flag_ref[2] == 0
        mlp, back = 0.0, 0.0
        for k in range(chunks):
            up_ref, ub_ref, dn_ref = weights[3 * k : 3 * k + 3]
            pre = dot(hid_ref[...], up_ref[...]) + ub_ref[...]
            tanh = jnp.tanh(GELU_C * (pre + GELU_K * pre * pre * pre))
            act = (0.5 * pre * (1.0 + tanh)).astype(BF)
            slope = 0.5 * (1.0 + tanh) + 0.5 * pre * (1.0 - tanh * tanh) * GELU_C * (1.0 + 3.0 * GELU_K * pre * pre)
            pre_low = (dot_lanes(mg_ref[...], dn_ref[...]) * slope).astype(BF)
            mlp = mlp + dot(act, dn_ref[...])
            back = back + dot_lanes(pre_low, up_ref[...])
            sums = jnp.sum(pre_low.astype(F32), axis=0, keepdims=True)
            lanes = slice(k * LANES, (k + 1) * LANES)
            for at, value in ((0, act), (1, pre_low)):
                mine_ref[at, :, lanes] = jnp.where(first, value[:, :LANES], value[:, LANES:])
                send_ref[at, :, lanes] = jnp.where(first, value[:, LANES:], value[:, :LANES])
            bm_ref[:, lanes] = jnp.broadcast_to(jnp.where(first, sums[:, :LANES], sums[:, LANES:]), (8, LANES))
            bt_ref[:, lanes] = jnp.broadcast_to(jnp.where(first, sums[:, LANES:], sums[:, :LANES]), (8, LANES))

        @pl.when(step == 0)
        def _():
            macc[...] = mlp
            hacc[...] = back

        @pl.when(step > 0)
        def _():
            macc[...] += mlp
            hacc[...] += back

        @pl.when(step == steps - 1)
        def _():
            mlp_ref[...] = macc[...].astype(mlp_ref.dtype)
            hg_ref[...] = hacc[...].astype(hg_ref.dtype)

    chunk = pl.BlockSpec((2, rows, chunks * LANES), lambda i, f: (0, 0, i))
    bchunk = pl.BlockSpec((8, chunks * LANES), lambda i, f: (0, i))
    weight_args, weight_specs = [], []
    for k in range(chunks):
        weight_args += [up_weight, up_bias, down_weight]
        weight_specs += [
            pl.BlockSpec((width, wide), lambda i, f, k=k: (0, 2 * (chunks * i + k) + f[1])),
            pl.BlockSpec((1, wide), lambda i, f, k=k: (0, 2 * (chunks * i + k) + f[1])),
            pl.BlockSpec((wide, width), lambda i, f, k=k: (2 * (chunks * i + k) + f[1], 0)),
        ]
    return kernel_call(
        body,
        flags,
        [hidden, mlp_grad, *weight_args],
        [shape_of((2, rows, quarter), BF)] * 2 + [shape_of((8, quarter), F32)] * 2 + [shape_of((rows, width), out_dtype)] * 2,
        specs=[None, None] + weight_specs,
        out_specs=[chunk, chunk, bchunk, bchunk, None, None],
        grid=(steps,),
        scratch=[pltpu.VMEM((rows, width), F32), pltpu.VMEM((rows, width), F32)],
        vmem=20,
        flops=4 * rows * width * ff,
        name=name,
    )


def scale_cotangent(flags, cotangent, gates):
    rows, width = cotangent.shape

    def body(flag_ref, dy_ref, g_ref, out_ref, sums_ref):
        low = (per_frame((rows, width), g_ref[0:1], g_ref[1:2]) * dy_ref[...].astype(F32)).astype(BF)
        out_ref[...] = low
        sums_ref[...] = jnp.broadcast_to(jnp.sum(low.astype(F32), axis=0, keepdims=True), sums_ref.shape)

    return kernel_call(
        body,
        flags,
        [cotangent, gates],
        [shape_of((rows, width), BF), shape_of((8, width), F32)],
        pins=(0,),
        flops=rows * width,
        name="scale_cotangent",
    )


def layer_output(flags, mlp_own, mlp_recv, bias, resid, cotangent, gates):
    rows, width = resid.shape

    def body(flag_ref, a_ref, b_ref, bias_ref, r_ref, dy_ref, g_ref, out_ref, sums_ref):
        mlp = a_ref[...] + b_ref[...].astype(F32) + bias_ref[...]
        out_ref[...] = (r_ref[...] + per_frame((rows, width), g_ref[0:1], g_ref[1:2]) * mlp).astype(BF)
        sums_ref[0:1], sums_ref[1:2] = frame_sums(dy_ref[...].astype(F32) * mlp)
        sums_ref[2:8] = jnp.zeros((6, width), F32)

    return kernel_call(
        body,
        flags,
        [mlp_own, mlp_recv, bias, resid, cotangent, gates],
        [shape_of((rows, width), BF), shape_of((8, width), F32)],
        pins=(0, 3, 4),
        flops=rows * width * 4,
        name="layer_output",
    )


def pack_rows(flags, n_blk, mid, gate2, silu, down_b, up_sums, sum_long, sum_short, bias_long, bias_short):
    width = mid.shape[1]
    cols = bias_long.shape[1]

    def body(flag_ref, mid_ref, g_ref, s_ref, d_ref, m1, m2, t1, t2, sl, ss, bl, bs, out_ref):
        bias = bl[0:1] + bs[0:1]
        bias = jnp.concatenate([bias, jnp.zeros((1, 2 * width - cols), F32)], axis=1)
        rows = jnp.concatenate(
            [mid_ref[0:6], g_ref[0:2], s_ref[...].astype(F32), d_ref[0:1], mid_ref[6:7], m1[0:1] + m2[0:1], t1[0:1] + t2[0:1],
             sl[0:4], ss[0:4], bias[:, :width], bias[:, width:]],
            axis=0,
        ).astype(BF)
        for k in range(n_blk):
            out_ref[k] = rows

    return kernel_call(
        body,
        flags,
        [mid, gate2, silu, down_b, *up_sums, sum_long, sum_short, bias_long, bias_short],
        [shape_of((n_blk, PACK, width), BF)],
        flops=width * PACK,
        name="pack_rows",
    )[0]


def branch_back(flags, hid_own, hid_recv, cotangent, normed, inv_std, branch, mods, weight, lay):
    rows, width = normed.shape
    half = lay.heads * DH

    def body(flag_ref, a_ref, b_ref, dy_ref, n_ref, inv_ref, br_ref, mod_ref, w_ref, rg_ref, bg_ref, keep_ref, send_ref, sums_ref):
        side = flag_ref[1]
        hid = a_ref[...] + b_ref[...].astype(F32)
        norm = n_ref[...]
        scale = per_frame(hid.shape, mod_ref[4:5], mod_ref[5:6])
        resid = dy_ref[...].astype(F32) + norm_back(hid * (1.0 + scale), norm, inv_ref[:, 0:1])
        rg_ref[...] = resid
        gate = per_frame(hid.shape, mod_ref[0:1], mod_ref[1:2])
        low = (gate * resid).astype(BF)
        bg_ref[...] = low
        for out_ref, which in ((keep_ref, side), (send_ref, 1 - side)):
            grad = dot_lanes(low, w_ref[pl.ds(pl.multiple_of(which * half, half), half), :])
            for pair in range(lay.heads // 2):
                one, two = split_pair(grad[:, pair * LANES : (pair + 1) * LANES], lay.top)
                out_ref[2 * pair] = one.astype(BF)
                out_ref[2 * pair + 1] = two.astype(BF)
        sums_ref[0:1], sums_ref[1:2] = frame_sums(resid * br_ref[...])
        sums_ref[2:3], sums_ref[3:4] = frame_sums(hid)
        sums_ref[4:5], sums_ref[5:6] = frame_sums(hid * norm)
        sums_ref[6:7] = jnp.sum(low.astype(F32), axis=0, keepdims=True)
        sums_ref[7:8] = jnp.zeros((1, width), F32)

    packed = shape_of((lay.heads, lay.top, LANES), BF)
    return kernel_call(
        body,
        flags,
        [hid_own, hid_recv, cotangent, normed, inv_std, branch, mods, weight],
        [shape_of((rows, width), F32), shape_of((rows, width), BF), packed, packed, shape_of((8, width), F32)],
        pins=(0, 2, 3, 4, 5, 6),
        out_pins=(0,),
        vmem=24,
        flops=2 * rows * width * width,
        name="branch_back",
    )


def qkv_back(flags, grads, tok_own, tok_oth, weight, lay, is_long):
    rows, width = tok_own.shape
    cols = lay.heads * DH
    half = cols // 2

    def body(flag_ref, g_ref, own_ref, oth_ref, w_ref, hid_ref, low_ref, gm_ref, gt_ref, bias_ref, sums_ref, q_ref, acc_ref):
        step = pl.program_id(0)
        core = flag_ref[2]

        @pl.when(step == 0)
        def _():
            for pair in range(lay.heads // 2):
                one, two = g_ref[2 * pair, :rows, :].astype(F32), g_ref[2 * pair + 1, :rows, :].astype(F32)
                low = lane_low(one.shape)
                lanes = slice(pair * LANES, (pair + 1) * LANES)
                q_ref[0, :, lanes] = jnp.where(low, one, swap_halves(two)).astype(BF)
                q_ref[1, :, lanes] = jnp.where(low, swap_halves(one), two).astype(BF)
                one, two = g_ref[2 * pair, lay.vrow :, :].astype(F32), g_ref[2 * pair + 1, lay.vrow :, :].astype(F32)
                q_ref[2, :, lanes] = join_pair(one, two, rows).astype(BF)

        value = q_ref[step]
        part = dot_lanes(value, w_ref[...])

        @pl.when(step == 0)
        def _():
            acc_ref[...] = part

        @pl.when(step > 0)
        def _():
            acc_ref[...] += part

        first = core == 0
        gm_ref[...] = jnp.where(first, value[:, :half], value[:, half:])
        gt_ref[...] = jnp.where(first, value[:, half:], value[:, :half])
        bias_ref[...] = jnp.broadcast_to(jnp.sum(value.astype(F32), axis=0, keepdims=True), bias_ref.shape)

        @pl.when(step == 2)
        def _():
            hid = acc_ref[...]
            hid_ref[...] = hid
            low_ref[...] = hid.astype(BF)
            mine = (flag_ref[0] == 1) if is_long else (flag_ref[0] == 0)
            normed, _ = norm_rows(jnp.where(mine, own_ref[...].astype(F32), oth_ref[...].astype(F32)))
            sums_ref[0:1], sums_ref[1:2] = frame_sums(hid)
            sums_ref[2:3], sums_ref[3:4] = frame_sums(hid * normed)
            sums_ref[4:8] = jnp.zeros((4, width), F32)

    return kernel_call(
        body,
        flags,
        [grads, tok_own, tok_oth, weight],
        [
            shape_of((rows, width), F32),
            shape_of((rows, width), BF),
            shape_of((rows, 3 * half), BF),
            shape_of((rows, 3 * half), BF),
            shape_of((8, 3 * cols), F32),
            shape_of((8, width), F32),
        ],
        specs=[None, None, None, pl.BlockSpec((width, cols), lambda j, f: (0, 2 * j + f[1]))],
        out_specs=[
            None, None,
            pl.BlockSpec((rows, half), lambda j, f: (0, j)),
            pl.BlockSpec((rows, half), lambda j, f: (0, j)),
            pl.BlockSpec((8, cols), lambda j, f: (0, j)),
            None,
        ],
        pins=(1, 2),
        out_pins=(0,),
        grid=(3,),
        scratch=[pltpu.VMEM((3, rows, cols), BF), pltpu.VMEM((rows, width), F32)],
        flops=6 * rows * width * cols,
        name="qkv_back_long" if is_long else "qkv_back_short",
    )


def token_back(flags, hid_long, hid_short, recv, tokens, resid_grad, mods, lay):
    rows, width = tokens.shape

    def body(flag_ref, l_ref, s_ref, r_ref, tok_ref, rg_ref, mod_ref, out_ref):
        hid = jnp.where(flag_ref[0] == 1, l_ref[...], s_ref[...]) + r_ref[...].astype(F32)
        normed, inv_std = norm_rows(tok_ref[...].astype(F32))
        scale = per_frame(hid.shape, mod_ref[0:1, width : 2 * width], mod_ref[1:2, width : 2 * width])
        out_ref[...] = rg_ref[...] + norm_back(hid * (1.0 + scale), normed, inv_std)

    return kernel_call(
        body,
        flags,
        [hid_long, hid_short, recv, tokens, resid_grad, mods],
        [shape_of((rows, width), F32)],
        pins=(0, 1, 3, 4, 5),
        flops=rows * width * 20,
        name="token_back",
    )[0]


def add_head_rows(flags, part, got, send, keep, order):
    half_blk, total, width = send.shape
    n_blk = 2 * half_blk
    rows = part.shape[1] // n_blk
    bit = order[0]

    def body(flag_ref, part_ref, got_ref, send_in, keep_in, send_ref, keep_ref):
        both = (part_ref[flag_ref[2]].astype(F32) + got_ref[...].astype(F32)).astype(BF)
        for target in range(n_blk):
            place = relative_place(target, flag_ref[4], n_blk)
            at = ((place >> (bit + 1)) << bit) | (place & ((1 << bit) - 1))
            value = both[target * rows : (target + 1) * rows]
            sent = (place >> bit) & 1

            @pl.when(sent == 1)
            def _(value=value, at=at):
                send_ref[at] = value

            @pl.when(sent == 0)
            def _(value=value, at=at):
                keep_ref[at] = value

    block = pl.BlockSpec((half_blk, rows, width), lambda i, f: (0, (total - rows) // rows, 0))
    return kernel_call(
        body,
        flags,
        [part, got, send, keep],
        [shape_of(send.shape, BF)] * 2,
        specs=[None, None, pl.BlockSpec(memory_space=pl.ANY), pl.BlockSpec(memory_space=pl.ANY)],
        out_specs=[block, block],
        pins=(2, 3),
        out_pins=(0, 1),
        aliases={3: 0, 4: 1},
        flops=rows * width * n_blk,
        name="add_head_rows",
    )


def group_spec(pair, rows, wide, moves, per):
    index = pair[1]
    if index is None:
        return pl.BlockSpec((rows, wide), lambda i, f: (0, i // per if moves else 0))
    return pl.BlockSpec((None, rows, wide), lambda i, f: (index, 0, i // per if moves else 0))


def split_weight_grads(flags, lefts, rights, n_blk, orders, extra, name):
    count = len(lefts)
    rows, depth = lefts[0][0].shape[-2:]
    pieces = len(orders)
    cols = rights[0][0].shape[-1] // pieces
    tall = depth // n_blk
    wide = max(tall, LANES)
    per = wide // tall

    def body(flag_ref, *refs):
        outs = refs[2 * count :]
        acc = dot_rows(refs[0][...], refs[count][...])
        for k in range(1, count):
            acc += dot_rows(refs[k][...], refs[count + k][...])
        low = acc.astype(BF)
        for member in range(per):
            part = low[member * tall : (member + 1) * tall]
            place = relative_place(pl.program_id(0) * per + member, flag_ref[4], n_blk)
            for piece, order in enumerate(orders):
                bit = order[0]
                at = ((place >> (bit + 1)) << bit) | (place & ((1 << bit) - 1))
                value = part[:, piece * cols : (piece + 1) * cols]
                sent = (place >> bit) & 1

                @pl.when(sent == 1)
                def _(value=value, at=at, piece=piece):
                    outs[2 * piece][at, :tall] = value

                @pl.when(sent == 0)
                def _(value=value, at=at, piece=piece):
                    outs[2 * piece + 1][at, :tall] = value

    return kernel_call(
        body,
        flags,
        [array for array, _ in [*lefts, *rights]],
        [shape_of((n_blk // 2, tall + extra, cols), BF)] * (2 * pieces),
        specs=[group_spec(pair, rows, wide, True, 1) for pair in lefts]
        + [group_spec(pair, rows, cols * pieces, False, 1) for pair in rights],
        grid=(depth // wide,),
        flops=2 * count * rows * depth * cols * pieces,
        name=name,
    )


def head_weight_grads(flags, longs, shorts, grad_own, grad_oth, lay):
    rows, width = grad_own.shape
    pairs = lay.heads // 2

    def body(flag_ref, l_ref, s_ref, go_ref, gt_ref, out_ref):
        own_long = flag_ref[0] == 1
        grads = jnp.where(own_long, go_ref[...], gt_ref[...]), jnp.where(own_long, gt_ref[...], go_ref[...])
        for pair in range(pairs):
            acc = 0.0
            for ref, grad in zip((l_ref, s_ref), grads):
                left = join_pair(ref[2 * pair].astype(F32), ref[2 * pair + 1].astype(F32), rows).astype(BF)
                acc = acc + dot_rows(left, grad)
            out_ref[pair * LANES : (pair + 1) * LANES, :] = acc.astype(BF)

    return kernel_call(
        body,
        flags,
        [longs, shorts, grad_own, grad_oth],
        [shape_of((lay.heads * DH, width), BF)],
        pins=(0, 1),
        flops=4 * rows * width * lay.heads * DH,
        name="head_weight_grads",
    )[0]


def relative_place(target, here, n_blk):
    relative = target ^ here
    return relative ^ ((relative >> 1) & (10 & (n_blk - 1)))


def hop_of(bit):
    return (1 << bit) if bit == 0 or bit % 2 == 1 else (1 << bit) | (1 << (bit - 1))


class CubeSum:
    def __init__(self, send, keep, n_blk, order):
        self.n_blk, self.order, self.at = n_blk, order, 0
        self.bits = n_blk.bit_length() - 1
        self.axes = [bit for bit in range(self.bits)[::-1] if bit != order[0]]
        self.send = send.reshape((2,) * (self.bits - 1) + send.shape[1:])
        self.keep = keep.reshape((2,) * (self.bits - 1) + keep.shape[1:])
        self.value = None

    def step(self, starts=(), ends=()):
        hop = hop_of(self.order[self.at])
        send = after(self.send, *starts) if starts else self.send
        got = lax.ppermute(send, "blk", [(i, i ^ hop) for i in range(self.n_blk)])
        if ends:
            got = after(got, *ends)
        value = self.keep.astype(F32) + got.astype(F32)
        self.at += 1
        if self.at < self.bits:
            axis = self.axes.index(self.order[self.at])
            self.axes.pop(axis)
            index = (slice(None),) * axis
            value = value.astype(BF)
            self.send, self.keep = value[index + (1,)], value[index + (0,)]
        self.value = value
        return value

    def finish(self):
        while self.at < self.bits:
            self.step()
        return self.value


def lay_out_rows(flags, gathered, split, ff, name):
    n_uly, rows, total = gathered.shape
    cols = (total - split) // 3

    def body(flag_ref, in_ref, up_ref, attn_ref):
        for u in range(n_uly):
            for i in range(split // LANES):
                at = (i * n_uly + u) * LANES
                up_ref[:, at : at + LANES] = in_ref[u, :, i * LANES : (i + 1) * LANES].astype(F32)
            for j in range(3):
                at = (j * n_uly + u) * cols
                attn_ref[:, at : at + cols] = in_ref[u, :, split + j * cols : split + (j + 1) * cols].astype(F32)

    return kernel_call(
        body,
        flags,
        [gathered],
        [shape_of((rows, ff), F32), shape_of((rows, 3 * n_uly * cols), F32)],
        flops=rows * total,
        name=name,
    )


def modulation_grads(flags, long_rows, gathered, row_out, name):
    total, width = gathered.shape
    quarter = total // 4

    def body(flag_ref, long_ref, g_ref, out_ref, sums_ref, part_ref):
        start = flag_ref[5]
        block = pl.multiple_of((start // LANES) * LANES, LANES)
        silu = g_ref[:, pl.ds(block, LANES)].astype(F32)
        parts = [silu[k * quarter : (k + 1) * quarter] for k in (1, 0, 3, 2)]
        mate = jnp.concatenate(parts, axis=0)
        own_long = long_ref[...] > 0.5

        def place_of(index):
            return index - PACK * ((index * 2731) >> 16)

        place = place_of(lax.broadcasted_iota(jnp.int32, (total, LANES), 0))

        def aligned(value, base):
            return jnp.where((place == base) | (place == base + 1), pltpu.roll(value, (base - 8) % total, 0), 0.0)

        def owner(base, is_long):
            return jnp.where(own_long == is_long, aligned(silu, base), aligned(mate, base))

        lefts = [
            owner(14, True) + owner(18, False),
            owner(16, True) + owner(20, False),
            aligned(silu, 0),
            aligned(silu, 2),
            aligned(silu, 4),
            aligned(silu, 6),
        ]
        for k, left in enumerate(lefts):
            part_ref[...] = dot_rows(left.astype(BF), g_ref[...])
            out_ref[:, k * width : (k + 1) * width] = part_ref[pl.ds(pl.multiple_of(start - block, row_out), row_out), :]
        row = lax.broadcasted_iota(jnp.int32, (32, quarter), 0)
        which = jnp.where(row == place_of(lax.broadcasted_iota(jnp.int32, (32, quarter), 1)), 1.0, 0.0).astype(BF)
        for u in range(4):
            sums_ref[u] = dot(which, g_ref[u * quarter : (u + 1) * quarter, :])

    return kernel_call(
        body,
        flags,
        [long_rows, gathered],
        [shape_of((row_out, 6 * width), F32), shape_of((4, 32, width), F32)],
        scratch=[pltpu.VMEM((LANES, width), F32)],
        vmem=max(16, 16 * total // 768),
        flops=total * width * LANES * 12,
        name=name,
    )


def after(value, *earlier):
    return lax.optimization_barrier((value,) + earlier)[0]


def rotary_static(frames):
    n_time, n_row = DH // 8, 3 * DH // 16
    cosine = np.zeros((frames * PATCH, LANES), np.float32)
    sine = np.zeros((frames * PATCH, LANES), np.float32)
    patch = np.arange(frames * PATCH) % PATCH
    for group, place in ((0, patch // GRID), (1, patch % GRID)):
        for j in range(n_row):
            freq = np.exp(np.float32(-math.log(10000.0)) * np.float32(j) / np.float32(n_row)).astype(np.float32)
            angle = (place.astype(np.float32) * freq).astype(np.float64)
            pair = n_time + group * n_row + j
            for head in (0, HALF):
                cosine[:, head + 2 * pair] = np.cos(angle)
                cosine[:, head + 2 * pair + 1] = np.cos(angle)
                sine[:, head + 2 * pair] = -np.sin(angle)
                sine[:, head + 2 * pair + 1] = np.sin(angle)
    return cosine, sine


def rotary_time(times):
    n_time = DH // 8
    lane = jnp.arange(LANES, dtype=jnp.int32)
    pair = (lane % HALF) // 2
    freq = jnp.exp(-math.log(10000.0) * pair.astype(F32) / float(n_time))
    angle = times.astype(F32)[:, None] * freq[None, :]
    live = (pair < n_time)[None, :]
    sign = jnp.where(lane % 2 == 0, -1.0, 1.0)[None, :]
    return jnp.where(live, jnp.cos(angle), 0.0), jnp.where(live, sign * jnp.sin(angle), 0.0)


class Layout:
    def __init__(self, rows, heads, parts):
        self.rows = rows
        self.heads = heads
        self.parts = parts
        self.top = round_up(-(-rows // 2), 16)
        self.vrow = round_up(rows, 16)


def on_device(
    tokens, cotangent, noise_embed, frame_clip, frame_index, mod_weight, mod_bias, attn_weight, attn_bias,
    proj_weight, proj_bias, up_weight, up_bias, down_weight, down_bias,
):
    n_uly = lax.axis_size("uly")
    n_blk = lax.axis_size("blk")
    blk = lax.axis_index("blk")
    uly = lax.axis_index("uly")
    rows, width = tokens.shape
    frames = noise_embed.shape[0]
    side, core = uly // 2, uly % 2
    heads = width // DH // 2
    parts = n_blk // heads
    lay = Layout(rows, heads, parts)
    dev = blk * n_uly + uly

    def swap_side(value):
        return lax.ppermute(value, "uly", [(i, i ^ 2) for i in range(n_uly)])

    def swap_core(value):
        return lax.ppermute(value, "uly", [(i, i ^ 1) for i in range(n_uly)])

    def spread(value):
        return lax.all_to_all(value, "blk", split_axis=0, concat_axis=0, tiled=True)

    def gather_rest(many):
        both = jnp.stack([many, swap_side(many)])
        return jnp.stack([both, swap_core(both)])

    long_first = frame_clip[::FB] == n_blk
    own_long_b = lax.dynamic_index_in_dim(long_first, blk, 0, False) == (side == 0)
    own_long = own_long_b.astype(jnp.int32)
    row_out = width // (n_blk * n_uly)
    flags = jnp.stack([own_long, side, core, blk // heads, blk, dev * row_out]).astype(jnp.int32)

    tok_oth = swap_side(tokens)
    silu = jax.nn.silu(noise_embed.astype(F32)).astype(BF)
    bias = mod_bias.astype(F32)
    first_mod = dot(silu, mod_weight[:, : 2 * width]) + bias[: 2 * width]
    first_mods = jnp.concatenate([first_mod, swap_side(first_mod)], axis=0)
    rest_mod = dot(after(silu, first_mod), mod_weight[:, 2 * width :]) + bias[2 * width :]
    first_mods, rest_mod = lax.optimization_barrier((first_mods, rest_mod))

    block_time = frame_index.reshape(n_blk, FB)
    head_time, tail_time = block_time[:, : FB // 2], block_time[:, FB // 2 :]
    long_times = lax.dynamic_slice_in_dim(jnp.where(long_first[:, None], head_time, tail_time), core * frames, frames, 1)
    short_times = lax.dynamic_slice_in_dim(jnp.where(long_first[:, None], tail_time, head_time), core * frames, frames, 1)
    short_times = lax.dynamic_index_in_dim(short_times, blk, 0, False)
    time_cos, time_sin = rotary_time(jnp.concatenate([lax.dynamic_index_in_dim(long_times, blk, 0, False), short_times]))
    long_cos, long_sin = rotary_time(long_times.reshape(-1))
    short_cos, short_sin = time_cos[frames:, None], time_sin[frames:, None]
    long_cos, long_sin = long_cos[:, None], long_sin[:, None]
    tab_cos, tab_sin = (jnp.asarray(t) for t in rotary_static(frames))

    gate2 = rest_mod[:, 3 * width :]
    mid_mods = jnp.concatenate([rest_mod[:, :width], rest_mod[:, width : 2 * width], rest_mod[:, 2 * width : 3 * width]], axis=0)
    mid_mods = jnp.concatenate([mid_mods, jnp.zeros((2, width), F32)], axis=0)
    hidden1, qkv_long, qkv_short = tokens_to_qkv(
        flags, tokens, tok_oth, first_mods, attn_weight, attn_bias.astype(F32)[None], tab_cos, tab_sin, time_cos, time_sin, lay
    )
    sent = jnp.concatenate([qkv_long] * parts, axis=0) if parts > 1 else qkv_long
    long_own = spread(sent)
    short_oth = swap_core(qkv_short)
    out_short, ot_short, lse_short = attend(flags, qkv_short, short_oth, lay, False)
    mlp_grad, down_b = scale_cotangent(flags, after(cotangent, qkv_long), gate2)
    mlp_grad_oth = swap_side(mlp_grad)
    long_own, out_short, mlp_grad = lax.optimization_barrier((long_own, out_short, mlp_grad))
    long_oth = swap_core(long_own)
    out_long_all, ot_long, lse_long = attend(flags, long_own, long_oth, lay, True)
    out_long_all, mlp_grad_oth = lax.optimization_barrier((out_long_all, mlp_grad_oth))

    def own_part(value):
        if parts == 1:
            return value
        return lax.dynamic_slice_in_dim(value, ((blk // 2) % parts) * heads, heads, 0)

    out_long = own_part(spread(out_long_all))
    out_recv = swap_side(jnp.where(own_long_b, out_short, out_long))
    branch, resid, normed2, inv2, hidden2 = project_and_norm(
        flags, out_long, out_short, out_recv, proj_weight, proj_bias.astype(F32)[None], tokens, mid_mods, lay
    )

    hidden2_oth = swap_side(hidden2)
    up_b = up_bias.astype(F32)[None]
    mine, send, bm, bt, mlp_own, hid_own = mlp_both(
        flags, hidden2, mlp_grad, up_weight, up_b, down_weight, lay, F32, "mlp_own"
    )
    hidden2_oth, mlp_own, hid_own = lax.optimization_barrier((hidden2_oth, mlp_own, hid_own))
    mine2, send2, bm2, bt2, mlp_oth, hid_oth = mlp_both(
        flags, hidden2_oth, mlp_grad_oth, up_weight, up_b, down_weight, lay, BF, "mlp_other"
    )
    hid_recv = swap_side(hid_oth)

    got, got2 = swap_core(send), swap_core(send2)
    hid_c, hid_c2, mg_c, mg_c2 = (swap_core(v) for v in (hidden2, hidden2_oth, mlp_grad, mlp_grad_oth))
    plain = lambda *arrays: [(v, None) for v in arrays]
    blocks = [mine, mine2, got, got2]
    bits = list(range(n_blk.bit_length() - 1))
    orders = [bits[k % len(bits) :] + bits[: k % len(bits)] for k in range(3)]
    down_order, up_order = [0, 2, 1] + bits[3:], [1, 0, 2] + bits[3:]
    down_send, down_keep = split_weight_grads(
        flags, [(v, 0) for v in blocks], plain(mlp_grad, mlp_grad_oth, mg_c, mg_c2), n_blk, [down_order], 0, "down_grads"
    )
    hid_recv, down_send, down_keep = lax.optimization_barrier((hid_recv, down_send, down_keep))

    resid_grad, branch_grad, do_keep, do_send, mid_sums = branch_back(
        flags, hid_own, hid_recv, cotangent, normed2, inv2, branch, mid_mods, proj_weight, lay
    )
    down_sum = CubeSum(down_send, down_keep, n_blk, down_order)
    do_recv = swap_side(do_send)
    hid_late = after(hidden2, do_send)
    up_send, up_keep = split_weight_grads(
        flags, plain(hid_late, hidden2_oth, hid_c, hid_c2), [(v, 1) for v in blocks], n_blk, [up_order], width // 4 // n_blk, "up_grads"
    )
    do_recv, up_send, up_keep = lax.optimization_barrier((do_recv, up_send, up_keep))
    do_long = jnp.where(own_long_b, do_keep, do_recv)
    if parts > 1:
        hot = (jnp.arange(parts) == (blk // 2) % parts)[:, None, None, None]
        do_sent = jnp.where(hot, do_long[None], 0).reshape((n_blk,) + do_long.shape[1:])
    else:
        do_sent = do_long
    do_all = spread(do_sent)
    dq_s, mine_s, theirs_s = attend_back(
        flags, qkv_short, short_oth, [do_keep, do_recv], ot_short, lse_short, tab_cos, tab_sin, short_cos, short_sin, lay, False
    )
    branch_grad_oth = swap_side(after(branch_grad, do_recv))
    mlp_recv = swap_side(after(mlp_oth, branch_grad_oth))
    do_all, dq_s, mine_s, theirs_s, branch_grad_oth = lax.optimization_barrier((do_all, dq_s, mine_s, theirs_s, branch_grad_oth))
    proj_part = head_weight_grads(flags, out_long, out_short, branch_grad, branch_grad_oth, lay)
    proj_part = proj_part.reshape(2, -1, width)
    proj_got = swap_core(jnp.where(core == 0, proj_part[1], proj_part[0]))
    up_send, up_keep = add_head_rows(flags, proj_part, proj_got, up_send, up_keep, up_order)
    up_sum = CubeSum(up_send, up_keep, n_blk, up_order)
    down_sum.step()
    do_all, up_sum.send, down_sum.send, down_sum.keep = lax.optimization_barrier(
        (do_all, up_sum.send, down_sum.send, down_sum.keep)
    )

    dq_l, mine_l, theirs_l = attend_back(
        flags, long_own, long_oth, [do_all], ot_long, lse_long, tab_cos, tab_sin, long_cos, long_sin, lay, True
    )
    grads_sent = finish_keys(flags, dq_l, mine_l, swap_core(theirs_l), tab_cos, tab_sin, long_cos, long_sin, lay, True)
    grads_all = spread(grads_sent)
    if parts > 1:
        grads_long = jnp.sum(grads_all.astype(F32).reshape((parts, heads) + grads_all.shape[1:]), axis=0).astype(BF)
    else:
        grads_long = grads_all

    theirs_s = swap_core(theirs_s)
    mlp_recv, dq_s, theirs_s, _ = lax.optimization_barrier((mlp_recv, dq_s, theirs_s, grads_sent))
    down_sum.step(ends=(grads_sent,))
    up_sum.step(ends=(grads_sent,))
    grads_short = finish_keys(flags, dq_s, mine_s, theirs_s, tab_cos, tab_sin, short_cos, short_sin, lay, False)
    hidS, hidS_low, gmS, gtS, abS, sumS = qkv_back(flags, grads_short, tokens, tok_oth, attn_weight, lay, False)
    output, gate2_sums = layer_output(flags, mlp_own, mlp_recv, down_bias.astype(F32)[None], resid, cotangent, gate2)
    h1_core = swap_core(hidden1)
    gtS_got = swap_core(gtS)
    grads_long, output, h1_core, gtS_got, hidS_low, up_sum.send, up_sum.keep, down_sum.send, down_sum.keep = lax.optimization_barrier(
        (grads_long, output, h1_core, gtS_got, hidS_low, up_sum.send, up_sum.keep, down_sum.send, down_sum.keep)
    )

    hidL, hidL_low, gmL, gtL, abL, sumL = qkv_back(flags, grads_long, tokens, tok_oth, attn_weight, lay, True)
    gtL_got = swap_core(gtL)
    hid1_recv = swap_side(jnp.where(own_long_b, hidS_low, hidL_low))
    pack = pack_rows(flags, n_blk, mid_sums, gate2_sums, silu, down_b, (bm, bm2, bt, bt2), sumL, sumS, abL, abS)
    halves = split_weight_grads(
        flags, [(hidden1, 0), (hidden1, 1), (h1_core, 0), (h1_core, 1)], plain(gmL, gmS, after(gtL_got, pack), gtS_got),
        n_blk, orders, 0, "attn_grads"
    )
    many = spread(pack)
    hid1_recv, many, *halves = lax.optimization_barrier((hid1_recv, many, *halves))
    packs = gather_rest(many).reshape(-1, width)
    attn_sums = [CubeSum(halves[2 * k], halves[2 * k + 1], n_blk, order) for k, order in enumerate(orders)]
    for part in attn_sums:
        part.step()
    up_sum.step(starts=(attn_sums[0].send,))
    down_sum.step(starts=(attn_sums[0].send,))
    attn_mine = [part.finish().astype(BF) for part in attn_sums]
    up_all, down_mine = up_sum.finish(), down_sum.finish()
    up_mine, proj_mine = up_all[: width // n_blk].astype(BF), up_all[width // n_blk :]
    token_grad = token_back(flags, hidL, hidS, hid1_recv, tokens, resid_grad, first_mod, lay)

    quarters = jnp.concatenate([up_mine] + attn_mine, axis=1)
    quarters = lax.all_to_all(quarters.reshape(n_uly, row_out, -1), "uly", 0, 0, tiled=True)
    ff = up_weight.shape[1]
    g_up_weight, g_attn_weight = lay_out_rows(flags, quarters, ff // n_uly, ff, "lay_out_rows")

    g = ff // (n_blk * n_uly)

    def down_home(index):
        b, u = divmod(index, n_uly)
        start = ((b * g // LANES) * n_uly + u) * LANES + (b * g) % LANES
        return start // g

    down_map = [(i, down_home(i)) for i in range(n_blk * n_uly)]
    g_down_weight = down_mine.astype(F32)
    if any(a != b for a, b in down_map):
        g_down_weight = lax.ppermute(g_down_weight, ("blk", "uly"), down_map)
    proj_map = [(b * n_uly + u, u * n_blk + b) for b in range(n_blk) for u in range(n_uly)]
    g_proj_weight = lax.ppermute(proj_mine.astype(F32), ("blk", "uly"), proj_map)

    own_long_all = (long_first[None, :] == ((side ^ jnp.arange(2)) == 0)[:, None]).astype(F32)
    long_rows = jnp.broadcast_to(own_long_all[None, :, :, None, None], (2, 2, n_blk, PACK, LANES)).reshape(-1, LANES)
    g_mod_weight, sums = modulation_grads(flags, long_rows, packs, row_out, "modulation_grads")

    def cut(vector, size):
        return lax.dynamic_slice_in_dim(vector, dev * size, size, 0)

    total_dev = n_blk * n_uly
    whole_sum = jnp.sum(sums, axis=0)
    mod_line = jnp.concatenate([whole_sum[14:16] + whole_sum[18:20], whole_sum[16:18] + whole_sum[20:22], whole_sum[0:8]], axis=0)
    g_mod_bias = cut(mod_line.reshape(6, 2, width).sum(axis=1).reshape(-1), 6 * width // total_dev)
    g_down_bias = cut(whole_sum[10], width // total_dev)
    g_proj_bias = cut(whole_sum[11], width // total_dev)
    first = dev * g
    steps = (first // LANES) % n_uly ^ uly
    core_step, side_step = steps % 2, steps // 2
    up_mine_sum = sums[2 * core_step + side_step, 12] + sums[2 * (1 - core_step) + side_step, 13]
    g_up_bias = lax.dynamic_slice_in_dim(up_mine_sum, first // (LANES * n_uly) * LANES + first % LANES, g, 0)
    by_step = (sums[0:2, 22:24] + sums[2:4, 22:24]).reshape(2, 2 * width)[:, : 3 * width // 2]
    by_side = jnp.where(side == 0, by_step, by_step[::-1])
    g_attn_bias = cut(jnp.swapaxes(by_side.reshape(2, 3, width // 2), 0, 1).reshape(-1), 3 * width // total_dev)
    return (
        output, token_grad, g_mod_weight, g_mod_bias, g_attn_weight, g_attn_bias,
        g_proj_weight, g_proj_bias, g_up_weight, g_up_bias, g_down_weight, g_down_bias,
    )


def solution(mesh):
    row = P(("blk", "uly"), None)
    flat = P(("blk", "uly"))
    in_specs = (row, row, row) + (P(),) * 12
    out_specs = (row, row, row, flat, row, flat, row, flat, row, flat, row, flat)
    return jax.shard_map(on_device, mesh=mesh, in_specs=in_specs, out_specs=out_specs, check_vma=False)
```

```python
import functools
import math

import jax
import jax.numpy as jnp
import numpy as np
from jax import lax
from jax.experimental import pallas as pl
from jax.experimental.pallas import tpu as pltpu
from jax.sharding import PartitionSpec as P

DH = 64
GRID = 10
FB = 8
PATCH = 100
HALF = 64
LANES = 128

GELU_C = 0.7978845608028654
GELU_K = 0.044715
NEG_BIG = -1e30
MIB = 1 << 20
UNROLL = 2
PACK = 24

BF = jnp.bfloat16
F32 = jnp.float32


def round_up(value, step):
    return -(-value // step) * step


def lane_low(shape):
    return lax.broadcasted_iota(jnp.int32, shape, len(shape) - 1) < HALF


def first_frame(shape):
    return lax.broadcasted_iota(jnp.int32, shape, 0) < PATCH


def swap_halves(value):
    return pltpu.roll(value, HALF, 1)


def swap_pairs(value):
    even = lax.broadcasted_iota(jnp.int32, value.shape, 1) % 2 == 0
    return jnp.where(even, pltpu.roll(value, LANES - 1, 1), pltpu.roll(value, 1, 1))


def per_frame(shape, first, second):
    return jnp.where(first_frame(shape), jnp.broadcast_to(first, shape), jnp.broadcast_to(second, shape))


def frame_sums(value):
    head = first_frame(value.shape)
    one = jnp.sum(jnp.where(head, value, 0.0), axis=0, keepdims=True)
    two = jnp.sum(jnp.where(head, 0.0, value), axis=0, keepdims=True)
    return one, two


def norm_rows(values):
    center = values - jnp.mean(values, axis=-1, keepdims=True)
    inv_std = lax.rsqrt(jnp.mean(center * center, axis=-1, keepdims=True) + 1e-06)
    return center * inv_std, inv_std


def norm_back(grad, normed, inv_std):
    return inv_std * (
        grad
        - jnp.mean(grad, axis=-1, keepdims=True)
        - normed * jnp.mean(grad * normed, axis=-1, keepdims=True)
    )


def dot(left, right):
    return jnp.dot(left, right, preferred_element_type=F32)


def dot_lanes(left, right):
    return lax.dot_general(left, right, (((1,), (1,)), ((), ())), preferred_element_type=F32)


def dot_rows(left, right):
    return lax.dot_general(left, right, (((0,), (0,)), ((), ())), preferred_element_type=F32)


def split_pair(value, rows_top):
    rows = value.shape[0]
    top = value[:rows_top]
    bottom = jnp.concatenate(
        [value[rows_top:], jnp.zeros((2 * rows_top - rows, LANES), value.dtype)], axis=0
    )
    low = lane_low(top.shape)
    return jnp.where(low, top, swap_halves(bottom)), jnp.where(low, swap_halves(top), bottom)


def join_pair(one, two, rows):
    rows_top = one.shape[0]
    low = lane_low(one.shape)
    top = jnp.where(low, one, swap_halves(two))
    bottom = jnp.where(low, swap_halves(one), two)
    return jnp.concatenate([top, bottom[: rows - rows_top]], axis=0)


def smem():
    return pl.BlockSpec(memory_space=pltpu.SMEM)


def whole(shape):
    return pl.BlockSpec(shape, lambda *_: (0,) * len(shape))


def kernel_call(body, flags, args, outs, *, specs=None, out_specs=None, grid=(1,), scratch=(), vmem=16, pins=(), out_pins=(), aliases=None, flops, name):
    specs = specs or [None] * len(args)
    out_specs = out_specs or [None] * len(outs)
    return pl.pallas_call(
        body,
        grid_spec=pltpu.PrefetchScalarGridSpec(
            num_scalar_prefetch=1,
            grid=grid,
            in_specs=[spec or whole(a.shape) for spec, a in zip(specs, args)],
            out_specs=[spec or whole(o.shape) for spec, o in zip(out_specs, outs)],
            scratch_shapes=list(scratch),
        ),
        out_shape=[pltpu.HBM(o.shape, o.dtype) if k in out_pins else o for k, o in enumerate(outs)],
        input_output_aliases=aliases or {},
        compiler_params=pltpu.CompilerParams(vmem_limit_bytes=vmem * MIB),
        cost_estimate=pl.CostEstimate(flops=flops // 4096, bytes_accessed=4096, transcendentals=0),
        name=name,
    )(flags, *[pltpu.with_memory_space_constraint(a, pltpu.HBM) if a.size >= MIB or k in pins else a for k, a in enumerate(args)])


def shape_of(dims, dtype):
    return jax.ShapeDtypeStruct(dims, dtype)


def tokens_to_qkv(flags, tok_own, tok_oth, mods, weight, bias, tab_cos, tab_sin, time_cos, time_sin, lay):
    rows, width = tok_own.shape
    cols = lay.heads * DH

    def body(flag_ref, own_ref, oth_ref, mod_ref, w_ref, b_ref, tc_ref, ts_ref, qc_ref, qs_ref, hid_ref, long_ref, short_ref, both_ref):
        step = pl.program_id(0)
        own_long = flag_ref[0]

        @pl.when(step == 0)
        def _():
            hidden = []
            for src, base in ((own_ref, 0), (oth_ref, 2)):
                normed, _ = norm_rows(src[...].astype(F32))
                shift = per_frame(normed.shape, mod_ref[base : base + 1, :width], mod_ref[base + 1 : base + 2, :width])
                scale = per_frame(
                    normed.shape, mod_ref[base : base + 1, width : 2 * width], mod_ref[base + 1 : base + 2, width : 2 * width]
                )
                hidden.append(normed * (1.0 + scale) + shift)
            swapped = own_long == 0
            first = jnp.where(swapped, hidden[1], hidden[0])
            second = jnp.where(swapped, hidden[0], hidden[1])
            hid_ref[0] = first.astype(BF)
            hid_ref[1] = second.astype(BF)
            both_ref[...] = jnp.concatenate([first, second], axis=0).astype(BF)

        result = dot(both_ref[...], w_ref[...]) + b_ref[...]
        for slot, out_ref in ((0, long_ref), (1, short_ref)):
            acc = result[slot * rows : (slot + 1) * rows]

            def rotated(pair):
                value = acc[:, pair * LANES : (pair + 1) * LANES]
                cosine = tc_ref[...] + per_frame(value.shape, qc_ref[2 * slot : 2 * slot + 1], qc_ref[2 * slot + 1 : 2 * slot + 2])
                sine = ts_ref[...] + per_frame(value.shape, qs_ref[2 * slot : 2 * slot + 1], qs_ref[2 * slot + 1 : 2 * slot + 2])
                return value * cosine + swap_pairs(value) * sine

            @pl.when(step == 0)
            def _():
                for pair in range(cols // LANES):
                    turned = rotated(pair)
                    out_ref[2 * pair, :rows, :HALF] = turned[:, :HALF].astype(BF)
                    out_ref[2 * pair + 1, :rows, :HALF] = swap_halves(turned)[:, :HALF].astype(BF)

            @pl.when(step == 1)
            def _():
                for pair in range(cols // LANES):
                    turned = rotated(pair)
                    out_ref[2 * pair, :rows, HALF:] = swap_halves(turned)[:, HALF:].astype(BF)
                    out_ref[2 * pair + 1, :rows, HALF:] = turned[:, HALF:].astype(BF)

            @pl.when(step == 2)
            def _():
                for pair in range(cols // LANES):
                    one, two = split_pair(acc[:, pair * LANES : (pair + 1) * LANES], lay.top)
                    out_ref[2 * pair, lay.vrow :, :] = one.astype(BF)
                    out_ref[2 * pair + 1, lay.vrow :, :] = two.astype(BF)

    packed = (lay.heads, lay.vrow + lay.top, LANES)
    return kernel_call(
        body,
        flags,
        [tok_own, tok_oth, mods, weight, bias, tab_cos, tab_sin, time_cos, time_sin],
        [shape_of((2, rows, width), BF), shape_of(packed, BF), shape_of(packed, BF)],
        specs=[
            None, None, None,
            pl.BlockSpec((width, cols), lambda j, f: (0, 2 * j + f[1])),
            pl.BlockSpec((1, cols), lambda j, f: (0, 2 * j + f[1])),
            None, None, None, None,
        ],
        scratch=[pltpu.VMEM((2 * rows, width), BF)],
        out_pins=(0,),
        grid=(3,),
        flops=12 * rows * width * cols,
        name="tokens_to_qkv",
    )


def unpack_values(ref, at, lay):
    part = ref[at, lay.vrow :, :].astype(F32)
    return jnp.concatenate([part, swap_halves(part)[: lay.rows - lay.top]], axis=0)


def hundreds(value):
    return (value * 1311) >> 17


def diag_mask(keys, queries, core):
    key = hundreds(lax.broadcasted_iota(jnp.int32, (keys, 1), 0)) ^ (2 * core)
    query = hundreds(lax.broadcasted_iota(jnp.int32, (1, queries), 1))
    query = ((query & 2) << 1) + (query & 1) + 2 * core
    return key <= query


def load_keys(own_ref, oth_ref, group, lay):
    low = lane_low((lay.rows, LANES))
    halves = [
        jnp.where(low, unpack_values(ref, group, lay), ref[group, : lay.rows, :].astype(F32))
        for ref in (own_ref, oth_ref)
    ]
    return jnp.concatenate(halves, axis=0)


def load_query(own_ref, at, lay):
    value = swap_halves(own_ref[at, : lay.rows, :].astype(F32)) * (1.0 / math.sqrt(DH))
    return jnp.where(lane_low(value.shape), 0.0, value)


def load_rows(load, groups):
    return jnp.concatenate([load(g) for g in groups], axis=0)


def fold_rows(value, op):
    return op(value.reshape(value.shape[0] // 8, 8, value.shape[1]), axis=0)


def unpack_rows(ref, at, lay):
    packed = ref[at].astype(F32)
    grad = jnp.concatenate([packed, swap_halves(packed)[: lay.rows - lay.top]], axis=0)
    return jnp.where(lane_low(grad.shape), grad, 0.0)


def attend(flags, own, oth, lay, long_clip):
    groups = own.shape[0]
    parts = lay.parts if long_clip else 1
    per = 2 if long_clip else 1
    count = groups // per
    keys, queries = 2 * lay.rows * per, lay.rows * per
    depth = count if long_clip else UNROLL

    def body(flag_ref, own_ref, oth_ref, o_ref, ot_ref, lse_ref, kv_ref, vt_ref, st_ref):
        core = flag_ref[2]
        part = flag_ref[3]

        def prepare(tile, slot):
            rows = jnp.concatenate([load_keys(own_ref, oth_ref, per * tile + k, lay) for k in range(per)], axis=0)
            kv_ref[slot] = rows.astype(BF)
            vt_ref[slot] = rows.T[:HALF].astype(BF)

        def block(at, slot):
            query = load_rows(lambda g: load_query(own_ref, g, lay), [per * at + k for k in range(per)]).astype(BF)

            def scores(kt, top):
                score = dot_lanes(kv_ref[kt], query)
                st_ref[kt] = score
                return jnp.maximum(top, fold_rows(score, jnp.max))

            top = jnp.full((8, queries), NEG_BIG, F32)
            if long_clip:
                top = lax.fori_loop(0, at, scores, top)
            score = dot_lanes(kv_ref[slot], query)
            score = jnp.where(diag_mask(keys, queries, core), score, NEG_BIG)
            st_ref[slot] = score
            top = jnp.max(jnp.maximum(top, fold_rows(score, jnp.max)), axis=0, keepdims=True)

            def mix(kt, carry):
                total, acc = carry
                expo = jnp.exp(st_ref[kt] - top)
                total = total + fold_rows(expo, jnp.sum)
                return total, acc + dot(vt_ref[kt], expo.astype(BF))

            zero = (jnp.zeros((8, queries), F32), jnp.zeros((HALF, queries), F32))
            if long_clip:
                total, acc = lax.fori_loop(0, at + 1, mix, zero)
            else:
                total, acc = mix(slot, zero)
            total = jnp.sum(total, axis=0, keepdims=True)
            acc = acc / total
            ot_ref[at] = acc
            lse_ref[at] = jnp.broadcast_to(top + jnp.log(total), (8, queries))
            out = jnp.concatenate([acc, jnp.zeros_like(acc)], axis=0).T
            for k in range(per):
                o_ref[per * at + k] = split_pair(out[k * lay.rows : (k + 1) * lay.rows], lay.top)[0].astype(BF)

        if long_clip:
            def prepare_loop(tile, _):
                prepare(tile, tile)
                return 0

            lax.fori_loop(0, count, prepare_loop, 0)
            if parts > 1:
                o_ref[...] = jnp.zeros_like(o_ref)

            def block_loop(step, _):
                at = step * parts + part if parts > 1 else step
                block(at, at)
                return 0

            lax.fori_loop(0, count // parts, block_loop, 0)
        else:
            def head_loop(step, _):
                for k in range(UNROLL):
                    prepare(UNROLL * step + k, k)
                for k in range(UNROLL):
                    block(UNROLL * step + k, k)
                return 0

            lax.fori_loop(0, count // UNROLL, head_loop, 0)

    pairs = count * (count + 1) // 2 if long_clip else count
    return kernel_call(
        body,
        flags,
        [own, oth],
        [
            shape_of((groups, lay.top, LANES), BF),
            shape_of((count, HALF, queries), F32),
            shape_of((count, 8, queries), F32),
        ],
        scratch=[
            pltpu.VMEM((depth, keys, LANES), BF),
            pltpu.VMEM((depth, HALF, keys), BF),
            pltpu.VMEM((depth, keys, queries), F32),
        ],
        out_pins=(1, 2),
        vmem=max(24, 3 * groups) if long_clip else 16,
        flops=pairs * 16 * keys * queries * DH // parts,
        name="attend_long" if long_clip else "attend_short",
    )


def attend_back(flags, own, oth, d_outs, ot, lse, tab_cos, tab_sin, time_cos, time_sin, lay, long_clip):
    groups = own.shape[0]
    parts = lay.parts if long_clip else 1
    per = 2 if long_clip else 1
    count = groups // per
    keys, queries = 2 * lay.rows * per, lay.rows * per
    depth = count if long_clip else UNROLL

    def body(flag_ref, own_ref, oth_ref, *refs):
        do_refs, refs = refs[: len(d_outs)], refs[len(d_outs) :]
        ot_ref, lse_ref, tc_ref, ts_ref, qc_ref, qs_ref, dq_ref, down_ref, doth_ref, kv_ref, kt_ref, acc_ref = refs
        own_long = flag_ref[0]
        core = flag_ref[2]
        part = flag_ref[3]

        def prepare(tile, slot):
            rows = jnp.concatenate([load_keys(own_ref, oth_ref, per * tile + k, lay) for k in range(per)], axis=0)
            kv_ref[slot] = rows.astype(BF)
            kt_ref[slot] = rows.T[HALF:].astype(BF)
            if long_clip:
                acc_ref[slot] = jnp.zeros((keys, LANES), F32)

        def block(at, slot):
            members = [per * at + k for k in range(per)]
            query = load_rows(lambda g: load_query(own_ref, g, lay), members).astype(BF)
            if long_clip:
                grad = load_rows(lambda g: unpack_rows(do_refs[0], g, lay), members)
            else:
                grad = load_rows(
                    lambda g: jnp.where(own_long == 1, unpack_rows(do_refs[1], g, lay), unpack_rows(do_refs[0], g, lay)), members
                )
            delta = jnp.sum(grad.T[:HALF] * ot_ref[at], axis=0, keepdims=True)
            grad = grad.astype(BF)
            lse_row = lse_ref[at][0:1]

            def tile_back(kt, acc, diag):
                tile = kv_ref[kt]
                prob = jnp.exp(dot_lanes(tile, query) - lse_row)
                if diag:
                    prob = jnp.where(diag_mask(keys, queries, core), prob, 0.0)
                score_grad = (prob * (dot_lanes(tile, grad) - delta)).astype(BF)
                both = dot(score_grad, query) + dot(prob.astype(BF), grad)
                if long_clip:
                    acc_ref[kt] += both
                else:
                    acc_ref[kt] = both
                return acc + dot(kt_ref[kt], score_grad)

            acc = tile_back(slot, jnp.zeros((HALF, queries), F32), True)
            if long_clip:
                acc = lax.fori_loop(0, at, lambda kt, a: tile_back(kt, a, False), acc)
            acc = acc * (1.0 / math.sqrt(DH))
            turned = jnp.concatenate([acc, jnp.zeros_like(acc)], axis=0).T
            for k, group in enumerate(members):
                dq = turned[k * lay.rows : (k + 1) * lay.rows]
                tab = group if long_clip else 0
                cosine = tc_ref[...] + per_frame(dq.shape, qc_ref[2 * tab], qc_ref[2 * tab + 1])
                sine = ts_ref[...] + per_frame(dq.shape, qs_ref[2 * tab], qs_ref[2 * tab + 1])
                dq_ref[group] = (dq * cosine - swap_pairs(dq) * sine).astype(BF)

        def flush(tile, slot):
            for k in range(per):
                down_ref[per * tile + k] = acc_ref[slot, 2 * k * lay.rows : (2 * k + 1) * lay.rows]
                doth_ref[per * tile + k] = acc_ref[slot, (2 * k + 1) * lay.rows : (2 * k + 2) * lay.rows].astype(BF)

        if long_clip:
            def prepare_loop(tile, _):
                prepare(tile, tile)
                return 0

            lax.fori_loop(0, count, prepare_loop, 0)
            if parts > 1:
                dq_ref[...] = jnp.zeros_like(dq_ref)

            def block_loop(step, _):
                at = step * parts + part if parts > 1 else step
                block(at, at)
                return 0

            lax.fori_loop(0, count // parts, block_loop, 0)

            def flush_loop(tile, _):
                flush(tile, tile)
                return 0

            lax.fori_loop(0, count, flush_loop, 0)
        else:
            def head_loop(step, _):
                for k in range(UNROLL):
                    prepare(UNROLL * step + k, k)
                for k in range(UNROLL):
                    block(UNROLL * step + k, k)
                for k in range(UNROLL):
                    flush(UNROLL * step + k, k)
                return 0

            lax.fori_loop(0, count // UNROLL, head_loop, 0)

    pairs = count * (count + 1) // 2 if long_clip else count
    return kernel_call(
        body,
        flags,
        [own, oth, *d_outs, ot, lse, tab_cos, tab_sin, time_cos, time_sin],
        [
            shape_of((groups, lay.rows, LANES), BF),
            shape_of((groups, lay.rows, LANES), F32),
            shape_of((groups, lay.rows, LANES), BF),
        ],
        scratch=[
            pltpu.VMEM((depth, keys, LANES), BF),
            pltpu.VMEM((depth, HALF, keys), BF),
            pltpu.VMEM((depth, keys, LANES), F32),
        ],
        out_pins=(0, 1),
        vmem=max(24, 3 * groups) if long_clip else 20,
        pins=(0, 1) + tuple(range(2 + len(d_outs), 8 + len(d_outs))),
        flops=pairs * 40 * keys * queries * DH // parts,
        name="attend_back_long" if long_clip else "attend_back_short",
    )


def finish_keys(flags, dq, mine, theirs, tab_cos, tab_sin, time_cos, time_sin, lay, long_clip):
    groups = dq.shape[0]

    def body(flag_ref, dq_ref, a_ref, b_ref, tc_ref, ts_ref, qc_ref, qs_ref, out_ref):
        def one(group, _):
            both = a_ref[group] + b_ref[group].astype(F32)
            tab = group if long_clip else 0
            cosine = tc_ref[...] + per_frame(both.shape, qc_ref[2 * tab], qc_ref[2 * tab + 1])
            sine = ts_ref[...] + per_frame(both.shape, qs_ref[2 * tab], qs_ref[2 * tab + 1])
            keys = both * cosine - swap_pairs(both) * sine
            out_ref[group, : lay.rows, :] = jnp.where(lane_low(keys.shape), dq_ref[group].astype(F32), keys).astype(BF)
            out_ref[group, lay.vrow :, :] = split_pair(both, lay.top)[0].astype(BF)
            return 0

        lax.fori_loop(0, groups, one, 0)

    return kernel_call(
        body,
        flags,
        [dq, mine, theirs, tab_cos, tab_sin, time_cos, time_sin],
        [shape_of((groups, lay.vrow + lay.top, LANES), BF)],
        pins=(0, 1),
        vmem=max(16, groups),
        flops=groups * lay.rows * LANES * 10,
        name="finish_keys",
    )[0]


def project_and_norm(flags, long_out, short_out, recv, weight, bias, tokens, mods, lay):
    rows, width = tokens.shape
    half = lay.heads * DH

    def body(flag_ref, long_ref, short_ref, recv_ref, w_ref, b_ref, tok_ref, mod_ref, branch_ref, resid_ref, normed_ref, inv_ref, hid_ref, att_ref):
        own_long = flag_ref[0]
        side = flag_ref[1]
        for pair in range(lay.heads // 2):
            kept = [
                jnp.where(own_long == 1, long_ref[2 * pair + k].astype(F32), short_ref[2 * pair + k].astype(F32)) for k in (0, 1)
            ]
            got = [recv_ref[2 * pair + k].astype(F32) for k in (0, 1)]
            lanes = slice(pair * LANES, (pair + 1) * LANES)
            att_ref[side, :, lanes] = join_pair(kept[0], kept[1], rows).astype(BF)
            att_ref[1 - side, :, lanes] = join_pair(got[0], got[1], rows).astype(BF)
        branch = dot(att_ref[0], w_ref[:half]) + dot(att_ref[1], w_ref[half:]) + b_ref[...]
        branch_ref[...] = branch
        gate = per_frame(branch.shape, mod_ref[0:1], mod_ref[1:2])
        resid = tok_ref[...].astype(F32) + gate * branch
        resid_ref[...] = resid
        normed, inv_std = norm_rows(resid)
        normed_ref[...] = normed
        inv_ref[...] = jnp.broadcast_to(inv_std, inv_ref.shape)
        shift = per_frame(branch.shape, mod_ref[2:3], mod_ref[3:4])
        scale = per_frame(branch.shape, mod_ref[4:5], mod_ref[5:6])
        hid_ref[...] = (normed * (1.0 + scale) + shift).astype(BF)

    full = shape_of((rows, width), F32)
    return kernel_call(
        body,
        flags,
        [long_out, short_out, recv, weight, bias, tokens, mods],
        [full, full, full, shape_of((rows, LANES), F32), shape_of((rows, width), BF)],
        scratch=[pltpu.VMEM((2, rows, half), BF)],
        out_pins=(0, 1, 2, 3),
        vmem=24,
        flops=2 * rows * width * width,
        name="project_and_norm",
    )


def hidden_blocks(width, wide, chunks, weight_rows):
    def pick(k):
        def at(i, f):
            block = 2 * (chunks * i + k) + f[1]
            return (block, 0) if weight_rows else (0, block)
        return at

    return [pl.BlockSpec((wide, width) if weight_rows else (width, wide), pick(k)) for k in range(chunks)]


def ahead_grads(flags, mlp_grad, down_weight, name):
    rows, width = mlp_grad.shape
    ff = down_weight.shape[0]
    wide, chunks = 2 * LANES, 2

    def body(flag_ref, mg_ref, *refs):
        out_ref = refs[-1]
        for k in range(chunks):
            out_ref[:, k * wide : (k + 1) * wide] = dot_lanes(mg_ref[...], refs[k][...])

    return kernel_call(
        body,
        flags,
        [mlp_grad] + [down_weight] * chunks,
        [shape_of((rows, ff // 2), F32)],
        specs=[None] + hidden_blocks(width, wide, chunks, True),
        out_specs=[pl.BlockSpec((rows, chunks * wide), lambda i, f: (0, i))],
        out_pins=(0,),
        grid=(ff // (2 * wide * chunks),),
        flops=rows * width * ff,
        name=name,
    )[0]


def hidden_grads(flags, hidden, ahead, up_weight, up_bias, lay, out_dtype, name):
    rows, width = hidden.shape
    ff = up_weight.shape[1]
    wide, chunks = 2 * LANES, 2
    steps = ff // (2 * wide * chunks)
    quarter = ff // 4

    def body(flag_ref, hid_ref, ahead_ref, *refs):
        weights, outs = refs[: 2 * chunks], refs[2 * chunks :]
        mine_ref, send_ref, bm_ref, bt_ref, hg_ref, hacc = outs
        step = pl.program_id(0)
        first = flag_ref[2] == 0
        back = 0.0
        for k in range(chunks):
            up_ref, ub_ref = weights[k], weights[chunks + k]
            pre = dot(hid_ref[...], up_ref[...]) + ub_ref[...]
            tanh = jnp.tanh(GELU_C * (pre + GELU_K * pre * pre * pre))
            act = (0.5 * pre * (1.0 + tanh)).astype(BF)
            slope = 0.5 * (1.0 + tanh) + 0.5 * pre * (1.0 - tanh * tanh) * GELU_C * (1.0 + 3.0 * GELU_K * pre * pre)
            pre_low = (ahead_ref[:, k * wide : (k + 1) * wide] * slope).astype(BF)
            back = back + dot_lanes(pre_low, up_ref[...])
            sums = jnp.sum(pre_low.astype(F32), axis=0, keepdims=True)
            lanes = slice(k * LANES, (k + 1) * LANES)
            for at, value in ((0, act), (1, pre_low)):
                mine_ref[at, :, lanes] = jnp.where(first, value[:, :LANES], value[:, LANES:])
                send_ref[at, :, lanes] = jnp.where(first, value[:, LANES:], value[:, :LANES])
            bm_ref[:, lanes] = jnp.broadcast_to(jnp.where(first, sums[:, :LANES], sums[:, LANES:]), (8, LANES))
            bt_ref[:, lanes] = jnp.broadcast_to(jnp.where(first, sums[:, LANES:], sums[:, :LANES]), (8, LANES))

        @pl.when(step == 0)
        def _():
            hacc[...] = back

        @pl.when(step > 0)
        def _():
            hacc[...] += back

        @pl.when(step == steps - 1)
        def _():
            hg_ref[...] = hacc[...].astype(hg_ref.dtype)

    chunk = pl.BlockSpec((2, rows, chunks * LANES), lambda i, f: (0, 0, i))
    bchunk = pl.BlockSpec((8, chunks * LANES), lambda i, f: (0, i))
    return kernel_call(
        body,
        flags,
        [hidden, ahead] + [up_weight] * chunks + [up_bias] * chunks,
        [shape_of((2, rows, quarter), BF)] * 2 + [shape_of((8, quarter), F32)] * 2 + [shape_of((rows, width), out_dtype)],
        specs=[None, pl.BlockSpec((rows, chunks * wide), lambda i, f: (0, i))]
        + hidden_blocks(width, wide, chunks, False)
        + hidden_blocks(1, wide, chunks, False),
        out_specs=[chunk, chunk, bchunk, bchunk, None],
        grid=(steps,),
        scratch=[pltpu.VMEM((rows, width), F32)],
        pins=(1,),
        flops=2 * rows * width * ff,
        name=name,
    )


def forward_rows(flags, mine, send, mine2, send2, down_weight):
    _, rows, quarter = mine.shape
    ff, width = down_weight.shape
    wide, chunks = 2 * LANES, 2
    steps = ff // (2 * wide * chunks)

    def body(flag_ref, m_ref, s_ref, m2_ref, s2_ref, *refs):
        own_ref, oth_ref, acc_ref = refs[chunks:]
        first = flag_ref[2] == 0
        step = pl.program_id(0)
        for at, (a_ref, b_ref) in enumerate(((m_ref, s_ref), (m2_ref, s2_ref))):
            total = 0.0
            for k in range(chunks):
                lanes = slice(k * LANES, (k + 1) * LANES)
                a, b = a_ref[:, lanes], b_ref[:, lanes]
                act = jnp.concatenate([jnp.where(first, a, b), jnp.where(first, b, a)], axis=1)
                total = total + dot(act, refs[k][...])

            @pl.when(step == 0)
            def _(total=total, at=at):
                acc_ref[at] = total

            @pl.when(step > 0)
            def _(total=total, at=at):
                acc_ref[at] += total

        @pl.when(step == steps - 1)
        def _():
            own_ref[...] = acc_ref[0]
            oth_ref[...] = acc_ref[1].astype(BF)

    chunk = pl.BlockSpec((None, rows, chunks * LANES), lambda i, f: (0, 0, i))
    return kernel_call(
        body,
        flags,
        [mine, send, mine2, send2] + [down_weight] * chunks,
        [shape_of((rows, width), F32), shape_of((rows, width), BF)],
        specs=[chunk] * 4 + hidden_blocks(width, wide, chunks, True),
        scratch=[pltpu.VMEM((2, rows, width), F32)],
        out_pins=(0,),
        grid=(steps,),
        flops=2 * rows * width * ff,
        name="forward_rows",
    )


def scale_cotangent(flags, cotangent, gates):
    rows, width = cotangent.shape

    def body(flag_ref, dy_ref, g_ref, out_ref, sums_ref):
        low = (per_frame((rows, width), g_ref[0:1], g_ref[1:2]) * dy_ref[...].astype(F32)).astype(BF)
        out_ref[...] = low
        sums_ref[...] = jnp.broadcast_to(jnp.sum(low.astype(F32), axis=0, keepdims=True), sums_ref.shape)

    return kernel_call(
        body,
        flags,
        [cotangent, gates],
        [shape_of((rows, width), BF), shape_of((8, width), F32)],
        pins=(0,),
        flops=rows * width,
        name="scale_cotangent",
    )


def layer_output(flags, mlp_own, mlp_recv, bias, resid, cotangent, gates):
    rows, width = resid.shape

    def body(flag_ref, a_ref, b_ref, bias_ref, r_ref, dy_ref, g_ref, out_ref, sums_ref):
        mlp = a_ref[...] + b_ref[...].astype(F32) + bias_ref[...]
        out_ref[...] = (r_ref[...] + per_frame((rows, width), g_ref[0:1], g_ref[1:2]) * mlp).astype(BF)
        sums_ref[0:1], sums_ref[1:2] = frame_sums(dy_ref[...].astype(F32) * mlp)
        sums_ref[2:8] = jnp.zeros((6, width), F32)

    return kernel_call(
        body,
        flags,
        [mlp_own, mlp_recv, bias, resid, cotangent, gates],
        [shape_of((rows, width), BF), shape_of((8, width), F32)],
        pins=(0, 3, 4),
        flops=rows * width * 4,
        name="layer_output",
    )


def pack_rows(flags, n_blk, mid, gate2, silu, down_b, up_sums, sum_long, sum_short, bias_long, bias_short):
    width = mid.shape[1]
    cols = bias_long.shape[1]

    def body(flag_ref, mid_ref, g_ref, s_ref, d_ref, m1, m2, t1, t2, sl, ss, bl, bs, out_ref):
        bias = bl[0:1] + bs[0:1]
        bias = jnp.concatenate([bias, jnp.zeros((1, 2 * width - cols), F32)], axis=1)
        rows = jnp.concatenate(
            [mid_ref[0:6], g_ref[0:2], s_ref[...].astype(F32), d_ref[0:1], mid_ref[6:7], m1[0:1] + m2[0:1], t1[0:1] + t2[0:1],
             sl[0:4], ss[0:4], bias[:, :width], bias[:, width:]],
            axis=0,
        ).astype(BF)
        for k in range(n_blk):
            out_ref[k] = rows

    return kernel_call(
        body,
        flags,
        [mid, gate2, silu, down_b, *up_sums, sum_long, sum_short, bias_long, bias_short],
        [shape_of((n_blk, PACK, width), BF)],
        flops=width * PACK,
        name="pack_rows",
    )[0]


def branch_back(flags, hid_own, hid_recv, cotangent, normed, inv_std, branch, mods, weight, lay):
    rows, width = normed.shape
    half = lay.heads * DH

    def body(flag_ref, a_ref, b_ref, dy_ref, n_ref, inv_ref, br_ref, mod_ref, w_ref, rg_ref, bg_ref, keep_ref, send_ref, sums_ref):
        side = flag_ref[1]
        hid = a_ref[...] + b_ref[...].astype(F32)
        norm = n_ref[...]
        scale = per_frame(hid.shape, mod_ref[4:5], mod_ref[5:6])
        resid = dy_ref[...].astype(F32) + norm_back(hid * (1.0 + scale), norm, inv_ref[:, 0:1])
        rg_ref[...] = resid
        gate = per_frame(hid.shape, mod_ref[0:1], mod_ref[1:2])
        low = (gate * resid).astype(BF)
        bg_ref[...] = low
        for out_ref, which in ((keep_ref, side), (send_ref, 1 - side)):
            grad = dot_lanes(low, w_ref[pl.ds(pl.multiple_of(which * half, half), half), :])
            for pair in range(lay.heads // 2):
                one, two = split_pair(grad[:, pair * LANES : (pair + 1) * LANES], lay.top)
                out_ref[2 * pair] = one.astype(BF)
                out_ref[2 * pair + 1] = two.astype(BF)
        sums_ref[0:1], sums_ref[1:2] = frame_sums(resid * br_ref[...])
        sums_ref[2:3], sums_ref[3:4] = frame_sums(hid)
        sums_ref[4:5], sums_ref[5:6] = frame_sums(hid * norm)
        sums_ref[6:7] = jnp.sum(low.astype(F32), axis=0, keepdims=True)
        sums_ref[7:8] = jnp.zeros((1, width), F32)

    packed = shape_of((lay.heads, lay.top, LANES), BF)
    return kernel_call(
        body,
        flags,
        [hid_own, hid_recv, cotangent, normed, inv_std, branch, mods, weight],
        [shape_of((rows, width), F32), shape_of((rows, width), BF), packed, packed, shape_of((8, width), F32)],
        pins=(0, 2, 3, 4, 5, 6),
        out_pins=(0,),
        vmem=24,
        flops=2 * rows * width * width,
        name="branch_back",
    )


def qkv_back(flags, grads, tok_own, tok_oth, weight, lay, is_long):
    rows, width = tok_own.shape
    cols = lay.heads * DH
    half = cols // 2

    def body(flag_ref, g_ref, own_ref, oth_ref, w_ref, hid_ref, low_ref, gm_ref, gt_ref, bias_ref, sums_ref, q_ref, acc_ref):
        step = pl.program_id(0)
        core = flag_ref[2]

        @pl.when(step == 0)
        def _():
            for pair in range(lay.heads // 2):
                one, two = g_ref[2 * pair, :rows, :].astype(F32), g_ref[2 * pair + 1, :rows, :].astype(F32)
                low = lane_low(one.shape)
                lanes = slice(pair * LANES, (pair + 1) * LANES)
                q_ref[0, :, lanes] = jnp.where(low, one, swap_halves(two)).astype(BF)
                q_ref[1, :, lanes] = jnp.where(low, swap_halves(one), two).astype(BF)
                one, two = g_ref[2 * pair, lay.vrow :, :].astype(F32), g_ref[2 * pair + 1, lay.vrow :, :].astype(F32)
                q_ref[2, :, lanes] = join_pair(one, two, rows).astype(BF)

        value = q_ref[step]
        part = dot_lanes(value, w_ref[...])

        @pl.when(step == 0)
        def _():
            acc_ref[...] = part

        @pl.when(step > 0)
        def _():
            acc_ref[...] += part

        first = core == 0
        gm_ref[...] = jnp.where(first, value[:, :half], value[:, half:])
        gt_ref[...] = jnp.where(first, value[:, half:], value[:, :half])
        bias_ref[...] = jnp.broadcast_to(jnp.sum(value.astype(F32), axis=0, keepdims=True), bias_ref.shape)

        @pl.when(step == 2)
        def _():
            hid = acc_ref[...]
            hid_ref[...] = hid
            low_ref[...] = hid.astype(BF)
            mine = (flag_ref[0] == 1) if is_long else (flag_ref[0] == 0)
            normed, _ = norm_rows(jnp.where(mine, own_ref[...].astype(F32), oth_ref[...].astype(F32)))
            sums_ref[0:1], sums_ref[1:2] = frame_sums(hid)
            sums_ref[2:3], sums_ref[3:4] = frame_sums(hid * normed)
            sums_ref[4:8] = jnp.zeros((4, width), F32)

    return kernel_call(
        body,
        flags,
        [grads, tok_own, tok_oth, weight],
        [
            shape_of((rows, width), F32),
            shape_of((rows, width), BF),
            shape_of((rows, 3 * half), BF),
            shape_of((rows, 3 * half), BF),
            shape_of((8, 3 * cols), F32),
            shape_of((8, width), F32),
        ],
        specs=[None, None, None, pl.BlockSpec((width, cols), lambda j, f: (0, 2 * j + f[1]))],
        out_specs=[
            None, None,
            pl.BlockSpec((rows, half), lambda j, f: (0, j)),
            pl.BlockSpec((rows, half), lambda j, f: (0, j)),
            pl.BlockSpec((8, cols), lambda j, f: (0, j)),
            None,
        ],
        pins=(1, 2),
        out_pins=(0,),
        grid=(3,),
        scratch=[pltpu.VMEM((3, rows, cols), BF), pltpu.VMEM((rows, width), F32)],
        flops=6 * rows * width * cols,
        name="qkv_back_long" if is_long else "qkv_back_short",
    )


def token_back(flags, hid_long, hid_short, recv, tokens, resid_grad, mods, lay):
    rows, width = tokens.shape

    def body(flag_ref, l_ref, s_ref, r_ref, tok_ref, rg_ref, mod_ref, out_ref):
        hid = jnp.where(flag_ref[0] == 1, l_ref[...], s_ref[...]) + r_ref[...].astype(F32)
        normed, inv_std = norm_rows(tok_ref[...].astype(F32))
        scale = per_frame(hid.shape, mod_ref[0:1, width : 2 * width], mod_ref[1:2, width : 2 * width])
        out_ref[...] = rg_ref[...] + norm_back(hid * (1.0 + scale), normed, inv_std)

    return kernel_call(
        body,
        flags,
        [hid_long, hid_short, recv, tokens, resid_grad, mods],
        [shape_of((rows, width), F32)],
        pins=(0, 1, 3, 4, 5),
        flops=rows * width * 20,
        name="token_back",
    )[0]


def group_spec(pair, rows, wide, moves):
    index = pair[1]
    if index is None:
        return pl.BlockSpec((rows, wide), lambda i, f: (0, i if moves else 0))
    return pl.BlockSpec((None, rows, wide), lambda i, f: (index, 0, i if moves else 0))


def width_of(jobs):
    return sum(rights[0][0].shape[-1] for _, rights in jobs)


def split_weight_grads(flags, jobs, n_blk, cuts, head_rows, name):
    count = len(jobs[0][0])
    rows, depth = jobs[0][0][0][0].shape[-2:]
    pieces = [(job, *cut) for job, many in enumerate(cuts) for cut in many]
    tall = depth // n_blk
    wide = max(tall, LANES)
    per = wide // tall
    operands = [pair for lefts, rights in jobs for pair in [*lefts, *rights]]
    extra = 0
    if head_rows:
        head = head_rows[0].shape[1] // n_blk
        turns = head_rows[0].shape[2] // cuts[0][-1][1]
        extra = head * turns

    def body(flag_ref, *refs):
        outs = refs[len(operands) + len(head_rows) :]
        step = pl.program_id(0)
        results = []
        for job in range(len(jobs)):
            mine = refs[2 * count * job : 2 * count * (job + 1)]
            acc = dot_rows(mine[0][...], mine[count][...])
            for k in range(1, count):
                acc += dot_rows(mine[k][...], mine[count + k][...])
            results.append(acc.astype(BF))
        for member in range(per):
            place = relative_place(step * per + member, flag_ref[4], n_blk)
            if head_rows:
                part_ref, got_ref = refs[len(operands) : len(operands) + 2]
                at = pl.ds(pl.multiple_of((step * per + member) * head, head), head)
                both = (part_ref[flag_ref[2], at].astype(F32) + got_ref[at].astype(F32)).astype(BF)
            for out, (job, start, cols, order) in enumerate(pieces):
                sent, at = half_place(place, order)
                values = [results[job][member * tall : (member + 1) * tall, start : start + cols]]
                if head_rows and out == len(pieces) - 1:
                    values += [both[:, turn * cols : (turn + 1) * cols] for turn in range(turns)]

                def store(out_ref, values=values, at=at):
                    row = 0
                    for value in values:
                        out_ref[at, row : row + value.shape[0]] = value
                        row += value.shape[0]

                pl.when(sent == 1)(functools.partial(store, outs[2 * out]))
                pl.when(sent == 0)(functools.partial(store, outs[2 * out + 1]))

    specs = []
    for lefts, rights in jobs:
        specs += [group_spec(pair, rows, wide, True) for pair in lefts]
        specs += [group_spec(pair, rows, pair[0].shape[-1], False) for pair in rights]
    outs = []
    for out, (job, start, cols, order) in enumerate(pieces):
        outs += [shape_of((n_blk // 2, tall + (extra if out == len(pieces) - 1 else 0), cols), BF)] * 2
    return kernel_call(
        body,
        flags,
        [array for array, _ in operands] + list(head_rows),
        outs,
        specs=specs + [None] * len(head_rows),
        grid=(depth // wide,),
        vmem=24,
        pins=tuple(range(len(operands))) if head_rows else (),
        flops=2 * count * rows * depth * width_of(jobs),
        name=name,
    )


def head_weight_grads(flags, longs, shorts, grad_own, grad_oth, lay):
    rows, width = grad_own.shape
    pairs = lay.heads // 2

    def body(flag_ref, l_ref, s_ref, go_ref, gt_ref, out_ref):
        own_long = flag_ref[0] == 1
        grads = jnp.where(own_long, go_ref[...], gt_ref[...]), jnp.where(own_long, gt_ref[...], go_ref[...])
        for pair in range(pairs):
            acc = 0.0
            for ref, grad in zip((l_ref, s_ref), grads):
                left = join_pair(ref[2 * pair].astype(F32), ref[2 * pair + 1].astype(F32), rows).astype(BF)
                acc = acc + dot_rows(left, grad)
            out_ref[pair * LANES : (pair + 1) * LANES, :] = acc.astype(BF)

    return kernel_call(
        body,
        flags,
        [longs, shorts, grad_own, grad_oth],
        [shape_of((lay.heads * DH, width), BF)],
        pins=(0, 1),
        flops=4 * rows * width * lay.heads * DH,
        name="head_weight_grads",
    )[0]


def relative_place(target, here, n_blk):
    relative = target ^ here
    return relative ^ ((relative >> 1) & (10 & (n_blk - 1)))


def half_place(place, order):
    at = 0
    for bit in order[1:]:
        at = 2 * at + ((place >> bit) & 1)
    return (place >> order[0]) & 1, at


def hop_of(bit):
    return (1 << bit) if bit == 0 or bit % 2 == 1 else (1 << bit) | (1 << (bit - 1))


class CubeSum:
    def __init__(self, send, keep, n_blk, order):
        self.n_blk, self.order, self.at = n_blk, order, 0
        self.bits = n_blk.bit_length() - 1
        self.send, self.keep, self.value, self.got = send, keep, None, None

    def move(self, *starts):
        hop = hop_of(self.order[self.at])
        send = after(self.send, *starts) if starts else self.send
        self.got = lax.ppermute(send, "blk", [(i, i ^ hop) for i in range(self.n_blk)])

    def add(self):
        self.at += 1
        half = self.keep.shape[0] // 2
        if self.at == self.bits:
            self.value = (self.keep.astype(F32) + self.got.astype(F32))[0]
        else:
            low = [(self.keep[k].astype(F32) + self.got[k].astype(F32)).astype(BF) for k in (slice(half), slice(half, None))]
            self.keep, self.send = low

    def finish(self):
        while self.at < self.bits:
            self.move()
            self.add()
        return self.value


def lay_out_rows(flags, gathered, split, ff, name):
    n_uly, rows, total = gathered.shape
    cols = (total - split) // 3

    def body(flag_ref, in_ref, up_ref, attn_ref):
        for u in range(n_uly):
            for i in range(split // LANES):
                at = (i * n_uly + u) * LANES
                up_ref[:, at : at + LANES] = in_ref[u, :, i * LANES : (i + 1) * LANES].astype(F32)
            for j in range(3):
                at = (j * n_uly + u) * cols
                attn_ref[:, at : at + cols] = in_ref[u, :, split + j * cols : split + (j + 1) * cols].astype(F32)

    return kernel_call(
        body,
        flags,
        [gathered],
        [shape_of((rows, ff), F32), shape_of((rows, 3 * n_uly * cols), F32)],
        flops=rows * total,
        name=name,
    )


def modulation_grads(flags, long_rows, gathered, row_out, name):
    total, width = gathered.shape
    quarter = total // 4

    def body(flag_ref, long_ref, g_ref, out_ref, sums_ref, part_ref):
        start = flag_ref[5]
        block = pl.multiple_of((start // LANES) * LANES, LANES)
        silu = g_ref[:, pl.ds(block, LANES)].astype(F32)
        parts = [silu[k * quarter : (k + 1) * quarter] for k in (1, 0, 3, 2)]
        mate = jnp.concatenate(parts, axis=0)
        own_long = long_ref[...] > 0.5

        def place_of(index):
            return index - PACK * ((index * 2731) >> 16)

        place = place_of(lax.broadcasted_iota(jnp.int32, (total, LANES), 0))

        def aligned(value, base):
            return jnp.where((place == base) | (place == base + 1), pltpu.roll(value, (base - 8) % total, 0), 0.0)

        def owner(base, is_long):
            return jnp.where(own_long == is_long, aligned(silu, base), aligned(mate, base))

        lefts = [
            owner(14, True) + owner(18, False),
            owner(16, True) + owner(20, False),
            aligned(silu, 0),
            aligned(silu, 2),
            aligned(silu, 4),
            aligned(silu, 6),
        ]
        for k, left in enumerate(lefts):
            part_ref[...] = dot_rows(left.astype(BF), g_ref[...])
            out_ref[:, k * width : (k + 1) * width] = part_ref[pl.ds(pl.multiple_of(start - block, row_out), row_out), :]
        row = lax.broadcasted_iota(jnp.int32, (32, quarter), 0)
        which = jnp.where(row == place_of(lax.broadcasted_iota(jnp.int32, (32, quarter), 1)), 1.0, 0.0).astype(BF)
        for u in range(4):
            sums_ref[u] = dot(which, g_ref[u * quarter : (u + 1) * quarter, :])

    return kernel_call(
        body,
        flags,
        [long_rows, gathered],
        [shape_of((row_out, 6 * width), F32), shape_of((4, 32, width), F32)],
        scratch=[pltpu.VMEM((LANES, width), F32)],
        vmem=max(16, 16 * total // 768),
        flops=total * width * LANES * 12,
        name=name,
    )


def after(value, *earlier):
    return lax.optimization_barrier((value,) + earlier)[0]


def rotary_static(frames):
    n_time, n_row = DH // 8, 3 * DH // 16
    cosine = np.zeros((frames * PATCH, LANES), np.float32)
    sine = np.zeros((frames * PATCH, LANES), np.float32)
    patch = np.arange(frames * PATCH) % PATCH
    for group, place in ((0, patch // GRID), (1, patch % GRID)):
        for j in range(n_row):
            freq = np.exp(np.float32(-math.log(10000.0)) * np.float32(j) / np.float32(n_row)).astype(np.float32)
            angle = (place.astype(np.float32) * freq).astype(np.float64)
            pair = n_time + group * n_row + j
            for head in (0, HALF):
                cosine[:, head + 2 * pair] = np.cos(angle)
                cosine[:, head + 2 * pair + 1] = np.cos(angle)
                sine[:, head + 2 * pair] = -np.sin(angle)
                sine[:, head + 2 * pair + 1] = np.sin(angle)
    return cosine, sine


def rotary_time(times):
    n_time = DH // 8
    lane = jnp.arange(LANES, dtype=jnp.int32)
    pair = (lane % HALF) // 2
    freq = jnp.exp(-math.log(10000.0) * pair.astype(F32) / float(n_time))
    angle = times.astype(F32)[:, None] * freq[None, :]
    live = (pair < n_time)[None, :]
    sign = jnp.where(lane % 2 == 0, -1.0, 1.0)[None, :]
    return jnp.where(live, jnp.cos(angle), 0.0), jnp.where(live, sign * jnp.sin(angle), 0.0)


class Layout:
    def __init__(self, rows, heads, parts):
        self.rows = rows
        self.heads = heads
        self.parts = parts
        self.top = round_up(-(-rows // 2), 16)
        self.vrow = round_up(rows, 16)


def on_device(
    tokens, cotangent, noise_embed, frame_clip, frame_index, mod_weight, mod_bias, attn_weight, attn_bias,
    proj_weight, proj_bias, up_weight, up_bias, down_weight, down_bias,
):
    n_uly = lax.axis_size("uly")
    n_blk = lax.axis_size("blk")
    blk = lax.axis_index("blk")
    uly = lax.axis_index("uly")
    rows, width = tokens.shape
    frames = noise_embed.shape[0]
    side, core = uly // 2, uly % 2
    heads = width // DH // 2
    parts = n_blk // heads
    lay = Layout(rows, heads, parts)
    dev = blk * n_uly + uly

    def swap_side(value):
        return lax.ppermute(value, "uly", [(i, i ^ 2) for i in range(n_uly)])

    def swap_core(value):
        return lax.ppermute(value, "uly", [(i, i ^ 1) for i in range(n_uly)])

    def spread(value):
        return lax.all_to_all(value, "blk", split_axis=0, concat_axis=0, tiled=True)

    long_first = frame_clip[::FB] == n_blk
    own_long_b = lax.dynamic_index_in_dim(long_first, blk, 0, False) == (side == 0)
    own_long = own_long_b.astype(jnp.int32)
    row_out = width // (n_blk * n_uly)
    flags = jnp.stack([own_long, side, core, blk // heads, blk, dev * row_out]).astype(jnp.int32)

    tok_oth = swap_side(tokens)
    silu = jax.nn.silu(noise_embed.astype(F32)).astype(BF)
    bias = mod_bias.astype(F32)
    first_mod = dot(silu, mod_weight[:, : 2 * width]) + bias[: 2 * width]
    first_mods = jnp.concatenate([first_mod, swap_side(first_mod)], axis=0)
    rest_mod = dot(after(silu, first_mod), mod_weight[:, 2 * width :]) + bias[2 * width :]

    block_time = frame_index.reshape(n_blk, FB)
    head_time, tail_time = block_time[:, : FB // 2], block_time[:, FB // 2 :]
    long_times = lax.dynamic_slice_in_dim(jnp.where(long_first[:, None], head_time, tail_time), core * frames, frames, 1)
    short_times = lax.dynamic_slice_in_dim(jnp.where(long_first[:, None], tail_time, head_time), core * frames, frames, 1)
    short_times = lax.dynamic_index_in_dim(short_times, blk, 0, False)
    time_cos, time_sin = rotary_time(jnp.concatenate([lax.dynamic_index_in_dim(long_times, blk, 0, False), short_times]))
    long_cos, long_sin = rotary_time(long_times.reshape(-1))
    short_cos, short_sin = time_cos[frames:, None], time_sin[frames:, None]
    long_cos, long_sin = long_cos[:, None], long_sin[:, None]
    tab_cos, tab_sin = (jnp.asarray(t) for t in rotary_static(frames))
    own_long_all = (long_first[None, :] == ((side ^ jnp.arange(2)) == 0)[:, None]).astype(F32)
    long_rows = jnp.broadcast_to(own_long_all[None, :, :, None, None], (2, 2, n_blk, PACK, LANES)).reshape(-1, LANES)
    first_mods, rest_mod, long_cos, long_sin, short_cos, short_sin, long_rows = lax.optimization_barrier(
        (first_mods, rest_mod, long_cos, long_sin, short_cos, short_sin, long_rows)
    )

    gate2 = rest_mod[:, 3 * width :]
    mid_mods = jnp.concatenate([rest_mod[:, :width], rest_mod[:, width : 2 * width], rest_mod[:, 2 * width : 3 * width]], axis=0)
    mid_mods = jnp.concatenate([mid_mods, jnp.zeros((2, width), F32)], axis=0)
    hidden1, qkv_long, qkv_short = tokens_to_qkv(
        flags, tokens, tok_oth, first_mods, attn_weight, attn_bias.astype(F32)[None], tab_cos, tab_sin, time_cos, time_sin, lay
    )
    sent = jnp.concatenate([qkv_long] * parts, axis=0) if parts > 1 else qkv_long
    long_own = spread(sent)
    short_oth = swap_core(qkv_short)
    out_short, ot_short, lse_short = attend(flags, qkv_short, short_oth, lay, False)
    mlp_grad, down_b = scale_cotangent(flags, after(cotangent, qkv_long), gate2)
    mlp_grad_oth = swap_side(mlp_grad)
    ahead_own = ahead_grads(flags, mlp_grad, down_weight, "ahead_own")
    long_own, out_short, mlp_grad, ahead_own = lax.optimization_barrier((long_own, out_short, mlp_grad, ahead_own))
    long_oth = swap_core(long_own)
    out_long_all, ot_long, lse_long = attend(flags, long_own, long_oth, lay, True)
    out_long_all, mlp_grad_oth = lax.optimization_barrier((out_long_all, mlp_grad_oth))

    def own_part(value):
        if parts == 1:
            return value
        return lax.dynamic_slice_in_dim(value, ((blk // 2) % parts) * heads, heads, 0)

    ahead_oth = ahead_grads(flags, mlp_grad_oth, down_weight, "ahead_other")
    out_long = own_part(spread(out_long_all))
    out_long, ahead_oth = lax.optimization_barrier((out_long, ahead_oth))
    out_recv = swap_side(jnp.where(own_long_b, out_short, out_long))
    branch, resid, normed2, inv2, hidden2 = project_and_norm(
        flags, out_long, out_short, out_recv, proj_weight, proj_bias.astype(F32)[None], tokens, mid_mods, lay
    )

    hidden2_oth = swap_side(hidden2)
    up_b = up_bias.astype(F32)[None]
    mine, send, bm, bt, hid_own = hidden_grads(flags, hidden2, ahead_own, up_weight, up_b, lay, F32, "hidden_own")
    hidden2_oth, hid_own = lax.optimization_barrier((hidden2_oth, hid_own))
    mine2, send2, bm2, bt2, hid_oth = hidden_grads(flags, hidden2_oth, ahead_oth, up_weight, up_b, lay, BF, "hidden_other")
    hid_recv = swap_side(hid_oth)

    got, got2 = swap_core(send), swap_core(send2)
    hid_c, hid_c2, mg_c, mg_c2 = (swap_core(v) for v in (hidden2, hidden2_oth, mlp_grad, mlp_grad_oth))
    plain = lambda *arrays: [(v, None) for v in arrays]
    blocks = [mine, mine2, got, got2]
    bits = list(range(n_blk.bit_length() - 1))
    orders = [bits, [1, 0] + bits[2:]]
    down_order, up_order = ([0, 2, 1], [1, 0, 2]) if len(bits) == 3 else (bits, bits)
    mlp_halves = split_weight_grads(
        flags,
        [
            ([(v, 0) for v in blocks], plain(mlp_grad, mlp_grad_oth, mg_c, mg_c2)),
            (plain(hidden2, hidden2_oth, hid_c, hid_c2), [(v, 1) for v in blocks]),
        ],
        n_blk, [[(0, width, down_order)], [(0, width, up_order)]], [], "mlp_grads",
    )
    hid_recv, *mlp_halves = lax.optimization_barrier((hid_recv, *mlp_halves))

    resid_grad, branch_grad, do_keep, do_send, mid_sums = branch_back(
        flags, hid_own, hid_recv, cotangent, normed2, inv2, branch, mid_mods, proj_weight, lay
    )
    mlp_sums = [CubeSum(*mlp_halves[:2], n_blk, down_order), CubeSum(*mlp_halves[2:], n_blk, up_order)]
    for part in mlp_sums:
        part.move()
    do_recv = swap_side(do_send)
    mlp_own, mlp_oth = forward_rows(flags, mine, send, mine2, after(send2, do_send), down_weight)
    do_recv, mlp_own, mlp_oth = lax.optimization_barrier((do_recv, mlp_own, mlp_oth))
    do_long = jnp.where(own_long_b, do_keep, do_recv)
    if parts > 1:
        hot = (jnp.arange(parts) == (blk // 2) % parts)[:, None, None, None]
        do_sent = jnp.where(hot, do_long[None], 0).reshape((n_blk,) + do_long.shape[1:])
    else:
        do_sent = do_long
    do_all = spread(do_sent)
    dq_s, mine_s, theirs_s = attend_back(
        flags, qkv_short, short_oth, [do_keep, do_recv], ot_short, lse_short, tab_cos, tab_sin, short_cos, short_sin, lay, False
    )
    branch_grad_oth = swap_side(after(branch_grad, do_recv))
    mlp_recv = swap_side(after(mlp_oth, branch_grad_oth))
    do_all, dq_s, mine_s, theirs_s, branch_grad_oth, mlp_sums[0].got, mlp_sums[1].got = lax.optimization_barrier(
        (do_all, dq_s, mine_s, theirs_s, branch_grad_oth, mlp_sums[0].got, mlp_sums[1].got)
    )
    for part in mlp_sums:
        part.add()
    do_all, mlp_sums[0].send, mlp_sums[1].send = lax.optimization_barrier((do_all, mlp_sums[0].send, mlp_sums[1].send))
    for part in mlp_sums:
        part.move()

    dq_l, mine_l, theirs_l = attend_back(
        flags, long_own, long_oth, [do_all], ot_long, lse_long, tab_cos, tab_sin, long_cos, long_sin, lay, True
    )
    theirs_l, mlp_sums[0].got, mlp_sums[1].got = lax.optimization_barrier(
        (swap_core(theirs_l), mlp_sums[0].got, mlp_sums[1].got)
    )
    grads_sent = finish_keys(flags, dq_l, mine_l, theirs_l, tab_cos, tab_sin, long_cos, long_sin, lay, True)
    grads_all = spread(grads_sent)
    if parts > 1:
        grads_long = jnp.sum(grads_all.astype(F32).reshape((parts, heads) + grads_all.shape[1:]), axis=0).astype(BF)
    else:
        grads_long = grads_all

    theirs_s = swap_core(theirs_s)
    branch_grad_oth, dq_s, theirs_s, mlp_sums[0].got, mlp_sums[1].got, _ = lax.optimization_barrier(
        (branch_grad_oth, dq_s, theirs_s, mlp_sums[0].got, mlp_sums[1].got, grads_sent)
    )
    for part in mlp_sums:
        part.add()
    grads_short = finish_keys(flags, dq_s, mine_s, theirs_s, tab_cos, tab_sin, short_cos, short_sin, lay, False)
    hidS, hidS_low, gmS, gtS, abS, sumS = qkv_back(flags, grads_short, tokens, tok_oth, attn_weight, lay, False)
    output, gate2_sums = layer_output(flags, mlp_own, after(mlp_recv, grads_sent), down_bias.astype(F32)[None], resid, cotangent, gate2)
    proj_part = head_weight_grads(flags, out_long, out_short, branch_grad, branch_grad_oth, lay).reshape(2, -1, width)
    proj_got = swap_core(jnp.where(core == 0, proj_part[1], proj_part[0]))
    h1_core = swap_core(hidden1)
    gtS_got = swap_core(gtS)
    grads_long, hidS_low, gate2_sums, mlp_sums[0].send, mlp_sums[1].send = lax.optimization_barrier(
        (grads_long, hidS_low, gate2_sums, mlp_sums[0].send, mlp_sums[1].send)
    )
    for part in mlp_sums:
        part.move()

    hidL, hidL_low, gmL, gtL, abL, sumL = qkv_back(flags, grads_long, tokens, tok_oth, attn_weight, lay, True)
    gtL_got = swap_core(gtL)
    hid1_recv = swap_side(jnp.where(own_long_b, hidS_low, hidL_low))
    pack = pack_rows(flags, n_blk, mid_sums, gate2_sums, silu, down_b, (bm, bm2, bt, bt2), sumL, sumS, abL, abS)
    many = spread(pack)
    quarter = 3 * width // n_uly
    split = 2 * quarter // 3
    halves = split_weight_grads(
        flags,
        [([(hidden1, 0), (hidden1, 1), (h1_core, 0), (h1_core, 1)], plain(gmL, gmS, after(gtL_got, pack), gtS_got))],
        n_blk, [[(0, split, orders[0]), (split, quarter - split, orders[1])]], [proj_part, proj_got], "attn_grads",
    )
    hid1_recv, mlp_sums[0].got, mlp_sums[1].got, *halves = lax.optimization_barrier(
        (hid1_recv, mlp_sums[0].got, mlp_sums[1].got, *halves)
    )
    attn_sums = [CubeSum(*halves[2 * k : 2 * k + 2], n_blk, order) for k, order in enumerate(orders)]
    for part in attn_sums:
        part.move()
    token_grad = token_back(flags, hidL, hidS, hid1_recv, tokens, resid_grad, first_mod, lay)
    many, token_grad, *gots = lax.optimization_barrier((many, token_grad, *[part.got for part in attn_sums]))
    both = swap_side(many)
    for part, got in zip(attn_sums, gots):
        part.got = got
        part.add()
        part.move()
    for part in mlp_sums:
        part.add()
    down_mine, up_mine = mlp_sums[0].finish(), mlp_sums[1].finish().astype(BF)
    both, down_mine, up_mine, *gots = lax.optimization_barrier((both, down_mine, up_mine, *[part.got for part in attn_sums]))
    for part, got in zip(attn_sums, gots):
        part.got = got
        part.add()
        part.move()
    both = jnp.stack([many, both])
    packs = jnp.stack([both, swap_core(both)]).reshape(-1, width)
    g_mod_weight, sums = modulation_grads(flags, long_rows, packs, row_out, "modulation_grads")
    if len(bits) == 3:
        sums, *gots = lax.optimization_barrier((sums, *[part.got for part in attn_sums]))
        for part, got in zip(attn_sums, gots):
            part.got = got
    for part in attn_sums:
        part.add()
    attn_mine = [part.finish() for part in attn_sums]
    attn_rows = width // n_blk
    head = proj_part.shape[1] // n_blk
    proj_mine = jnp.concatenate(
        [attn_mine[1][attn_rows + k * head : attn_rows + (k + 1) * head] for k in range(width // (quarter - split))], axis=1
    )
    attn_mine = [part[:attn_rows].astype(BF) for part in attn_mine]

    quarters = jnp.concatenate([up_mine] + attn_mine, axis=1)
    quarters = lax.all_to_all(quarters.reshape(n_uly, row_out, -1), "uly", 0, 0, tiled=True)
    ff = up_weight.shape[1]

    g = ff // (n_blk * n_uly)

    def down_home(index):
        b, u = divmod(index, n_uly)
        start = ((b * g // LANES) * n_uly + u) * LANES + (b * g) % LANES
        return start // g

    down_map = [(i, down_home(i)) for i in range(n_blk * n_uly)]
    g_down_weight = down_mine.astype(F32)
    if any(a != b for a, b in down_map):
        g_down_weight = lax.ppermute(g_down_weight, ("blk", "uly"), down_map)
    proj_map = [(b * n_uly + u, u * n_blk + b) for b in range(n_blk) for u in range(n_uly)]
    g_proj_weight = lax.ppermute(proj_mine.astype(F32), ("blk", "uly"), proj_map)


    def cut(vector, size):
        return lax.dynamic_slice_in_dim(vector, dev * size, size, 0)

    total_dev = n_blk * n_uly
    whole_sum = jnp.sum(sums, axis=0)
    mod_line = jnp.concatenate([whole_sum[14:16] + whole_sum[18:20], whole_sum[16:18] + whole_sum[20:22], whole_sum[0:8]], axis=0)
    g_mod_bias = cut(mod_line.reshape(6, 2, width).sum(axis=1).reshape(-1), 6 * width // total_dev)
    g_down_bias = cut(whole_sum[10], width // total_dev)
    g_proj_bias = cut(whole_sum[11], width // total_dev)
    first = dev * g
    steps = (first // LANES) % n_uly ^ uly
    core_step, side_step = steps % 2, steps // 2
    up_mine_sum = sums[2 * core_step + side_step, 12] + sums[2 * (1 - core_step) + side_step, 13]
    g_up_bias = lax.dynamic_slice_in_dim(up_mine_sum, first // (LANES * n_uly) * LANES + first % LANES, g, 0)
    by_step = (sums[0:2, 22:24] + sums[2:4, 22:24]).reshape(2, 2 * width)[:, : 3 * width // 2]
    by_side = jnp.where(side == 0, by_step, by_step[::-1])
    g_attn_bias = cut(jnp.swapaxes(by_side.reshape(2, 3, width // 2), 0, 1).reshape(-1), 3 * width // total_dev)
    quarters, g_mod_bias, g_down_bias, g_proj_bias, g_up_bias, g_attn_bias, g_down_weight = lax.optimization_barrier(
        (quarters, g_mod_bias, g_down_bias, g_proj_bias, g_up_bias, g_attn_bias, g_down_weight)
    )
    g_up_weight, g_attn_weight = lay_out_rows(flags, quarters, ff // n_uly, ff, "lay_out_rows")
    return (
        output, token_grad, g_mod_weight, g_mod_bias, g_attn_weight, g_attn_bias,
        g_proj_weight, g_proj_bias, g_up_weight, g_up_bias, g_down_weight, g_down_bias,
    )


def solution(mesh):
    row = P(("blk", "uly"), None)
    flat = P(("blk", "uly"))
    in_specs = (row, row, row) + (P(),) * 12
    out_specs = (row, row, row, flat, row, flat, row, flat, row, flat, row, flat)
    return jax.shard_map(on_device, mesh=mesh, in_specs=in_specs, out_specs=out_specs, check_vma=False)
```

```python
import functools
import math

import jax
import jax.numpy as jnp
import numpy as np
from jax import lax
from jax.experimental import pallas as pl
from jax.experimental.pallas import tpu as pltpu
from jax.sharding import PartitionSpec as P

DH = 64
GRID = 10
FB = 8
PATCH = 100
HALF = 64
LANES = 128

GELU_C = 0.7978845608028654
GELU_K = 0.044715
NEG_BIG = -1e30
MIB = 1 << 20
UNROLL = 2
PACK = 24

BF = jnp.bfloat16
F32 = jnp.float32


def round_up(value, step):
    return -(-value // step) * step


def lane_low(shape):
    return lax.broadcasted_iota(jnp.int32, shape, len(shape) - 1) < HALF


def first_frame(shape):
    return lax.broadcasted_iota(jnp.int32, shape, 0) < PATCH


def swap_halves(value):
    return pltpu.roll(value, HALF, 1)


def swap_pairs(value):
    even = lax.broadcasted_iota(jnp.int32, value.shape, 1) % 2 == 0
    return jnp.where(even, pltpu.roll(value, LANES - 1, 1), pltpu.roll(value, 1, 1))


def per_frame(shape, first, second):
    return jnp.where(first_frame(shape), jnp.broadcast_to(first, shape), jnp.broadcast_to(second, shape))


def frame_sums(value):
    head = first_frame(value.shape)
    one = jnp.sum(jnp.where(head, value, 0.0), axis=0, keepdims=True)
    two = jnp.sum(jnp.where(head, 0.0, value), axis=0, keepdims=True)
    return one, two


def norm_rows(values):
    center = values - jnp.mean(values, axis=-1, keepdims=True)
    inv_std = lax.rsqrt(jnp.mean(center * center, axis=-1, keepdims=True) + 1e-06)
    return center * inv_std, inv_std


def norm_back(grad, normed, inv_std):
    return inv_std * (
        grad
        - jnp.mean(grad, axis=-1, keepdims=True)
        - normed * jnp.mean(grad * normed, axis=-1, keepdims=True)
    )


def dot(left, right):
    return jnp.dot(left, right, preferred_element_type=F32)


def dot_lanes(left, right):
    return lax.dot_general(left, right, (((1,), (1,)), ((), ())), preferred_element_type=F32)


def dot_rows(left, right):
    return lax.dot_general(left, right, (((0,), (0,)), ((), ())), preferred_element_type=F32)


def split_pair(value, rows_top):
    rows = value.shape[0]
    top = value[:rows_top]
    bottom = jnp.concatenate(
        [value[rows_top:], jnp.zeros((2 * rows_top - rows, LANES), value.dtype)], axis=0
    )
    low = lane_low(top.shape)
    return jnp.where(low, top, swap_halves(bottom)), jnp.where(low, swap_halves(top), bottom)


def join_pair(one, two, rows):
    rows_top = one.shape[0]
    low = lane_low(one.shape)
    top = jnp.where(low, one, swap_halves(two))
    bottom = jnp.where(low, swap_halves(one), two)
    return jnp.concatenate([top, bottom[: rows - rows_top]], axis=0)


def smem():
    return pl.BlockSpec(memory_space=pltpu.SMEM)


def whole(shape):
    return pl.BlockSpec(shape, lambda *_: (0,) * len(shape))


def kernel_call(body, flags, args, outs, *, specs=None, out_specs=None, grid=(1,), scratch=(), vmem=16, pins=(), out_pins=(), aliases=None, flops, name):
    specs = specs or [None] * len(args)
    out_specs = out_specs or [None] * len(outs)
    return pl.pallas_call(
        body,
        grid_spec=pltpu.PrefetchScalarGridSpec(
            num_scalar_prefetch=1,
            grid=grid,
            in_specs=[spec or whole(a.shape) for spec, a in zip(specs, args)],
            out_specs=[spec or whole(o.shape) for spec, o in zip(out_specs, outs)],
            scratch_shapes=list(scratch),
        ),
        out_shape=[pltpu.HBM(o.shape, o.dtype) if k in out_pins else o for k, o in enumerate(outs)],
        input_output_aliases=aliases or {},
        compiler_params=pltpu.CompilerParams(vmem_limit_bytes=vmem * MIB),
        cost_estimate=pl.CostEstimate(flops=flops // 4096, bytes_accessed=4096, transcendentals=0),
        name=name,
    )(flags, *[pltpu.with_memory_space_constraint(a, pltpu.HBM) if a.size >= MIB or k in pins else a for k, a in enumerate(args)])


def shape_of(dims, dtype):
    return jax.ShapeDtypeStruct(dims, dtype)


def tokens_to_qkv(flags, tok_own, tok_oth, mods, weight, bias, tab_cos, tab_sin, time_cos, time_sin, lay):
    rows, width = tok_own.shape
    cols = lay.heads * DH

    def body(flag_ref, own_ref, oth_ref, mod_ref, w_ref, b_ref, tc_ref, ts_ref, qc_ref, qs_ref, hid_ref, long_ref, short_ref, both_ref):
        step = pl.program_id(0)
        own_long = flag_ref[0]

        @pl.when(step == 0)
        def _():
            hidden = []
            for src, base in ((own_ref, 0), (oth_ref, 2)):
                normed, _ = norm_rows(src[...].astype(F32))
                shift = per_frame(normed.shape, mod_ref[base : base + 1, :width], mod_ref[base + 1 : base + 2, :width])
                scale = per_frame(
                    normed.shape, mod_ref[base : base + 1, width : 2 * width], mod_ref[base + 1 : base + 2, width : 2 * width]
                )
                hidden.append(normed * (1.0 + scale) + shift)
            swapped = own_long == 0
            first = jnp.where(swapped, hidden[1], hidden[0])
            second = jnp.where(swapped, hidden[0], hidden[1])
            hid_ref[0] = first.astype(BF)
            hid_ref[1] = second.astype(BF)
            both_ref[...] = jnp.concatenate([first, second], axis=0).astype(BF)

        result = dot(both_ref[...], w_ref[...]) + b_ref[...]
        for slot, out_ref in ((0, long_ref), (1, short_ref)):
            acc = result[slot * rows : (slot + 1) * rows]

            def rotated(pair):
                value = acc[:, pair * LANES : (pair + 1) * LANES]
                cosine = tc_ref[...] + per_frame(value.shape, qc_ref[2 * slot : 2 * slot + 1], qc_ref[2 * slot + 1 : 2 * slot + 2])
                sine = ts_ref[...] + per_frame(value.shape, qs_ref[2 * slot : 2 * slot + 1], qs_ref[2 * slot + 1 : 2 * slot + 2])
                return value * cosine + swap_pairs(value) * sine

            @pl.when(step == 0)
            def _():
                for pair in range(cols // LANES):
                    turned = rotated(pair)
                    out_ref[2 * pair, :rows, :HALF] = turned[:, :HALF].astype(BF)
                    out_ref[2 * pair + 1, :rows, :HALF] = swap_halves(turned)[:, :HALF].astype(BF)

            @pl.when(step == 1)
            def _():
                for pair in range(cols // LANES):
                    turned = rotated(pair)
                    out_ref[2 * pair, :rows, HALF:] = swap_halves(turned)[:, HALF:].astype(BF)
                    out_ref[2 * pair + 1, :rows, HALF:] = turned[:, HALF:].astype(BF)

            @pl.when(step == 2)
            def _():
                for pair in range(cols // LANES):
                    one, two = split_pair(acc[:, pair * LANES : (pair + 1) * LANES], lay.top)
                    out_ref[2 * pair, lay.vrow :, :] = one.astype(BF)
                    out_ref[2 * pair + 1, lay.vrow :, :] = two.astype(BF)

    packed = (lay.heads, lay.vrow + lay.top, LANES)
    return kernel_call(
        body,
        flags,
        [tok_own, tok_oth, mods, weight, bias, tab_cos, tab_sin, time_cos, time_sin],
        [shape_of((2, rows, width), BF), shape_of(packed, BF), shape_of(packed, BF)],
        specs=[
            None, None, None,
            pl.BlockSpec((width, cols), lambda j, f: (0, 2 * j + f[1])),
            pl.BlockSpec((1, cols), lambda j, f: (0, 2 * j + f[1])),
            None, None, None, None,
        ],
        scratch=[pltpu.VMEM((2 * rows, width), BF)],
        out_pins=(0,),
        grid=(3,),
        flops=12 * rows * width * cols,
        name="tokens_to_qkv",
    )


def unpack_values(ref, at, lay):
    part = ref[at, lay.vrow :, :].astype(F32)
    return jnp.concatenate([part, swap_halves(part)[: lay.rows - lay.top]], axis=0)


def hundreds(value):
    return (value * 1311) >> 17


def diag_mask(keys, queries, core):
    key = hundreds(lax.broadcasted_iota(jnp.int32, (keys, 1), 0)) ^ (2 * core)
    query = hundreds(lax.broadcasted_iota(jnp.int32, (1, queries), 1))
    query = ((query & 2) << 1) + (query & 1) + 2 * core
    return key <= query


def load_keys(own_ref, oth_ref, group, lay):
    low = lane_low((lay.rows, LANES))
    halves = [
        jnp.where(low, unpack_values(ref, group, lay), ref[group, : lay.rows, :].astype(F32))
        for ref in (own_ref, oth_ref)
    ]
    return jnp.concatenate(halves, axis=0)


def load_query(own_ref, at, lay):
    value = swap_halves(own_ref[at, : lay.rows, :].astype(F32)) * (1.0 / math.sqrt(DH))
    return jnp.where(lane_low(value.shape), 0.0, value)


def load_rows(load, groups):
    return jnp.concatenate([load(g) for g in groups], axis=0)


def fold_rows(value, op):
    return op(value.reshape(value.shape[0] // 8, 8, value.shape[1]), axis=0)


def unpack_rows(ref, at, lay):
    packed = ref[at].astype(F32)
    grad = jnp.concatenate([packed, swap_halves(packed)[: lay.rows - lay.top]], axis=0)
    return jnp.where(lane_low(grad.shape), grad, 0.0)


def attend(flags, own, oth, lay, long_clip):
    groups = own.shape[0]
    parts = lay.parts if long_clip else 1
    per = 2 if long_clip else 1
    count = groups // per
    keys, queries = 2 * lay.rows * per, lay.rows * per
    depth = count if long_clip else UNROLL

    def body(flag_ref, own_ref, oth_ref, o_ref, ot_ref, lse_ref, kv_ref, vt_ref, st_ref):
        core = flag_ref[2]
        part = flag_ref[3]

        def prepare(tile, slot):
            rows = jnp.concatenate([load_keys(own_ref, oth_ref, per * tile + k, lay) for k in range(per)], axis=0)
            kv_ref[slot] = rows.astype(BF)
            vt_ref[slot] = rows.T[:HALF].astype(BF)

        def block(at, slot):
            query = load_rows(lambda g: load_query(own_ref, g, lay), [per * at + k for k in range(per)]).astype(BF)

            def scores(kt, top):
                score = dot_lanes(kv_ref[kt], query)
                st_ref[kt] = score
                return jnp.maximum(top, fold_rows(score, jnp.max))

            top = jnp.full((8, queries), NEG_BIG, F32)
            if long_clip:
                top = lax.fori_loop(0, at, scores, top)
            score = dot_lanes(kv_ref[slot], query)
            score = jnp.where(diag_mask(keys, queries, core), score, NEG_BIG)
            st_ref[slot] = score
            top = jnp.max(jnp.maximum(top, fold_rows(score, jnp.max)), axis=0, keepdims=True)

            def mix(kt, carry):
                total, acc = carry
                expo = jnp.exp(st_ref[kt] - top)
                total = total + fold_rows(expo, jnp.sum)
                return total, acc + dot(vt_ref[kt], expo.astype(BF))

            zero = (jnp.zeros((8, queries), F32), jnp.zeros((HALF, queries), F32))
            if long_clip:
                total, acc = lax.fori_loop(0, at + 1, mix, zero)
            else:
                total, acc = mix(slot, zero)
            total = jnp.sum(total, axis=0, keepdims=True)
            acc = acc / total
            ot_ref[at] = acc
            lse_ref[at] = jnp.broadcast_to(top + jnp.log(total), (8, queries))
            out = jnp.concatenate([acc, jnp.zeros_like(acc)], axis=0).T
            for k in range(per):
                o_ref[per * at + k] = split_pair(out[k * lay.rows : (k + 1) * lay.rows], lay.top)[0].astype(BF)

        if long_clip:
            def prepare_loop(tile, _):
                prepare(tile, tile)
                return 0

            lax.fori_loop(0, count, prepare_loop, 0)
            if parts > 1:
                o_ref[...] = jnp.zeros_like(o_ref)

            def block_loop(step, _):
                at = step * parts + part if parts > 1 else step
                block(at, at)
                return 0

            lax.fori_loop(0, count // parts, block_loop, 0)
        else:
            def head_loop(step, _):
                for k in range(UNROLL):
                    prepare(UNROLL * step + k, k)
                for k in range(UNROLL):
                    block(UNROLL * step + k, k)
                return 0

            lax.fori_loop(0, count // UNROLL, head_loop, 0)

    pairs = count * (count + 1) // 2 if long_clip else count
    return kernel_call(
        body,
        flags,
        [own, oth],
        [
            shape_of((groups, lay.top, LANES), BF),
            shape_of((count, HALF, queries), F32),
            shape_of((count, 8, queries), F32),
        ],
        scratch=[
            pltpu.VMEM((depth, keys, LANES), BF),
            pltpu.VMEM((depth, HALF, keys), BF),
            pltpu.VMEM((depth, keys, queries), F32),
        ],
        out_pins=(1, 2),
        vmem=max(24, 3 * groups) if long_clip else 16,
        flops=pairs * 16 * keys * queries * DH // parts,
        name="attend_long" if long_clip else "attend_short",
    )


def attend_back(flags, own, oth, d_outs, ot, lse, tab_cos, tab_sin, time_cos, time_sin, lay, long_clip):
    groups = own.shape[0]
    parts = lay.parts if long_clip else 1
    per = 2 if long_clip else 1
    count = groups // per
    keys, queries = 2 * lay.rows * per, lay.rows * per
    depth = count if long_clip else UNROLL

    def body(flag_ref, own_ref, oth_ref, *refs):
        do_refs, refs = refs[: len(d_outs)], refs[len(d_outs) :]
        ot_ref, lse_ref, tc_ref, ts_ref, qc_ref, qs_ref, dq_ref, down_ref, doth_ref, kv_ref, kt_ref, acc_ref = refs
        own_long = flag_ref[0]
        core = flag_ref[2]
        part = flag_ref[3]

        def prepare(tile, slot):
            rows = jnp.concatenate([load_keys(own_ref, oth_ref, per * tile + k, lay) for k in range(per)], axis=0)
            kv_ref[slot] = rows.astype(BF)
            kt_ref[slot] = rows.T[HALF:].astype(BF)
            if long_clip:
                acc_ref[slot] = jnp.zeros((keys, LANES), F32)

        def block(at, slot):
            members = [per * at + k for k in range(per)]
            query = load_rows(lambda g: load_query(own_ref, g, lay), members).astype(BF)
            if long_clip:
                grad = load_rows(lambda g: unpack_rows(do_refs[0], g, lay), members)
            else:
                grad = load_rows(
                    lambda g: jnp.where(own_long == 1, unpack_rows(do_refs[1], g, lay), unpack_rows(do_refs[0], g, lay)), members
                )
            delta = jnp.sum(grad.T[:HALF] * ot_ref[at], axis=0, keepdims=True)
            grad = grad.astype(BF)
            lse_row = lse_ref[at][0:1]

            def tile_back(kt, acc, diag):
                tile = kv_ref[kt]
                prob = jnp.exp(dot_lanes(tile, query) - lse_row)
                if diag:
                    prob = jnp.where(diag_mask(keys, queries, core), prob, 0.0)
                score_grad = (prob * (dot_lanes(tile, grad) - delta)).astype(BF)
                both = dot(score_grad, query) + dot(prob.astype(BF), grad)
                if long_clip:
                    acc_ref[kt] += both
                else:
                    acc_ref[kt] = both
                return acc + dot(kt_ref[kt], score_grad)

            acc = tile_back(slot, jnp.zeros((HALF, queries), F32), True)
            if long_clip:
                acc = lax.fori_loop(0, at, lambda kt, a: tile_back(kt, a, False), acc)
            acc = acc * (1.0 / math.sqrt(DH))
            turned = jnp.concatenate([acc, jnp.zeros_like(acc)], axis=0).T
            for k, group in enumerate(members):
                dq = turned[k * lay.rows : (k + 1) * lay.rows]
                tab = group if long_clip else 0
                cosine = tc_ref[...] + per_frame(dq.shape, qc_ref[2 * tab], qc_ref[2 * tab + 1])
                sine = ts_ref[...] + per_frame(dq.shape, qs_ref[2 * tab], qs_ref[2 * tab + 1])
                dq_ref[group] = (dq * cosine - swap_pairs(dq) * sine).astype(BF)

        def flush(tile, slot):
            for k in range(per):
                down_ref[per * tile + k] = acc_ref[slot, 2 * k * lay.rows : (2 * k + 1) * lay.rows]
                doth_ref[per * tile + k] = acc_ref[slot, (2 * k + 1) * lay.rows : (2 * k + 2) * lay.rows].astype(BF)

        if long_clip:
            def prepare_loop(tile, _):
                prepare(tile, tile)
                return 0

            lax.fori_loop(0, count, prepare_loop, 0)
            if parts > 1:
                dq_ref[...] = jnp.zeros_like(dq_ref)

            def block_loop(step, _):
                at = step * parts + part if parts > 1 else step
                block(at, at)
                return 0

            lax.fori_loop(0, count // parts, block_loop, 0)

            def flush_loop(tile, _):
                flush(tile, tile)
                return 0

            lax.fori_loop(0, count, flush_loop, 0)
        else:
            def head_loop(step, _):
                for k in range(UNROLL):
                    prepare(UNROLL * step + k, k)
                for k in range(UNROLL):
                    block(UNROLL * step + k, k)
                for k in range(UNROLL):
                    flush(UNROLL * step + k, k)
                return 0

            lax.fori_loop(0, count // UNROLL, head_loop, 0)

    pairs = count * (count + 1) // 2 if long_clip else count
    return kernel_call(
        body,
        flags,
        [own, oth, *d_outs, ot, lse, tab_cos, tab_sin, time_cos, time_sin],
        [
            shape_of((groups, lay.rows, LANES), BF),
            shape_of((groups, lay.rows, LANES), F32),
            shape_of((groups, lay.rows, LANES), BF),
        ],
        scratch=[
            pltpu.VMEM((depth, keys, LANES), BF),
            pltpu.VMEM((depth, HALF, keys), BF),
            pltpu.VMEM((depth, keys, LANES), F32),
        ],
        out_pins=(0, 1),
        vmem=max(24, 3 * groups) if long_clip else 20,
        pins=(0, 1) + tuple(range(2 + len(d_outs), 8 + len(d_outs))),
        flops=pairs * 40 * keys * queries * DH // parts,
        name="attend_back_long" if long_clip else "attend_back_short",
    )


def finish_keys(flags, dq, mine, theirs, tab_cos, tab_sin, time_cos, time_sin, lay, long_clip):
    groups = dq.shape[0]

    def body(flag_ref, dq_ref, a_ref, b_ref, tc_ref, ts_ref, qc_ref, qs_ref, out_ref):
        def one(group, _):
            both = a_ref[group] + b_ref[group].astype(F32)
            tab = group if long_clip else 0
            cosine = tc_ref[...] + per_frame(both.shape, qc_ref[2 * tab], qc_ref[2 * tab + 1])
            sine = ts_ref[...] + per_frame(both.shape, qs_ref[2 * tab], qs_ref[2 * tab + 1])
            keys = both * cosine - swap_pairs(both) * sine
            out_ref[group, : lay.rows, :] = jnp.where(lane_low(keys.shape), dq_ref[group].astype(F32), keys).astype(BF)
            out_ref[group, lay.vrow :, :] = split_pair(both, lay.top)[0].astype(BF)
            return 0

        lax.fori_loop(0, groups, one, 0)

    return kernel_call(
        body,
        flags,
        [dq, mine, theirs, tab_cos, tab_sin, time_cos, time_sin],
        [shape_of((groups, lay.vrow + lay.top, LANES), BF)],
        pins=(0, 1),
        vmem=max(16, groups),
        flops=groups * lay.rows * LANES * 10,
        name="finish_keys",
    )[0]


def project_and_norm(flags, long_out, short_out, recv, weight, bias, tokens, mods, lay):
    rows, width = tokens.shape
    half = lay.heads * DH

    def body(flag_ref, long_ref, short_ref, recv_ref, w_ref, b_ref, tok_ref, mod_ref, branch_ref, resid_ref, normed_ref, inv_ref, hid_ref, att_ref):
        own_long = flag_ref[0]
        side = flag_ref[1]
        for pair in range(lay.heads // 2):
            kept = [
                jnp.where(own_long == 1, long_ref[2 * pair + k].astype(F32), short_ref[2 * pair + k].astype(F32)) for k in (0, 1)
            ]
            got = [recv_ref[2 * pair + k].astype(F32) for k in (0, 1)]
            lanes = slice(pair * LANES, (pair + 1) * LANES)
            att_ref[side, :, lanes] = join_pair(kept[0], kept[1], rows).astype(BF)
            att_ref[1 - side, :, lanes] = join_pair(got[0], got[1], rows).astype(BF)
        branch = dot(att_ref[0], w_ref[:half]) + dot(att_ref[1], w_ref[half:]) + b_ref[...]
        branch_ref[...] = branch
        gate = per_frame(branch.shape, mod_ref[0:1], mod_ref[1:2])
        resid = tok_ref[...].astype(F32) + gate * branch
        resid_ref[...] = resid
        normed, inv_std = norm_rows(resid)
        normed_ref[...] = normed
        inv_ref[...] = jnp.broadcast_to(inv_std, inv_ref.shape)
        shift = per_frame(branch.shape, mod_ref[2:3], mod_ref[3:4])
        scale = per_frame(branch.shape, mod_ref[4:5], mod_ref[5:6])
        hid_ref[...] = (normed * (1.0 + scale) + shift).astype(BF)

    full = shape_of((rows, width), F32)
    return kernel_call(
        body,
        flags,
        [long_out, short_out, recv, weight, bias, tokens, mods],
        [full, full, full, shape_of((rows, LANES), F32), shape_of((rows, width), BF)],
        scratch=[pltpu.VMEM((2, rows, half), BF)],
        out_pins=(0, 1, 2, 3),
        vmem=24,
        flops=2 * rows * width * width,
        name="project_and_norm",
    )


def hidden_blocks(width, wide, chunks, weight_rows):
    def pick(k):
        def at(i, f):
            block = 2 * (chunks * i + k) + f[1]
            return (block, 0) if weight_rows else (0, block)
        return at

    return [pl.BlockSpec((wide, width) if weight_rows else (width, wide), pick(k)) for k in range(chunks)]


def ahead_grads(flags, mlp_grad, down_weight, name):
    rows, width = mlp_grad.shape
    ff = down_weight.shape[0]
    wide, chunks = 2 * LANES, 2

    def body(flag_ref, mg_ref, *refs):
        out_ref = refs[-1]
        for k in range(chunks):
            out_ref[:, k * wide : (k + 1) * wide] = dot_lanes(mg_ref[...], refs[k][...])

    return kernel_call(
        body,
        flags,
        [mlp_grad] + [down_weight] * chunks,
        [shape_of((rows, ff // 2), F32)],
        specs=[None] + hidden_blocks(width, wide, chunks, True),
        out_specs=[pl.BlockSpec((rows, chunks * wide), lambda i, f: (0, i))],
        out_pins=(0,),
        grid=(ff // (2 * wide * chunks),),
        flops=rows * width * ff,
        name=name,
    )[0]


def hidden_grads(flags, hidden, ahead, up_weight, up_bias, lay, out_dtype, name):
    rows, width = hidden.shape
    ff = up_weight.shape[1]
    wide, chunks = 2 * LANES, 2
    steps = ff // (2 * wide * chunks)
    quarter = ff // 4

    def body(flag_ref, hid_ref, ahead_ref, *refs):
        weights, outs = refs[: 2 * chunks], refs[2 * chunks :]
        mine_ref, send_ref, bm_ref, bt_ref, hg_ref, hacc = outs
        step = pl.program_id(0)
        first = flag_ref[2] == 0
        back = 0.0
        for k in range(chunks):
            up_ref, ub_ref = weights[k], weights[chunks + k]
            pre = dot(hid_ref[...], up_ref[...]) + ub_ref[...]
            tanh = jnp.tanh(GELU_C * (pre + GELU_K * pre * pre * pre))
            act = (0.5 * pre * (1.0 + tanh)).astype(BF)
            slope = 0.5 * (1.0 + tanh) + 0.5 * pre * (1.0 - tanh * tanh) * GELU_C * (1.0 + 3.0 * GELU_K * pre * pre)
            pre_low = (ahead_ref[:, k * wide : (k + 1) * wide] * slope).astype(BF)
            back = back + dot_lanes(pre_low, up_ref[...])
            sums = jnp.sum(pre_low.astype(F32), axis=0, keepdims=True)
            lanes = slice(k * LANES, (k + 1) * LANES)
            for at, value in ((0, act), (1, pre_low)):
                mine_ref[at, :, lanes] = jnp.where(first, value[:, :LANES], value[:, LANES:])
                send_ref[at, :, lanes] = jnp.where(first, value[:, LANES:], value[:, :LANES])
            bm_ref[:, lanes] = jnp.broadcast_to(jnp.where(first, sums[:, :LANES], sums[:, LANES:]), (8, LANES))
            bt_ref[:, lanes] = jnp.broadcast_to(jnp.where(first, sums[:, LANES:], sums[:, :LANES]), (8, LANES))

        @pl.when(step == 0)
        def _():
            hacc[...] = back

        @pl.when(step > 0)
        def _():
            hacc[...] += back

        @pl.when(step == steps - 1)
        def _():
            hg_ref[...] = hacc[...].astype(hg_ref.dtype)

    chunk = pl.BlockSpec((2, rows, chunks * LANES), lambda i, f: (0, 0, i))
    bchunk = pl.BlockSpec((8, chunks * LANES), lambda i, f: (0, i))
    return kernel_call(
        body,
        flags,
        [hidden, ahead] + [up_weight] * chunks + [up_bias] * chunks,
        [shape_of((2, rows, quarter), BF)] * 2 + [shape_of((8, quarter), F32)] * 2 + [shape_of((rows, width), out_dtype)],
        specs=[None, pl.BlockSpec((rows, chunks * wide), lambda i, f: (0, i))]
        + hidden_blocks(width, wide, chunks, False)
        + hidden_blocks(1, wide, chunks, False),
        out_specs=[chunk, chunk, bchunk, bchunk, None],
        grid=(steps,),
        scratch=[pltpu.VMEM((rows, width), F32)],
        pins=(1,),
        flops=2 * rows * width * ff,
        name=name,
    )


def forward_rows(flags, mine, send, mine2, send2, down_weight):
    _, rows, quarter = mine.shape
    ff, width = down_weight.shape
    wide, chunks = 2 * LANES, 2
    steps = ff // (2 * wide * chunks)

    def body(flag_ref, m_ref, s_ref, m2_ref, s2_ref, *refs):
        own_ref, oth_ref, acc_ref = refs[chunks:]
        first = flag_ref[2] == 0
        step = pl.program_id(0)
        for at, (a_ref, b_ref) in enumerate(((m_ref, s_ref), (m2_ref, s2_ref))):
            total = 0.0
            for k in range(chunks):
                lanes = slice(k * LANES, (k + 1) * LANES)
                a, b = a_ref[:, lanes], b_ref[:, lanes]
                act = jnp.concatenate([jnp.where(first, a, b), jnp.where(first, b, a)], axis=1)
                total = total + dot(act, refs[k][...])

            @pl.when(step == 0)
            def _(total=total, at=at):
                acc_ref[at] = total

            @pl.when(step > 0)
            def _(total=total, at=at):
                acc_ref[at] += total

        @pl.when(step == steps - 1)
        def _():
            own_ref[...] = acc_ref[0]
            oth_ref[...] = acc_ref[1].astype(BF)

    chunk = pl.BlockSpec((None, rows, chunks * LANES), lambda i, f: (0, 0, i))
    return kernel_call(
        body,
        flags,
        [mine, send, mine2, send2] + [down_weight] * chunks,
        [shape_of((rows, width), F32), shape_of((rows, width), BF)],
        specs=[chunk] * 4 + hidden_blocks(width, wide, chunks, True),
        scratch=[pltpu.VMEM((2, rows, width), F32)],
        out_pins=(0,),
        grid=(steps,),
        flops=2 * rows * width * ff,
        name="forward_rows",
    )


def scale_cotangent(flags, cotangent, gates):
    rows, width = cotangent.shape

    def body(flag_ref, dy_ref, g_ref, out_ref, sums_ref):
        low = (per_frame((rows, width), g_ref[0:1], g_ref[1:2]) * dy_ref[...].astype(F32)).astype(BF)
        out_ref[...] = low
        sums_ref[...] = jnp.broadcast_to(jnp.sum(low.astype(F32), axis=0, keepdims=True), sums_ref.shape)

    return kernel_call(
        body,
        flags,
        [cotangent, gates],
        [shape_of((rows, width), BF), shape_of((8, width), F32)],
        pins=(0,),
        flops=rows * width,
        name="scale_cotangent",
    )


def layer_output(flags, mlp_own, mlp_recv, bias, resid, cotangent, gates):
    rows, width = resid.shape

    def body(flag_ref, a_ref, b_ref, bias_ref, r_ref, dy_ref, g_ref, out_ref, sums_ref):
        mlp = a_ref[...] + b_ref[...].astype(F32) + bias_ref[...]
        out_ref[...] = (r_ref[...] + per_frame((rows, width), g_ref[0:1], g_ref[1:2]) * mlp).astype(BF)
        sums_ref[0:1], sums_ref[1:2] = frame_sums(dy_ref[...].astype(F32) * mlp)
        sums_ref[2:8] = jnp.zeros((6, width), F32)

    return kernel_call(
        body,
        flags,
        [mlp_own, mlp_recv, bias, resid, cotangent, gates],
        [shape_of((rows, width), BF), shape_of((8, width), F32)],
        pins=(0, 3, 4),
        flops=rows * width * 4,
        name="layer_output",
    )


def pack_rows(flags, n_blk, mid, gate2, silu, down_b, up_sums, sum_long, sum_short, bias_long, bias_short):
    width = mid.shape[1]
    cols = bias_long.shape[1]

    def body(flag_ref, mid_ref, g_ref, s_ref, d_ref, m1, m2, t1, t2, sl, ss, bl, bs, out_ref):
        bias = bl[0:1] + bs[0:1]
        bias = jnp.concatenate([bias, jnp.zeros((1, 2 * width - cols), F32)], axis=1)
        rows = jnp.concatenate(
            [mid_ref[0:6], g_ref[0:2], s_ref[...].astype(F32), d_ref[0:1], mid_ref[6:7], m1[0:1] + m2[0:1], t1[0:1] + t2[0:1],
             sl[0:4], ss[0:4], bias[:, :width], bias[:, width:]],
            axis=0,
        ).astype(BF)
        for k in range(n_blk):
            out_ref[k] = rows

    return kernel_call(
        body,
        flags,
        [mid, gate2, silu, down_b, *up_sums, sum_long, sum_short, bias_long, bias_short],
        [shape_of((n_blk, PACK, width), BF)],
        flops=width * PACK,
        name="pack_rows",
    )[0]


def branch_back(flags, hid_own, hid_recv, cotangent, normed, inv_std, branch, mods, weight, lay):
    rows, width = normed.shape
    half = lay.heads * DH

    def body(flag_ref, a_ref, b_ref, dy_ref, n_ref, inv_ref, br_ref, mod_ref, w_ref, rg_ref, bg_ref, keep_ref, send_ref, sums_ref):
        side = flag_ref[1]
        hid = a_ref[...] + b_ref[...].astype(F32)
        norm = n_ref[...]
        scale = per_frame(hid.shape, mod_ref[4:5], mod_ref[5:6])
        resid = dy_ref[...].astype(F32) + norm_back(hid * (1.0 + scale), norm, inv_ref[:, 0:1])
        rg_ref[...] = resid
        gate = per_frame(hid.shape, mod_ref[0:1], mod_ref[1:2])
        low = (gate * resid).astype(BF)
        bg_ref[...] = low
        for out_ref, which in ((keep_ref, side), (send_ref, 1 - side)):
            grad = dot_lanes(low, w_ref[pl.ds(pl.multiple_of(which * half, half), half), :])
            for pair in range(lay.heads // 2):
                one, two = split_pair(grad[:, pair * LANES : (pair + 1) * LANES], lay.top)
                out_ref[2 * pair] = one.astype(BF)
                out_ref[2 * pair + 1] = two.astype(BF)
        sums_ref[0:1], sums_ref[1:2] = frame_sums(resid * br_ref[...])
        sums_ref[2:3], sums_ref[3:4] = frame_sums(hid)
        sums_ref[4:5], sums_ref[5:6] = frame_sums(hid * norm)
        sums_ref[6:7] = jnp.sum(low.astype(F32), axis=0, keepdims=True)
        sums_ref[7:8] = jnp.zeros((1, width), F32)

    packed = shape_of((lay.heads, lay.top, LANES), BF)
    return kernel_call(
        body,
        flags,
        [hid_own, hid_recv, cotangent, normed, inv_std, branch, mods, weight],
        [shape_of((rows, width), F32), shape_of((rows, width), BF), packed, packed, shape_of((8, width), F32)],
        pins=(0, 2, 3, 4, 5, 6),
        out_pins=(0,),
        vmem=24,
        flops=2 * rows * width * width,
        name="branch_back",
    )


def qkv_back(flags, grads, tok_own, tok_oth, weight, lay, is_long):
    rows, width = tok_own.shape
    cols = lay.heads * DH
    half = cols // 2

    def body(flag_ref, *refs):
        g_refs, refs = refs[: len(grads)], refs[len(grads) :]
        own_ref, oth_ref, w_ref, hid_ref, low_ref, gm_ref, gt_ref, bias_ref, sums_ref, q_ref, acc_ref = refs
        step = pl.program_id(0)
        core = flag_ref[2]

        @pl.when(step == 0)
        def _():
            if not is_long:
                dq_ref, a_ref, b_ref, tc_ref, ts_ref, qc_ref, qs_ref = g_refs
                table = (rows, LANES)
                cosine = tc_ref[...] + per_frame(table, qc_ref[0], qc_ref[1])
                sine = ts_ref[...] + per_frame(table, qs_ref[0], qs_ref[1])
            for pair in range(lay.heads // 2):
                lanes = slice(pair * LANES, (pair + 1) * LANES)
                low = lane_low((rows, LANES))
                if is_long:
                    g_ref = g_refs[0]
                    one, two = (g_ref[2 * pair + k, :rows, :].astype(F32) for k in (0, 1))
                    query, key = jnp.where(low, one, swap_halves(two)), jnp.where(low, swap_halves(one), two)
                    value = join_pair(*(g_ref[2 * pair + k, lay.vrow :, :].astype(F32) for k in (0, 1)), rows)
                else:
                    one, two = (dq_ref[2 * pair + k].astype(F32) for k in (0, 1))
                    query = jnp.where(low, one, swap_halves(two))
                    one, two = (a_ref[2 * pair + k] + b_ref[2 * pair + k].astype(F32) for k in (0, 1))
                    value = jnp.where(low, one, swap_halves(two))
                    one, two = (v * cosine - swap_pairs(v) * sine for v in (one, two))
                    key = jnp.where(low, swap_halves(one), two)
                q_ref[0, :, lanes] = query.astype(BF)
                q_ref[1, :, lanes] = key.astype(BF)
                q_ref[2, :, lanes] = value.astype(BF)

        value = q_ref[step]
        part = dot_lanes(value, w_ref[...])

        @pl.when(step == 0)
        def _():
            acc_ref[...] = part

        @pl.when(step > 0)
        def _():
            acc_ref[...] += part

        first = core == 0
        gm_ref[...] = jnp.where(first, value[:, :half], value[:, half:])
        gt_ref[...] = jnp.where(first, value[:, half:], value[:, :half])
        bias_ref[...] = jnp.broadcast_to(jnp.sum(value.astype(F32), axis=0, keepdims=True), bias_ref.shape)

        @pl.when(step == 2)
        def _():
            hid = acc_ref[...]
            hid_ref[...] = hid
            low_ref[...] = hid.astype(BF)
            mine = (flag_ref[0] == 1) if is_long else (flag_ref[0] == 0)
            normed, _ = norm_rows(jnp.where(mine, own_ref[...].astype(F32), oth_ref[...].astype(F32)))
            sums_ref[0:1], sums_ref[1:2] = frame_sums(hid)
            sums_ref[2:3], sums_ref[3:4] = frame_sums(hid * normed)
            sums_ref[4:8] = jnp.zeros((4, width), F32)

    return kernel_call(
        body,
        flags,
        [*grads, tok_own, tok_oth, weight],
        [
            shape_of((rows, width), F32),
            shape_of((rows, width), BF),
            shape_of((rows, 3 * half), BF),
            shape_of((rows, 3 * half), BF),
            shape_of((8, 3 * cols), F32),
            shape_of((8, width), F32),
        ],
        specs=[None] * (len(grads) + 2) + [pl.BlockSpec((width, cols), lambda j, f: (0, 2 * j + f[1]))],
        out_specs=[
            None, None,
            pl.BlockSpec((rows, half), lambda j, f: (0, j)),
            pl.BlockSpec((rows, half), lambda j, f: (0, j)),
            pl.BlockSpec((8, cols), lambda j, f: (0, j)),
            None,
        ],
        pins=(len(grads), len(grads) + 1) + (() if is_long else (0, 1)),
        out_pins=(0,),
        grid=(3,),
        scratch=[pltpu.VMEM((3, rows, cols), BF), pltpu.VMEM((rows, width), F32)],
        flops=6 * rows * width * cols,
        name="qkv_back_long" if is_long else "qkv_back_short",
    )


def token_back(flags, hid_long, hid_short, recv, tokens, resid_grad, mods, lay):
    rows, width = tokens.shape

    def body(flag_ref, l_ref, s_ref, r_ref, tok_ref, rg_ref, mod_ref, out_ref):
        hid = jnp.where(flag_ref[0] == 1, l_ref[...], s_ref[...]) + r_ref[...].astype(F32)
        normed, inv_std = norm_rows(tok_ref[...].astype(F32))
        scale = per_frame(hid.shape, mod_ref[0:1, width : 2 * width], mod_ref[1:2, width : 2 * width])
        out_ref[...] = rg_ref[...] + norm_back(hid * (1.0 + scale), normed, inv_std)

    return kernel_call(
        body,
        flags,
        [hid_long, hid_short, recv, tokens, resid_grad, mods],
        [shape_of((rows, width), F32)],
        pins=(0, 1, 3, 4, 5),
        flops=rows * width * 20,
        name="token_back",
    )[0]


def group_spec(pair, rows, wide, moves):
    index = pair[1]
    if index is None:
        return pl.BlockSpec((rows, wide), lambda i, f: (0, i if moves else 0))
    return pl.BlockSpec((None, rows, wide), lambda i, f: (index, 0, i if moves else 0))


def width_of(jobs):
    return sum(rights[0][0].shape[-1] for _, rights in jobs)


def split_weight_grads(flags, jobs, n_blk, cuts, head_rows, name):
    count = len(jobs[0][0])
    rows, depth = jobs[0][0][0][0].shape[-2:]
    pieces = [(job, *cut) for job, many in enumerate(cuts) for cut in many]
    tall = depth // n_blk
    wide = max(tall, LANES)
    per = wide // tall
    operands = [pair for lefts, rights in jobs for pair in [*lefts, *rights]]
    extra = 0
    if head_rows:
        head = head_rows[0].shape[1] // n_blk
        turns = head_rows[0].shape[2] // cuts[0][-1][1]
        extra = head * turns

    def body(flag_ref, *refs):
        outs = refs[len(operands) + len(head_rows) :]
        step = pl.program_id(0)
        results = []
        for job in range(len(jobs)):
            mine = refs[2 * count * job : 2 * count * (job + 1)]
            acc = dot_rows(mine[0][...], mine[count][...])
            for k in range(1, count):
                acc += dot_rows(mine[k][...], mine[count + k][...])
            results.append(acc.astype(BF))
        for member in range(per):
            place = relative_place(step * per + member, flag_ref[4], n_blk)
            if head_rows:
                part_ref, got_ref = refs[len(operands) : len(operands) + 2]
                at = pl.ds(pl.multiple_of((step * per + member) * head, head), head)
                both = (part_ref[flag_ref[2], at].astype(F32) + got_ref[at].astype(F32)).astype(BF)
            for out, (job, start, cols, order) in enumerate(pieces):
                sent, at = half_place(place, order)
                values = [results[job][member * tall : (member + 1) * tall, start : start + cols]]
                if head_rows and out == len(pieces) - 1:
                    values += [both[:, turn * cols : (turn + 1) * cols] for turn in range(turns)]

                def store(out_ref, values=values, at=at):
                    row = 0
                    for value in values:
                        out_ref[at, row : row + value.shape[0]] = value
                        row += value.shape[0]

                pl.when(sent == 1)(functools.partial(store, outs[2 * out]))
                pl.when(sent == 0)(functools.partial(store, outs[2 * out + 1]))

    specs = []
    for lefts, rights in jobs:
        specs += [group_spec(pair, rows, wide, True) for pair in lefts]
        specs += [group_spec(pair, rows, pair[0].shape[-1], False) for pair in rights]
    outs = []
    for out, (job, start, cols, order) in enumerate(pieces):
        outs += [shape_of((n_blk // 2, tall + (extra if out == len(pieces) - 1 else 0), cols), BF)] * 2
    return kernel_call(
        body,
        flags,
        [array for array, _ in operands] + list(head_rows),
        outs,
        specs=specs + [None] * len(head_rows),
        grid=(depth // wide,),
        vmem=24,
        pins=tuple(range(len(operands))) if head_rows else (),
        flops=2 * count * rows * depth * width_of(jobs),
        name=name,
    )


def head_weight_grads(flags, longs, shorts, grad_own, grad_oth, lay):
    rows, width = grad_own.shape
    pairs = lay.heads // 2

    def body(flag_ref, l_ref, s_ref, go_ref, gt_ref, out_ref):
        own_long = flag_ref[0] == 1
        grads = jnp.where(own_long, go_ref[...], gt_ref[...]), jnp.where(own_long, gt_ref[...], go_ref[...])
        for pair in range(pairs):
            acc = 0.0
            for ref, grad in zip((l_ref, s_ref), grads):
                left = join_pair(ref[2 * pair].astype(F32), ref[2 * pair + 1].astype(F32), rows).astype(BF)
                acc = acc + dot_rows(left, grad)
            out_ref[pair * LANES : (pair + 1) * LANES, :] = acc.astype(BF)

    return kernel_call(
        body,
        flags,
        [longs, shorts, grad_own, grad_oth],
        [shape_of((lay.heads * DH, width), BF)],
        pins=(0, 1),
        flops=4 * rows * width * lay.heads * DH,
        name="head_weight_grads",
    )[0]


def relative_place(target, here, n_blk):
    relative = target ^ here
    return relative ^ ((relative >> 1) & (10 & (n_blk - 1)))


def half_place(place, order):
    at = 0
    for bit in order[1:]:
        at = 2 * at + ((place >> bit) & 1)
    return (place >> order[0]) & 1, at


def hop_of(bit):
    return (1 << bit) if bit == 0 or bit % 2 == 1 else (1 << bit) | (1 << (bit - 1))


class CubeSum:
    def __init__(self, send, keep, n_blk, order):
        self.n_blk, self.order, self.at = n_blk, order, 0
        self.bits = n_blk.bit_length() - 1
        self.send, self.keep, self.value, self.got = send, keep, None, None

    def move(self, *starts):
        hop = hop_of(self.order[self.at])
        send = after(self.send, *starts) if starts else self.send
        self.got = lax.ppermute(send, "blk", [(i, i ^ hop) for i in range(self.n_blk)])

    def add(self):
        self.at += 1
        half = self.keep.shape[0] // 2
        if self.at == self.bits:
            self.value = (self.keep.astype(F32) + self.got.astype(F32))[0]
        else:
            low = [(self.keep[k].astype(F32) + self.got[k].astype(F32)).astype(BF) for k in (slice(half), slice(half, None))]
            self.keep, self.send = low

    def finish(self):
        while self.at < self.bits:
            self.move()
            self.add()
        return self.value


def lay_out_rows(flags, gathered, split, ff, name):
    n_uly, rows, total = gathered.shape
    cols = (total - split) // 3

    def body(flag_ref, in_ref, up_ref, attn_ref):
        for u in range(n_uly):
            for i in range(split // LANES):
                at = (i * n_uly + u) * LANES
                up_ref[:, at : at + LANES] = in_ref[u, :, i * LANES : (i + 1) * LANES].astype(F32)
            for j in range(3):
                at = (j * n_uly + u) * cols
                attn_ref[:, at : at + cols] = in_ref[u, :, split + j * cols : split + (j + 1) * cols].astype(F32)

    return kernel_call(
        body,
        flags,
        [gathered],
        [shape_of((rows, ff), F32), shape_of((rows, 3 * n_uly * cols), F32)],
        flops=rows * total,
        name=name,
    )


def modulation_grads(flags, long_rows, gathered, row_out, name):
    total, width = gathered.shape
    quarter = total // 4

    def body(flag_ref, long_ref, g_ref, out_ref, sums_ref, part_ref):
        start = flag_ref[5]
        block = pl.multiple_of((start // LANES) * LANES, LANES)
        silu = g_ref[:, pl.ds(block, LANES)].astype(F32)
        parts = [silu[k * quarter : (k + 1) * quarter] for k in (1, 0, 3, 2)]
        mate = jnp.concatenate(parts, axis=0)
        own_long = long_ref[...] > 0.5

        def place_of(index):
            return index - PACK * ((index * 2731) >> 16)

        place = place_of(lax.broadcasted_iota(jnp.int32, (total, LANES), 0))

        def aligned(value, base):
            return jnp.where((place == base) | (place == base + 1), pltpu.roll(value, (base - 8) % total, 0), 0.0)

        def owner(base, is_long):
            return jnp.where(own_long == is_long, aligned(silu, base), aligned(mate, base))

        lefts = [
            owner(14, True) + owner(18, False),
            owner(16, True) + owner(20, False),
            aligned(silu, 0),
            aligned(silu, 2),
            aligned(silu, 4),
            aligned(silu, 6),
        ]
        for k, left in enumerate(lefts):
            part_ref[...] = dot_rows(left.astype(BF), g_ref[...])
            out_ref[:, k * width : (k + 1) * width] = part_ref[pl.ds(pl.multiple_of(start - block, row_out), row_out), :]
        row = lax.broadcasted_iota(jnp.int32, (32, quarter), 0)
        which = jnp.where(row == place_of(lax.broadcasted_iota(jnp.int32, (32, quarter), 1)), 1.0, 0.0).astype(BF)
        for u in range(4):
            sums_ref[u] = dot(which, g_ref[u * quarter : (u + 1) * quarter, :])

    return kernel_call(
        body,
        flags,
        [long_rows, gathered],
        [shape_of((row_out, 6 * width), F32), shape_of((4, 32, width), F32)],
        scratch=[pltpu.VMEM((LANES, width), F32)],
        vmem=max(16, 16 * total // 768),
        flops=total * width * LANES * 12,
        name=name,
    )


def after(value, *earlier):
    return lax.optimization_barrier((value,) + earlier)[0]


def rotary_static(frames):
    n_time, n_row = DH // 8, 3 * DH // 16
    cosine = np.zeros((frames * PATCH, LANES), np.float32)
    sine = np.zeros((frames * PATCH, LANES), np.float32)
    patch = np.arange(frames * PATCH) % PATCH
    for group, place in ((0, patch // GRID), (1, patch % GRID)):
        for j in range(n_row):
            freq = np.exp(np.float32(-math.log(10000.0)) * np.float32(j) / np.float32(n_row)).astype(np.float32)
            angle = (place.astype(np.float32) * freq).astype(np.float64)
            pair = n_time + group * n_row + j
            for head in (0, HALF):
                cosine[:, head + 2 * pair] = np.cos(angle)
                cosine[:, head + 2 * pair + 1] = np.cos(angle)
                sine[:, head + 2 * pair] = -np.sin(angle)
                sine[:, head + 2 * pair + 1] = np.sin(angle)
    return cosine, sine


def rotary_time(times):
    n_time = DH // 8
    lane = jnp.arange(LANES, dtype=jnp.int32)
    pair = (lane % HALF) // 2
    freq = jnp.exp(-math.log(10000.0) * pair.astype(F32) / float(n_time))
    angle = times.astype(F32)[:, None] * freq[None, :]
    live = (pair < n_time)[None, :]
    sign = jnp.where(lane % 2 == 0, -1.0, 1.0)[None, :]
    return jnp.where(live, jnp.cos(angle), 0.0), jnp.where(live, sign * jnp.sin(angle), 0.0)


class Layout:
    def __init__(self, rows, heads, parts):
        self.rows = rows
        self.heads = heads
        self.parts = parts
        self.top = round_up(-(-rows // 2), 16)
        self.vrow = round_up(rows, 16)


def on_device(
    tokens, cotangent, noise_embed, frame_clip, frame_index, mod_weight, mod_bias, attn_weight, attn_bias,
    proj_weight, proj_bias, up_weight, up_bias, down_weight, down_bias,
):
    n_uly = lax.axis_size("uly")
    n_blk = lax.axis_size("blk")
    blk = lax.axis_index("blk")
    uly = lax.axis_index("uly")
    rows, width = tokens.shape
    frames = noise_embed.shape[0]
    side, core = uly // 2, uly % 2
    heads = width // DH // 2
    parts = n_blk // heads
    lay = Layout(rows, heads, parts)
    dev = blk * n_uly + uly

    def swap_side(value):
        return lax.ppermute(value, "uly", [(i, i ^ 2) for i in range(n_uly)])

    def swap_core(value):
        return lax.ppermute(value, "uly", [(i, i ^ 1) for i in range(n_uly)])

    def spread(value):
        return lax.all_to_all(value, "blk", split_axis=0, concat_axis=0, tiled=True)

    long_first = frame_clip[::FB] == n_blk
    own_long_b = lax.dynamic_index_in_dim(long_first, blk, 0, False) == (side == 0)
    own_long = own_long_b.astype(jnp.int32)
    row_out = width // (n_blk * n_uly)
    flags = jnp.stack([own_long, side, core, blk // heads, blk, dev * row_out]).astype(jnp.int32)

    tok_oth = swap_side(tokens)
    silu = jax.nn.silu(noise_embed.astype(F32)).astype(BF)
    bias = mod_bias.astype(F32)
    first_mod = dot(silu, mod_weight[:, : 2 * width]) + bias[: 2 * width]
    first_mods = jnp.concatenate([first_mod, swap_side(first_mod)], axis=0)
    rest_mod = dot(after(silu, first_mod), mod_weight[:, 2 * width :]) + bias[2 * width :]

    block_time = frame_index.reshape(n_blk, FB)
    head_time, tail_time = block_time[:, : FB // 2], block_time[:, FB // 2 :]
    long_times = lax.dynamic_slice_in_dim(jnp.where(long_first[:, None], head_time, tail_time), core * frames, frames, 1)
    short_times = lax.dynamic_slice_in_dim(jnp.where(long_first[:, None], tail_time, head_time), core * frames, frames, 1)
    short_times = lax.dynamic_index_in_dim(short_times, blk, 0, False)
    time_cos, time_sin = rotary_time(jnp.concatenate([lax.dynamic_index_in_dim(long_times, blk, 0, False), short_times]))
    long_cos, long_sin = rotary_time(long_times.reshape(-1))
    short_cos, short_sin = time_cos[frames:, None], time_sin[frames:, None]
    long_cos, long_sin = long_cos[:, None], long_sin[:, None]
    tab_cos, tab_sin = (jnp.asarray(t) for t in rotary_static(frames))
    own_long_all = (long_first[None, :] == ((side ^ jnp.arange(2)) == 0)[:, None]).astype(F32)
    long_rows = jnp.broadcast_to(own_long_all[None, :, :, None, None], (2, 2, n_blk, PACK, LANES)).reshape(-1, LANES)
    first_mods, rest_mod, long_cos, long_sin, short_cos, short_sin, long_rows = lax.optimization_barrier(
        (first_mods, rest_mod, long_cos, long_sin, short_cos, short_sin, long_rows)
    )

    gate2 = rest_mod[:, 3 * width :]
    mid_mods = jnp.concatenate([rest_mod[:, :width], rest_mod[:, width : 2 * width], rest_mod[:, 2 * width : 3 * width]], axis=0)
    mid_mods = jnp.concatenate([mid_mods, jnp.zeros((2, width), F32)], axis=0)
    hidden1, qkv_long, qkv_short = tokens_to_qkv(
        flags, tokens, tok_oth, first_mods, attn_weight, attn_bias.astype(F32)[None], tab_cos, tab_sin, time_cos, time_sin, lay
    )
    sent = jnp.concatenate([qkv_long] * parts, axis=0) if parts > 1 else qkv_long
    long_own = spread(sent)
    short_oth = swap_core(qkv_short)
    out_short, ot_short, lse_short = attend(flags, qkv_short, short_oth, lay, False)
    mlp_grad, down_b = scale_cotangent(flags, after(cotangent, qkv_long), gate2)
    mlp_grad_oth = swap_side(mlp_grad)
    ahead_own = ahead_grads(flags, mlp_grad, down_weight, "ahead_own")
    long_own, out_short, mlp_grad, ahead_own = lax.optimization_barrier((long_own, out_short, mlp_grad, ahead_own))
    long_oth = swap_core(long_own)
    out_long_all, ot_long, lse_long = attend(flags, long_own, long_oth, lay, True)
    out_long_all, mlp_grad_oth = lax.optimization_barrier((out_long_all, mlp_grad_oth))

    def own_part(value):
        if parts == 1:
            return value
        return lax.dynamic_slice_in_dim(value, ((blk // 2) % parts) * heads, heads, 0)

    ahead_oth = ahead_grads(flags, mlp_grad_oth, down_weight, "ahead_other")
    out_long = own_part(spread(out_long_all))
    out_long, ahead_oth = lax.optimization_barrier((out_long, ahead_oth))
    out_recv = swap_side(jnp.where(own_long_b, out_short, out_long))
    branch, resid, normed2, inv2, hidden2 = project_and_norm(
        flags, out_long, out_short, out_recv, proj_weight, proj_bias.astype(F32)[None], tokens, mid_mods, lay
    )

    hidden2_oth = swap_side(hidden2)
    up_b = up_bias.astype(F32)[None]
    mine, send, bm, bt, hid_own = hidden_grads(flags, hidden2, ahead_own, up_weight, up_b, lay, F32, "hidden_own")
    hidden2_oth, hid_own = lax.optimization_barrier((hidden2_oth, hid_own))
    mine2, send2, bm2, bt2, hid_oth = hidden_grads(flags, hidden2_oth, ahead_oth, up_weight, up_b, lay, BF, "hidden_other")
    hid_recv = swap_side(hid_oth)

    got, got2 = swap_core(send), swap_core(send2)
    hid_c, hid_c2, mg_c, mg_c2 = (swap_core(v) for v in (hidden2, hidden2_oth, mlp_grad, mlp_grad_oth))
    plain = lambda *arrays: [(v, None) for v in arrays]
    blocks = [mine, mine2, got, got2]
    bits = list(range(n_blk.bit_length() - 1))
    orders = [bits, [1, 0] + bits[2:]]
    down_order, up_order = ([0, 2, 1], [1, 0, 2]) if len(bits) == 3 else (bits, bits)
    mlp_halves = split_weight_grads(
        flags,
        [
            ([(v, 0) for v in blocks], plain(mlp_grad, mlp_grad_oth, mg_c, mg_c2)),
            (plain(hidden2, hidden2_oth, hid_c, hid_c2), [(v, 1) for v in blocks]),
        ],
        n_blk, [[(0, width, down_order)], [(0, width, up_order)]], [], "mlp_grads",
    )
    hid_recv, *mlp_halves = lax.optimization_barrier((hid_recv, *mlp_halves))

    resid_grad, branch_grad, do_keep, do_send, mid_sums = branch_back(
        flags, hid_own, hid_recv, cotangent, normed2, inv2, branch, mid_mods, proj_weight, lay
    )
    mlp_sums = [CubeSum(*mlp_halves[:2], n_blk, down_order), CubeSum(*mlp_halves[2:], n_blk, up_order)]
    for part in mlp_sums:
        part.move()
    do_recv = swap_side(do_send)
    mlp_own, mlp_oth = forward_rows(flags, mine, send, mine2, after(send2, do_send), down_weight)
    do_recv, mlp_own, mlp_oth = lax.optimization_barrier((do_recv, mlp_own, mlp_oth))
    do_long = jnp.where(own_long_b, do_keep, do_recv)
    if parts > 1:
        hot = (jnp.arange(parts) == (blk // 2) % parts)[:, None, None, None]
        do_sent = jnp.where(hot, do_long[None], 0).reshape((n_blk,) + do_long.shape[1:])
    else:
        do_sent = do_long
    do_all = spread(do_sent)
    dq_s, mine_s, theirs_s = attend_back(
        flags, qkv_short, short_oth, [do_keep, do_recv], ot_short, lse_short, tab_cos, tab_sin, short_cos, short_sin, lay, False
    )
    branch_grad_oth = swap_side(after(branch_grad, do_recv))
    mlp_recv = swap_side(after(mlp_oth, branch_grad_oth))
    do_all, dq_s, mine_s, theirs_s, branch_grad_oth, mlp_sums[0].got, mlp_sums[1].got = lax.optimization_barrier(
        (do_all, dq_s, mine_s, theirs_s, branch_grad_oth, mlp_sums[0].got, mlp_sums[1].got)
    )
    for part in mlp_sums:
        part.add()
    do_all, mlp_sums[0].send, mlp_sums[1].send = lax.optimization_barrier((do_all, mlp_sums[0].send, mlp_sums[1].send))
    for part in mlp_sums:
        part.move()

    dq_l, mine_l, theirs_l = attend_back(
        flags, long_own, long_oth, [do_all], ot_long, lse_long, tab_cos, tab_sin, long_cos, long_sin, lay, True
    )
    theirs_l, mlp_sums[0].got, mlp_sums[1].got = lax.optimization_barrier(
        (swap_core(theirs_l), mlp_sums[0].got, mlp_sums[1].got)
    )
    grads_sent = finish_keys(flags, dq_l, mine_l, theirs_l, tab_cos, tab_sin, long_cos, long_sin, lay, True)
    grads_all = spread(grads_sent)
    if parts > 1:
        grads_long = jnp.sum(grads_all.astype(F32).reshape((parts, heads) + grads_all.shape[1:]), axis=0).astype(BF)
    else:
        grads_long = grads_all

    theirs_s = swap_core(theirs_s)
    branch_grad_oth, dq_s, theirs_s, mlp_sums[0].got, mlp_sums[1].got, _ = lax.optimization_barrier(
        (branch_grad_oth, dq_s, theirs_s, mlp_sums[0].got, mlp_sums[1].got, grads_sent)
    )
    for part in mlp_sums:
        part.add()
    hidS, hidS_low, gmS, gtS, abS, sumS = qkv_back(
        flags, [dq_s, mine_s, theirs_s, tab_cos, tab_sin, short_cos, short_sin], tokens, tok_oth, attn_weight, lay, False
    )
    proj_part = head_weight_grads(flags, out_long, out_short, branch_grad, branch_grad_oth, lay).reshape(2, -1, width)
    proj_got = swap_core(jnp.where(core == 0, proj_part[1], proj_part[0]))
    h1_core = swap_core(hidden1)
    gtS_got = swap_core(gtS)
    grads_long, hidS_low, mlp_sums[0].send, mlp_sums[1].send = lax.optimization_barrier(
        (grads_long, hidS_low, mlp_sums[0].send, mlp_sums[1].send)
    )
    for part in mlp_sums:
        part.move()

    hidL, hidL_low, gmL, gtL, abL, sumL = qkv_back(flags, [grads_long], tokens, tok_oth, attn_weight, lay, True)
    gtL_got = swap_core(gtL)
    hid1_recv = swap_side(jnp.where(own_long_b, hidS_low, hidL_low))
    quarter = 3 * width // n_uly
    split = 2 * quarter // 3
    halves = split_weight_grads(
        flags,
        [([(hidden1, 0), (hidden1, 1), (h1_core, 0), (h1_core, 1)], plain(gmL, gmS, gtL_got, gtS_got))],
        n_blk, [[(0, split, orders[0]), (split, quarter - split, orders[1])]], [proj_part, proj_got], "attn_grads",
    )
    hid1_recv, mlp_recv, mlp_sums[0].got, mlp_sums[1].got, *halves = lax.optimization_barrier(
        (hid1_recv, mlp_recv, mlp_sums[0].got, mlp_sums[1].got, *halves)
    )
    attn_sums = [CubeSum(*halves[2 * k : 2 * k + 2], n_blk, order) for k, order in enumerate(orders)]
    for part in attn_sums:
        part.move()
    token_grad = token_back(flags, hidL, hidS, hid1_recv, tokens, resid_grad, first_mod, lay)
    output, gate2_sums = layer_output(flags, mlp_own, mlp_recv, down_bias.astype(F32)[None], resid, cotangent, gate2)
    gate2_sums, token_grad, *gots = lax.optimization_barrier((gate2_sums, token_grad, *[part.got for part in attn_sums]))
    pack = pack_rows(flags, n_blk, mid_sums, gate2_sums, silu, down_b, (bm, bm2, bt, bt2), sumL, sumS, abL, abS)
    many = spread(pack)
    for part, got in zip(attn_sums, gots):
        part.got = got
        part.add()
        part.move()
    many, *gots = lax.optimization_barrier((many, *[part.got for part in attn_sums]))
    both = swap_side(many)
    for part, got in zip(attn_sums, gots):
        part.got = got
        part.add()
        part.move()
    for part in mlp_sums:
        part.add()
    down_mine, up_mine = mlp_sums[0].finish(), mlp_sums[1].finish().astype(BF)
    both, down_mine, up_mine, *gots = lax.optimization_barrier((both, down_mine, up_mine, *[part.got for part in attn_sums]))
    for part, got in zip(attn_sums, gots):
        part.got = got
    both = jnp.stack([many, both])
    packs = jnp.stack([both, swap_core(both)]).reshape(-1, width)
    g_mod_weight, sums = modulation_grads(flags, long_rows, packs, row_out, "modulation_grads")
    for part in attn_sums:
        part.add()
    attn_mine = [part.finish() for part in attn_sums]
    attn_rows = width // n_blk
    head = proj_part.shape[1] // n_blk
    proj_mine = jnp.concatenate(
        [attn_mine[1][attn_rows + k * head : attn_rows + (k + 1) * head] for k in range(width // (quarter - split))], axis=1
    )
    attn_mine = [part[:attn_rows].astype(BF) for part in attn_mine]

    quarters = jnp.concatenate([up_mine] + attn_mine, axis=1)
    quarters = lax.all_to_all(quarters.reshape(n_uly, row_out, -1), "uly", 0, 0, tiled=True)
    ff = up_weight.shape[1]

    g = ff // (n_blk * n_uly)

    def down_home(index):
        b, u = divmod(index, n_uly)
        start = ((b * g // LANES) * n_uly + u) * LANES + (b * g) % LANES
        return start // g

    down_map = [(i, down_home(i)) for i in range(n_blk * n_uly)]
    g_down_weight = down_mine.astype(F32)
    if any(a != b for a, b in down_map):
        g_down_weight = lax.ppermute(g_down_weight, ("blk", "uly"), down_map)
    proj_map = [(b * n_uly + u, u * n_blk + b) for b in range(n_blk) for u in range(n_uly)]
    g_proj_weight = lax.ppermute(proj_mine.astype(F32), ("blk", "uly"), proj_map)


    def cut(vector, size):
        return lax.dynamic_slice_in_dim(vector, dev * size, size, 0)

    total_dev = n_blk * n_uly
    whole_sum = jnp.sum(sums, axis=0)
    mod_line = jnp.concatenate([whole_sum[14:16] + whole_sum[18:20], whole_sum[16:18] + whole_sum[20:22], whole_sum[0:8]], axis=0)
    g_mod_bias = cut(mod_line.reshape(6, 2, width).sum(axis=1).reshape(-1), 6 * width // total_dev)
    g_down_bias = cut(whole_sum[10], width // total_dev)
    g_proj_bias = cut(whole_sum[11], width // total_dev)
    first = dev * g
    steps = (first // LANES) % n_uly ^ uly
    core_step, side_step = steps % 2, steps // 2
    up_mine_sum = sums[2 * core_step + side_step, 12] + sums[2 * (1 - core_step) + side_step, 13]
    g_up_bias = lax.dynamic_slice_in_dim(up_mine_sum, first // (LANES * n_uly) * LANES + first % LANES, g, 0)
    by_step = (sums[0:2, 22:24] + sums[2:4, 22:24]).reshape(2, 2 * width)[:, : 3 * width // 2]
    by_side = jnp.where(side == 0, by_step, by_step[::-1])
    g_attn_bias = cut(jnp.swapaxes(by_side.reshape(2, 3, width // 2), 0, 1).reshape(-1), 3 * width // total_dev)
    quarters, g_mod_bias, g_down_bias, g_proj_bias, g_up_bias, g_attn_bias, g_down_weight = lax.optimization_barrier(
        (quarters, g_mod_bias, g_down_bias, g_proj_bias, g_up_bias, g_attn_bias, g_down_weight)
    )
    g_up_weight, g_attn_weight = lay_out_rows(flags, quarters, ff // n_uly, ff, "lay_out_rows")
    return (
        output, token_grad, g_mod_weight, g_mod_bias, g_attn_weight, g_attn_bias,
        g_proj_weight, g_proj_bias, g_up_weight, g_up_bias, g_down_weight, g_down_bias,
    )


def solution(mesh):
    row = P(("blk", "uly"), None)
    flat = P(("blk", "uly"))
    in_specs = (row, row, row) + (P(),) * 12
    out_specs = (row, row, row, flat, row, flat, row, flat, row, flat, row, flat)
    return jax.shard_map(on_device, mesh=mesh, in_specs=in_specs, out_specs=out_specs, check_vma=False)
```

```python
import functools
import math

import jax
import jax.numpy as jnp
import numpy as np
from jax import lax
from jax.experimental import pallas as pl
from jax.experimental.pallas import tpu as pltpu
from jax.sharding import PartitionSpec as P

DH = 64
GRID = 10
FB = 8
PATCH = 100
HALF = 64
LANES = 128

GELU_C = 0.7978845608028654
GELU_K = 0.044715
NEG_BIG = -1e30
MIB = 1 << 20
UNROLL = 8
PACK = 24

BF = jnp.bfloat16
F32 = jnp.float32


def round_up(value, step):
    return -(-value // step) * step


def lane_low(shape):
    return lax.broadcasted_iota(jnp.int32, shape, len(shape) - 1) < HALF


def first_frame(shape):
    return lax.broadcasted_iota(jnp.int32, shape, 0) < PATCH


def swap_halves(value):
    return pltpu.roll(value, HALF, 1)


def swap_pairs(value):
    even = lax.broadcasted_iota(jnp.int32, value.shape, 1) % 2 == 0
    return jnp.where(even, pltpu.roll(value, LANES - 1, 1), pltpu.roll(value, 1, 1))


def per_frame(shape, first, second):
    return jnp.where(first_frame(shape), jnp.broadcast_to(first, shape), jnp.broadcast_to(second, shape))


def frame_sums(value):
    head = first_frame(value.shape)
    one = jnp.sum(jnp.where(head, value, 0.0), axis=0, keepdims=True)
    two = jnp.sum(jnp.where(head, 0.0, value), axis=0, keepdims=True)
    return one, two


def norm_rows(values):
    center = values - jnp.mean(values, axis=-1, keepdims=True)
    inv_std = lax.rsqrt(jnp.mean(center * center, axis=-1, keepdims=True) + 1e-06)
    return center * inv_std, inv_std


def norm_back(grad, normed, inv_std):
    return inv_std * (
        grad
        - jnp.mean(grad, axis=-1, keepdims=True)
        - normed * jnp.mean(grad * normed, axis=-1, keepdims=True)
    )


def dot(left, right):
    return jnp.dot(left, right, preferred_element_type=F32)


def dot_lanes(left, right):
    return lax.dot_general(left, right, (((1,), (1,)), ((), ())), preferred_element_type=F32)


def dot_rows(left, right):
    return lax.dot_general(left, right, (((0,), (0,)), ((), ())), preferred_element_type=F32)


def split_pair(value, rows_top):
    rows = value.shape[0]
    top = value[:rows_top]
    bottom = jnp.concatenate(
        [value[rows_top:], jnp.zeros((2 * rows_top - rows, LANES), value.dtype)], axis=0
    )
    low = lane_low(top.shape)
    return jnp.where(low, top, swap_halves(bottom)), jnp.where(low, swap_halves(top), bottom)


def join_pair(one, two, rows):
    rows_top = one.shape[0]
    low = lane_low(one.shape)
    top = jnp.where(low, one, swap_halves(two))
    bottom = jnp.where(low, swap_halves(one), two)
    return jnp.concatenate([top, bottom[: rows - rows_top]], axis=0)


def smem():
    return pl.BlockSpec(memory_space=pltpu.SMEM)


def whole(shape):
    return pl.BlockSpec(shape, lambda *_: (0,) * len(shape))


def kernel_call(body, flags, args, outs, *, specs=None, out_specs=None, grid=(1,), scratch=(), vmem=16, pins=(), out_pins=(), aliases=None, flops, name):
    specs = specs or [None] * len(args)
    out_specs = out_specs or [None] * len(outs)
    return pl.pallas_call(
        body,
        grid_spec=pltpu.PrefetchScalarGridSpec(
            num_scalar_prefetch=1,
            grid=grid,
            in_specs=[spec or whole(a.shape) for spec, a in zip(specs, args)],
            out_specs=[spec or whole(o.shape) for spec, o in zip(out_specs, outs)],
            scratch_shapes=list(scratch),
        ),
        out_shape=[pltpu.HBM(o.shape, o.dtype) if k in out_pins else o for k, o in enumerate(outs)],
        input_output_aliases=aliases or {},
        compiler_params=pltpu.CompilerParams(vmem_limit_bytes=vmem * MIB),
        cost_estimate=pl.CostEstimate(flops=flops // 4096, bytes_accessed=4096, transcendentals=0),
        name=name,
    )(flags, *[pltpu.with_memory_space_constraint(a, pltpu.HBM) if a.size >= MIB or k in pins else a for k, a in enumerate(args)])


def shape_of(dims, dtype):
    return jax.ShapeDtypeStruct(dims, dtype)


def tokens_to_qkv(flags, tok_own, tok_oth, mods, weight, bias, tab_cos, tab_sin, time_cos, time_sin, lay):
    rows, width = tok_own.shape
    cols = lay.heads * DH

    def body(flag_ref, own_ref, oth_ref, mod_ref, w_ref, b_ref, tc_ref, ts_ref, qc_ref, qs_ref, hid_ref, long_ref, short_ref, both_ref):
        step = pl.program_id(0)
        own_long = flag_ref[0]

        @pl.when(step == 0)
        def _():
            hidden = []
            for src, base in ((own_ref, 0), (oth_ref, 2)):
                normed, _ = norm_rows(src[...].astype(F32))
                shift = per_frame(normed.shape, mod_ref[base : base + 1, :width], mod_ref[base + 1 : base + 2, :width])
                scale = per_frame(
                    normed.shape, mod_ref[base : base + 1, width : 2 * width], mod_ref[base + 1 : base + 2, width : 2 * width]
                )
                hidden.append(normed * (1.0 + scale) + shift)
            swapped = own_long == 0
            first = jnp.where(swapped, hidden[1], hidden[0])
            second = jnp.where(swapped, hidden[0], hidden[1])
            hid_ref[0] = first.astype(BF)
            hid_ref[1] = second.astype(BF)
            both_ref[...] = jnp.concatenate([first, second], axis=0).astype(BF)

        result = dot(both_ref[...], w_ref[...]) + b_ref[...]
        for slot, out_ref in ((0, long_ref), (1, short_ref)):
            acc = result[slot * rows : (slot + 1) * rows]

            def rotated(pair):
                value = acc[:, pair * LANES : (pair + 1) * LANES]
                cosine = tc_ref[...] + per_frame(value.shape, qc_ref[2 * slot : 2 * slot + 1], qc_ref[2 * slot + 1 : 2 * slot + 2])
                sine = ts_ref[...] + per_frame(value.shape, qs_ref[2 * slot : 2 * slot + 1], qs_ref[2 * slot + 1 : 2 * slot + 2])
                return value * cosine + swap_pairs(value) * sine

            @pl.when(step == 0)
            def _():
                for pair in range(cols // LANES):
                    turned = rotated(pair)
                    out_ref[2 * pair, :rows, :HALF] = turned[:, :HALF].astype(BF)
                    out_ref[2 * pair + 1, :rows, :HALF] = swap_halves(turned)[:, :HALF].astype(BF)

            @pl.when(step == 1)
            def _():
                for pair in range(cols // LANES):
                    turned = rotated(pair)
                    out_ref[2 * pair, :rows, HALF:] = swap_halves(turned)[:, HALF:].astype(BF)
                    out_ref[2 * pair + 1, :rows, HALF:] = turned[:, HALF:].astype(BF)

            @pl.when(step == 2)
            def _():
                for pair in range(cols // LANES):
                    one, two = split_pair(acc[:, pair * LANES : (pair + 1) * LANES], lay.top)
                    out_ref[2 * pair, lay.vrow :, :] = one.astype(BF)
                    out_ref[2 * pair + 1, lay.vrow :, :] = two.astype(BF)

    packed = (lay.heads, lay.vrow + lay.top, LANES)
    return kernel_call(
        body,
        flags,
        [tok_own, tok_oth, mods, weight, bias, tab_cos, tab_sin, time_cos, time_sin],
        [shape_of((2, rows, width), BF), shape_of(packed, BF), shape_of(packed, BF)],
        specs=[
            None, None, None,
            pl.BlockSpec((width, cols), lambda j, f: (0, 2 * j + f[1])),
            pl.BlockSpec((1, cols), lambda j, f: (0, 2 * j + f[1])),
            None, None, None, None,
        ],
        scratch=[pltpu.VMEM((2 * rows, width), BF)],
        out_pins=(0,),
        grid=(3,),
        flops=12 * rows * width * cols,
        name="tokens_to_qkv",
    )


def unpack_values(ref, at, lay):
    part = ref[at, lay.vrow :, :].astype(F32)
    return jnp.concatenate([part, swap_halves(part)[: lay.rows - lay.top]], axis=0)


def hundreds(value):
    return (value * 1311) >> 17


def diag_mask(keys, queries, core):
    key = hundreds(lax.broadcasted_iota(jnp.int32, (keys, 1), 0)) ^ (2 * core)
    query = hundreds(lax.broadcasted_iota(jnp.int32, (1, queries), 1))
    query = ((query & 2) << 1) + (query & 1) + 2 * core
    return key <= query


def load_keys(own_ref, oth_ref, group, lay):
    low = lane_low((lay.rows, LANES))
    halves = [
        jnp.where(low, unpack_values(ref, group, lay), ref[group, : lay.rows, :].astype(F32))
        for ref in (own_ref, oth_ref)
    ]
    return jnp.concatenate(halves, axis=0)


def load_query(own_ref, at, lay):
    value = swap_halves(own_ref[at, : lay.rows, :].astype(F32)) * (1.0 / math.sqrt(DH))
    return jnp.where(lane_low(value.shape), 0.0, value)


def load_rows(load, groups):
    return jnp.concatenate([load(g) for g in groups], axis=0)


def fold_rows(value, op):
    return op(value.reshape(value.shape[0] // 8, 8, value.shape[1]), axis=0)


def unpack_rows(ref, at, lay):
    packed = ref[at].astype(F32)
    grad = jnp.concatenate([packed, swap_halves(packed)[: lay.rows - lay.top]], axis=0)
    return jnp.where(lane_low(grad.shape), grad, 0.0)


def attend(flags, own, oth, lay, long_clip):
    groups = own.shape[0]
    parts = lay.parts if long_clip else 1
    per = 2 if long_clip else 1
    count = groups // per
    keys, queries = 2 * lay.rows * per, lay.rows * per
    depth = count if long_clip else UNROLL

    def body(flag_ref, own_ref, oth_ref, o_ref, ot_ref, lse_ref, kv_ref, vt_ref, st_ref):
        core = flag_ref[2]
        part = flag_ref[3]

        def prepare(tile, slot):
            rows = jnp.concatenate([load_keys(own_ref, oth_ref, per * tile + k, lay) for k in range(per)], axis=0)
            kv_ref[slot] = rows.astype(BF)
            vt_ref[slot] = rows.T[:HALF].astype(BF)

        def block(at, slot):
            query = load_rows(lambda g: load_query(own_ref, g, lay), [per * at + k for k in range(per)]).astype(BF)

            def scores(kt, top):
                score = dot_lanes(kv_ref[kt], query)
                st_ref[kt] = score
                return jnp.maximum(top, fold_rows(score, jnp.max))

            top = jnp.full((8, queries), NEG_BIG, F32)
            if long_clip:
                top = lax.fori_loop(0, at, scores, top)
            score = dot_lanes(kv_ref[slot], query)
            score = jnp.where(diag_mask(keys, queries, core), score, NEG_BIG)
            st_ref[slot] = score
            top = jnp.max(jnp.maximum(top, fold_rows(score, jnp.max)), axis=0, keepdims=True)

            def mix(kt, carry):
                total, acc = carry
                expo = jnp.exp(st_ref[kt] - top)
                total = total + fold_rows(expo, jnp.sum)
                return total, acc + dot(vt_ref[kt], expo.astype(BF))

            zero = (jnp.zeros((8, queries), F32), jnp.zeros((HALF, queries), F32))
            if long_clip:
                total, acc = lax.fori_loop(0, at + 1, mix, zero)
            else:
                total, acc = mix(slot, zero)
            total = jnp.sum(total, axis=0, keepdims=True)
            acc = acc / total
            ot_ref[at] = acc
            lse_ref[at] = jnp.broadcast_to(top + jnp.log(total), (8, queries))
            out = jnp.concatenate([acc, jnp.zeros_like(acc)], axis=0).T
            for k in range(per):
                o_ref[per * at + k] = split_pair(out[k * lay.rows : (k + 1) * lay.rows], lay.top)[0].astype(BF)

        if long_clip:
            def prepare_loop(tile, _):
                prepare(tile, tile)
                return 0

            lax.fori_loop(0, count, prepare_loop, 0)
            if parts > 1:
                o_ref[...] = jnp.zeros_like(o_ref)

            def block_loop(step, _):
                at = step * parts + part if parts > 1 else step
                block(at, at)
                return 0

            lax.fori_loop(0, count // parts, block_loop, 0)
        else:
            def head_loop(step, _):
                for k in range(UNROLL):
                    prepare(UNROLL * step + k, k)
                for k in range(UNROLL):
                    block(UNROLL * step + k, k)
                return 0

            lax.fori_loop(0, count // UNROLL, head_loop, 0)

    pairs = count * (count + 1) // 2 if long_clip else count
    return kernel_call(
        body,
        flags,
        [own, oth],
        [
            shape_of((groups, lay.top, LANES), BF),
            shape_of((count, HALF, queries), F32),
            shape_of((count, 8, queries), F32),
        ],
        scratch=[
            pltpu.VMEM((depth, keys, LANES), BF),
            pltpu.VMEM((depth, HALF, keys), BF),
            pltpu.VMEM((depth, keys, queries), F32),
        ],
        out_pins=(1, 2),
        vmem=max(24, 3 * groups) if long_clip else 16,
        flops=pairs * 16 * keys * queries * DH // parts,
        name="attend_long" if long_clip else "attend_short",
    )


def attend_back(flags, own, oth, d_outs, ot, lse, tab_cos, tab_sin, time_cos, time_sin, lay, long_clip):
    groups = own.shape[0]
    parts = lay.parts if long_clip else 1
    per = 2 if long_clip else 1
    count = groups // per
    keys, queries = 2 * lay.rows * per, lay.rows * per
    depth = count if long_clip else UNROLL

    def body(flag_ref, own_ref, oth_ref, *refs):
        do_refs, refs = refs[: len(d_outs)], refs[len(d_outs) :]
        ot_ref, lse_ref, tc_ref, ts_ref, qc_ref, qs_ref, dq_ref, down_ref, doth_ref, kv_ref, kt_ref, acc_ref = refs
        own_long = flag_ref[0]
        core = flag_ref[2]
        part = flag_ref[3]

        def prepare(tile, slot):
            rows = jnp.concatenate([load_keys(own_ref, oth_ref, per * tile + k, lay) for k in range(per)], axis=0)
            kv_ref[slot] = rows.astype(BF)
            kt_ref[slot] = rows.T[HALF:].astype(BF)
            if long_clip:
                acc_ref[slot] = jnp.zeros((keys, LANES), F32)

        def block(at, slot):
            members = [per * at + k for k in range(per)]
            query = load_rows(lambda g: load_query(own_ref, g, lay), members).astype(BF)
            if long_clip:
                grad = load_rows(lambda g: unpack_rows(do_refs[0], g, lay), members)
            else:
                grad = load_rows(
                    lambda g: jnp.where(own_long == 1, unpack_rows(do_refs[1], g, lay), unpack_rows(do_refs[0], g, lay)), members
                )
            delta = jnp.sum(grad.T[:HALF] * ot_ref[at], axis=0, keepdims=True)
            grad = grad.astype(BF)
            lse_row = lse_ref[at][0:1]

            def tile_back(kt, acc, diag):
                tile = kv_ref[kt]
                prob = jnp.exp(dot_lanes(tile, query) - lse_row)
                if diag:
                    prob = jnp.where(diag_mask(keys, queries, core), prob, 0.0)
                score_grad = (prob * (dot_lanes(tile, grad) - delta)).astype(BF)
                both = dot(score_grad, query) + dot(prob.astype(BF), grad)
                if long_clip:
                    acc_ref[kt] += both
                else:
                    acc_ref[kt] = both
                return acc + dot(kt_ref[kt], score_grad)

            acc = tile_back(slot, jnp.zeros((HALF, queries), F32), True)
            if long_clip:
                acc = lax.fori_loop(0, at, lambda kt, a: tile_back(kt, a, False), acc)
            acc = acc * (1.0 / math.sqrt(DH))
            turned = jnp.concatenate([acc, jnp.zeros_like(acc)], axis=0).T
            for k, group in enumerate(members):
                dq = turned[k * lay.rows : (k + 1) * lay.rows]
                tab = group if long_clip else 0
                cosine = tc_ref[...] + per_frame(dq.shape, qc_ref[2 * tab], qc_ref[2 * tab + 1])
                sine = ts_ref[...] + per_frame(dq.shape, qs_ref[2 * tab], qs_ref[2 * tab + 1])
                dq_ref[group] = (dq * cosine - swap_pairs(dq) * sine).astype(BF)

        def flush(tile, slot):
            for k in range(per):
                down_ref[per * tile + k] = acc_ref[slot, 2 * k * lay.rows : (2 * k + 1) * lay.rows]
                doth_ref[per * tile + k] = acc_ref[slot, (2 * k + 1) * lay.rows : (2 * k + 2) * lay.rows].astype(BF)

        if long_clip:
            def prepare_loop(tile, _):
                prepare(tile, tile)
                return 0

            lax.fori_loop(0, count, prepare_loop, 0)
            if parts > 1:
                dq_ref[...] = jnp.zeros_like(dq_ref)

            def block_loop(step, _):
                at = step * parts + part if parts > 1 else step
                block(at, at)
                return 0

            lax.fori_loop(0, count // parts, block_loop, 0)

            def flush_loop(tile, _):
                flush(tile, tile)
                return 0

            lax.fori_loop(0, count, flush_loop, 0)
        else:
            def head_loop(step, _):
                for k in range(UNROLL):
                    prepare(UNROLL * step + k, k)
                for k in range(UNROLL):
                    block(UNROLL * step + k, k)
                for k in range(UNROLL):
                    flush(UNROLL * step + k, k)
                return 0

            lax.fori_loop(0, count // UNROLL, head_loop, 0)

    pairs = count * (count + 1) // 2 if long_clip else count
    return kernel_call(
        body,
        flags,
        [own, oth, *d_outs, ot, lse, tab_cos, tab_sin, time_cos, time_sin],
        [
            shape_of((groups, lay.rows, LANES), BF),
            shape_of((groups, lay.rows, LANES), F32),
            shape_of((groups, lay.rows, LANES), BF),
        ],
        scratch=[
            pltpu.VMEM((depth, keys, LANES), BF),
            pltpu.VMEM((depth, HALF, keys), BF),
            pltpu.VMEM((depth, keys, LANES), F32),
        ],
        out_pins=(0, 1),
        vmem=max(24, 3 * groups) if long_clip else 20,
        pins=(0, 1) + tuple(range(2 + len(d_outs), 8 + len(d_outs))),
        flops=pairs * 40 * keys * queries * DH // parts,
        name="attend_back_long" if long_clip else "attend_back_short",
    )


def finish_keys(flags, dq, mine, theirs, tab_cos, tab_sin, time_cos, time_sin, lay, long_clip):
    groups = dq.shape[0]

    def body(flag_ref, dq_ref, a_ref, b_ref, tc_ref, ts_ref, qc_ref, qs_ref, out_ref):
        def one(group, _):
            both = a_ref[group] + b_ref[group].astype(F32)
            tab = group if long_clip else 0
            cosine = tc_ref[...] + per_frame(both.shape, qc_ref[2 * tab], qc_ref[2 * tab + 1])
            sine = ts_ref[...] + per_frame(both.shape, qs_ref[2 * tab], qs_ref[2 * tab + 1])
            keys = both * cosine - swap_pairs(both) * sine
            out_ref[group, : lay.rows, :] = jnp.where(lane_low(keys.shape), dq_ref[group].astype(F32), keys).astype(BF)
            out_ref[group, lay.vrow :, :] = split_pair(both, lay.top)[0].astype(BF)
            return 0

        lax.fori_loop(0, groups, one, 0)

    return kernel_call(
        body,
        flags,
        [dq, mine, theirs, tab_cos, tab_sin, time_cos, time_sin],
        [shape_of((groups, lay.vrow + lay.top, LANES), BF)],
        pins=(0, 1),
        vmem=max(16, groups),
        flops=groups * lay.rows * LANES * 10,
        name="finish_keys",
    )[0]


def project_and_norm(flags, long_out, short_out, recv, weight, bias, tokens, mods, lay):
    rows, width = tokens.shape
    half = lay.heads * DH

    def body(flag_ref, long_ref, short_ref, recv_ref, w_ref, b_ref, tok_ref, mod_ref, branch_ref, resid_ref, hid_ref, att_ref):
        own_long = flag_ref[0]
        side = flag_ref[1]
        for pair in range(lay.heads // 2):
            kept = [
                jnp.where(own_long == 1, long_ref[2 * pair + k].astype(F32), short_ref[2 * pair + k].astype(F32)) for k in (0, 1)
            ]
            got = [recv_ref[2 * pair + k].astype(F32) for k in (0, 1)]
            lanes = slice(pair * LANES, (pair + 1) * LANES)
            att_ref[side, :, lanes] = join_pair(kept[0], kept[1], rows).astype(BF)
            att_ref[1 - side, :, lanes] = join_pair(got[0], got[1], rows).astype(BF)
        branch = dot(att_ref[0], w_ref[:half]) + dot(att_ref[1], w_ref[half:]) + b_ref[...]
        branch_ref[...] = branch
        gate = per_frame(branch.shape, mod_ref[0:1], mod_ref[1:2])
        resid = tok_ref[...].astype(F32) + gate * branch
        resid_ref[...] = resid
        normed, _ = norm_rows(resid)
        shift = per_frame(branch.shape, mod_ref[2:3], mod_ref[3:4])
        scale = per_frame(branch.shape, mod_ref[4:5], mod_ref[5:6])
        hid_ref[...] = (normed * (1.0 + scale) + shift).astype(BF)

    full = shape_of((rows, width), F32)
    return kernel_call(
        body,
        flags,
        [long_out, short_out, recv, weight, bias, tokens, mods],
        [full, full, shape_of((rows, width), BF)],
        scratch=[pltpu.VMEM((2, rows, half), BF)],
        out_pins=(0, 1),
        vmem=24,
        flops=2 * rows * width * width,
        name="project_and_norm",
    )


def hidden_blocks(width, wide, chunks, weight_rows):
    def pick(k):
        def at(i, f):
            block = 2 * (chunks * i + k) + f[1]
            return (block, 0) if weight_rows else (0, block)
        return at

    return [pl.BlockSpec((wide, width) if weight_rows else (width, wide), pick(k)) for k in range(chunks)]


def ahead_grads(flags, mlp_grad, down_weight, name):
    rows, width = mlp_grad.shape
    ff = down_weight.shape[0]
    wide, chunks = 2 * LANES, 2

    def body(flag_ref, mg_ref, *refs):
        out_ref = refs[-1]
        for k in range(chunks):
            out_ref[:, k * wide : (k + 1) * wide] = dot_lanes(mg_ref[...], refs[k][...])

    return kernel_call(
        body,
        flags,
        [mlp_grad] + [down_weight] * chunks,
        [shape_of((rows, ff // 2), F32)],
        specs=[None] + hidden_blocks(width, wide, chunks, True),
        out_specs=[pl.BlockSpec((rows, chunks * wide), lambda i, f: (0, i))],
        out_pins=(0,),
        grid=(ff // (2 * wide * chunks),),
        flops=rows * width * ff,
        name=name,
    )[0]


def hidden_grads(flags, hidden, ahead, up_weight, up_bias, lay, out_dtype, name):
    rows, width = hidden.shape
    ff = up_weight.shape[1]
    wide, chunks = 2 * LANES, 2
    steps = ff // (2 * wide * chunks)
    quarter = ff // 4

    def body(flag_ref, hid_ref, ahead_ref, *refs):
        weights, outs = refs[: 2 * chunks], refs[2 * chunks :]
        mine_ref, send_ref, bm_ref, bt_ref, hg_ref, hacc = outs
        step = pl.program_id(0)
        first = flag_ref[2] == 0
        back = 0.0
        for k in range(chunks):
            up_ref, ub_ref = weights[k], weights[chunks + k]
            pre = dot(hid_ref[...], up_ref[...]) + ub_ref[...]
            tanh = jnp.tanh(GELU_C * (pre + GELU_K * pre * pre * pre))
            act = (0.5 * pre * (1.0 + tanh)).astype(BF)
            slope = 0.5 * (1.0 + tanh) + 0.5 * pre * (1.0 - tanh * tanh) * GELU_C * (1.0 + 3.0 * GELU_K * pre * pre)
            pre_low = (ahead_ref[:, k * wide : (k + 1) * wide] * slope).astype(BF)
            back = back + dot_lanes(pre_low, up_ref[...])
            sums = jnp.sum(pre_low.astype(F32), axis=0, keepdims=True)
            lanes = slice(k * LANES, (k + 1) * LANES)
            for at, value in ((0, act), (1, pre_low)):
                mine_ref[at, :, lanes] = jnp.where(first, value[:, :LANES], value[:, LANES:])
                send_ref[at, :, lanes] = jnp.where(first, value[:, LANES:], value[:, :LANES])
            bm_ref[:, lanes] = jnp.broadcast_to(jnp.where(first, sums[:, :LANES], sums[:, LANES:]), (8, LANES))
            bt_ref[:, lanes] = jnp.broadcast_to(jnp.where(first, sums[:, LANES:], sums[:, :LANES]), (8, LANES))

        @pl.when(step == 0)
        def _():
            hacc[...] = back

        @pl.when(step > 0)
        def _():
            hacc[...] += back

        @pl.when(step == steps - 1)
        def _():
            hg_ref[...] = hacc[...].astype(hg_ref.dtype)

    chunk = pl.BlockSpec((2, rows, chunks * LANES), lambda i, f: (0, 0, i))
    bchunk = pl.BlockSpec((8, chunks * LANES), lambda i, f: (0, i))
    return kernel_call(
        body,
        flags,
        [hidden, ahead] + [up_weight] * chunks + [up_bias] * chunks,
        [shape_of((2, rows, quarter), BF)] * 2 + [shape_of((8, quarter), F32)] * 2 + [shape_of((rows, width), out_dtype)],
        specs=[None, pl.BlockSpec((rows, chunks * wide), lambda i, f: (0, i))]
        + hidden_blocks(width, wide, chunks, False)
        + hidden_blocks(1, wide, chunks, False),
        out_specs=[chunk, chunk, bchunk, bchunk, None],
        grid=(steps,),
        scratch=[pltpu.VMEM((rows, width), F32)],
        pins=(1,),
        flops=2 * rows * width * ff,
        name=name,
    )


def forward_rows(flags, mine, send, mine2, send2, down_weight):
    _, rows, quarter = mine.shape
    ff, width = down_weight.shape
    wide, chunks = 2 * LANES, 2
    steps = ff // (2 * wide * chunks)

    def body(flag_ref, m_ref, s_ref, m2_ref, s2_ref, *refs):
        own_ref, oth_ref, acc_ref = refs[chunks:]
        first = flag_ref[2] == 0
        step = pl.program_id(0)
        for at, (a_ref, b_ref) in enumerate(((m_ref, s_ref), (m2_ref, s2_ref))):
            total = 0.0
            for k in range(chunks):
                lanes = slice(k * LANES, (k + 1) * LANES)
                a, b = a_ref[:, lanes], b_ref[:, lanes]
                act = jnp.concatenate([jnp.where(first, a, b), jnp.where(first, b, a)], axis=1)
                total = total + dot(act, refs[k][...])

            @pl.when(step == 0)
            def _(total=total, at=at):
                acc_ref[at] = total

            @pl.when(step > 0)
            def _(total=total, at=at):
                acc_ref[at] += total

        @pl.when(step == steps - 1)
        def _():
            own_ref[...] = acc_ref[0]
            oth_ref[...] = acc_ref[1].astype(BF)

    chunk = pl.BlockSpec((None, rows, chunks * LANES), lambda i, f: (0, 0, i))
    return kernel_call(
        body,
        flags,
        [mine, send, mine2, send2] + [down_weight] * chunks,
        [shape_of((rows, width), F32), shape_of((rows, width), BF)],
        specs=[chunk] * 4 + hidden_blocks(width, wide, chunks, True),
        scratch=[pltpu.VMEM((2, rows, width), F32)],
        out_pins=(0,),
        grid=(steps,),
        flops=2 * rows * width * ff,
        name="forward_rows",
    )


def scale_cotangent(flags, cotangent, gates):
    rows, width = cotangent.shape

    def body(flag_ref, dy_ref, g_ref, out_ref, sums_ref):
        low = (per_frame((rows, width), g_ref[0:1], g_ref[1:2]) * dy_ref[...].astype(F32)).astype(BF)
        out_ref[...] = low
        sums_ref[...] = jnp.broadcast_to(jnp.sum(low.astype(F32), axis=0, keepdims=True), sums_ref.shape)

    return kernel_call(
        body,
        flags,
        [cotangent, gates],
        [shape_of((rows, width), BF), shape_of((8, width), F32)],
        pins=(0,),
        flops=rows * width,
        name="scale_cotangent",
    )


def layer_output(flags, mlp_own, mlp_recv, bias, resid, cotangent, gates):
    rows, width = resid.shape

    def body(flag_ref, a_ref, b_ref, bias_ref, r_ref, dy_ref, g_ref, out_ref, sums_ref):
        mlp = a_ref[...] + b_ref[...].astype(F32) + bias_ref[...]
        out_ref[...] = (r_ref[...] + per_frame((rows, width), g_ref[0:1], g_ref[1:2]) * mlp).astype(BF)
        sums_ref[0:1], sums_ref[1:2] = frame_sums(dy_ref[...].astype(F32) * mlp)
        sums_ref[2:8] = jnp.zeros((6, width), F32)

    return kernel_call(
        body,
        flags,
        [mlp_own, mlp_recv, bias, resid, cotangent, gates],
        [shape_of((rows, width), BF), shape_of((8, width), F32)],
        pins=(0, 3, 4),
        flops=rows * width * 4,
        name="layer_output",
    )


def pack_rows(flags, n_blk, mid, gate2, silu, down_b, up_sums, sum_long, sum_short, bias_long, bias_short):
    width = mid.shape[1]
    cols = bias_long.shape[1]

    def body(flag_ref, mid_ref, g_ref, s_ref, d_ref, m1, m2, t1, t2, sl, ss, bl, bs, out_ref):
        bias = bl[0:1] + bs[0:1]
        bias = jnp.concatenate([bias, jnp.zeros((1, 2 * width - cols), F32)], axis=1)
        rows = jnp.concatenate(
            [mid_ref[0:6], g_ref[0:2], s_ref[...].astype(F32), d_ref[0:1], mid_ref[6:7], m1[0:1] + m2[0:1], t1[0:1] + t2[0:1],
             sl[0:4], ss[0:4], bias[:, :width], bias[:, width:]],
            axis=0,
        ).astype(BF)
        for k in range(n_blk):
            out_ref[k] = rows

    return kernel_call(
        body,
        flags,
        [mid, gate2, silu, down_b, *up_sums, sum_long, sum_short, bias_long, bias_short],
        [shape_of((n_blk, PACK, width), BF)],
        flops=width * PACK,
        name="pack_rows",
    )[0]


def branch_back(flags, hid_own, hid_recv, cotangent, resid, branch, mods, weight, lay):
    rows, width = resid.shape
    half = lay.heads * DH

    def body(flag_ref, a_ref, b_ref, dy_ref, r_ref, br_ref, mod_ref, w_ref, rg_ref, bg_ref, keep_ref, send_ref, sums_ref):
        side = flag_ref[1]
        hid = a_ref[...] + b_ref[...].astype(F32)
        norm, inv_std = norm_rows(r_ref[...])
        scale = per_frame(hid.shape, mod_ref[4:5], mod_ref[5:6])
        resid = dy_ref[...].astype(F32) + norm_back(hid * (1.0 + scale), norm, inv_std)
        rg_ref[...] = resid
        gate = per_frame(hid.shape, mod_ref[0:1], mod_ref[1:2])
        low = (gate * resid).astype(BF)
        bg_ref[...] = low
        for out_ref, which in ((keep_ref, side), (send_ref, 1 - side)):
            grad = dot_lanes(low, w_ref[pl.ds(pl.multiple_of(which * half, half), half), :])
            for pair in range(lay.heads // 2):
                one, two = split_pair(grad[:, pair * LANES : (pair + 1) * LANES], lay.top)
                out_ref[2 * pair] = one.astype(BF)
                out_ref[2 * pair + 1] = two.astype(BF)
        sums_ref[0:1], sums_ref[1:2] = frame_sums(resid * br_ref[...])
        sums_ref[2:3], sums_ref[3:4] = frame_sums(hid)
        sums_ref[4:5], sums_ref[5:6] = frame_sums(hid * norm)
        sums_ref[6:7] = jnp.sum(low.astype(F32), axis=0, keepdims=True)
        sums_ref[7:8] = jnp.zeros((1, width), F32)

    packed = shape_of((lay.heads, lay.top, LANES), BF)
    return kernel_call(
        body,
        flags,
        [hid_own, hid_recv, cotangent, resid, branch, mods, weight],
        [shape_of((rows, width), F32), shape_of((rows, width), BF), packed, packed, shape_of((8, width), F32)],
        pins=(0, 2, 3, 4, 5),
        out_pins=(0,),
        vmem=24,
        flops=2 * rows * width * width,
        name="branch_back",
    )


def qkv_back(flags, grads, tok_own, tok_oth, weight, lay, is_long):
    rows, width = tok_own.shape
    cols = lay.heads * DH
    half = cols // 2

    def body(flag_ref, *refs):
        g_refs, refs = refs[: len(grads)], refs[len(grads) :]
        own_ref, oth_ref, w_ref, hid_ref, low_ref, gm_ref, gt_ref, bias_ref, sums_ref, q_ref, acc_ref = refs
        step = pl.program_id(0)
        core = flag_ref[2]

        @pl.when(step == 0)
        def _():
            if not is_long:
                dq_ref, a_ref, b_ref, tc_ref, ts_ref, qc_ref, qs_ref = g_refs
                table = (rows, LANES)
                cosine = tc_ref[...] + per_frame(table, qc_ref[0], qc_ref[1])
                sine = ts_ref[...] + per_frame(table, qs_ref[0], qs_ref[1])
            for pair in range(lay.heads // 2):
                lanes = slice(pair * LANES, (pair + 1) * LANES)
                low = lane_low((rows, LANES))
                if is_long:
                    g_ref = g_refs[0]
                    one, two = (g_ref[2 * pair + k, :rows, :].astype(F32) for k in (0, 1))
                    query, key = jnp.where(low, one, swap_halves(two)), jnp.where(low, swap_halves(one), two)
                    value = join_pair(*(g_ref[2 * pair + k, lay.vrow :, :].astype(F32) for k in (0, 1)), rows)
                else:
                    one, two = (dq_ref[2 * pair + k].astype(F32) for k in (0, 1))
                    query = jnp.where(low, one, swap_halves(two))
                    one, two = (a_ref[2 * pair + k] + b_ref[2 * pair + k].astype(F32) for k in (0, 1))
                    value = jnp.where(low, one, swap_halves(two))
                    one, two = (v * cosine - swap_pairs(v) * sine for v in (one, two))
                    key = jnp.where(low, swap_halves(one), two)
                q_ref[0, :, lanes] = query.astype(BF)
                q_ref[1, :, lanes] = key.astype(BF)
                q_ref[2, :, lanes] = value.astype(BF)

        value = q_ref[step]
        part = dot_lanes(value, w_ref[...])

        @pl.when(step == 0)
        def _():
            acc_ref[...] = part

        @pl.when(step > 0)
        def _():
            acc_ref[...] += part

        first = core == 0
        gm_ref[...] = jnp.where(first, value[:, :half], value[:, half:])
        gt_ref[...] = jnp.where(first, value[:, half:], value[:, :half])
        bias_ref[...] = jnp.broadcast_to(jnp.sum(value.astype(F32), axis=0, keepdims=True), bias_ref.shape)

        @pl.when(step == 2)
        def _():
            hid = acc_ref[...]
            hid_ref[...] = hid
            low_ref[...] = hid.astype(BF)
            mine = (flag_ref[0] == 1) if is_long else (flag_ref[0] == 0)
            normed, _ = norm_rows(jnp.where(mine, own_ref[...].astype(F32), oth_ref[...].astype(F32)))
            sums_ref[0:1], sums_ref[1:2] = frame_sums(hid)
            sums_ref[2:3], sums_ref[3:4] = frame_sums(hid * normed)
            sums_ref[4:8] = jnp.zeros((4, width), F32)

    return kernel_call(
        body,
        flags,
        [*grads, tok_own, tok_oth, weight],
        [
            shape_of((rows, width), F32),
            shape_of((rows, width), BF),
            shape_of((rows, 3 * half), BF),
            shape_of((rows, 3 * half), BF),
            shape_of((8, 3 * cols), F32),
            shape_of((8, width), F32),
        ],
        specs=[None] * (len(grads) + 2) + [pl.BlockSpec((width, cols), lambda j, f: (0, 2 * j + f[1]))],
        out_specs=[
            None, None,
            pl.BlockSpec((rows, half), lambda j, f: (0, j)),
            pl.BlockSpec((rows, half), lambda j, f: (0, j)),
            pl.BlockSpec((8, cols), lambda j, f: (0, j)),
            None,
        ],
        pins=(len(grads), len(grads) + 1) + (() if is_long else (0, 1)),
        out_pins=(0,),
        grid=(3,),
        scratch=[pltpu.VMEM((3, rows, cols), BF), pltpu.VMEM((rows, width), F32)],
        flops=6 * rows * width * cols,
        name="qkv_back_long" if is_long else "qkv_back_short",
    )


def token_back(flags, hid_long, hid_short, recv, tokens, resid_grad, mods, lay):
    rows, width = tokens.shape

    def body(flag_ref, l_ref, s_ref, r_ref, tok_ref, rg_ref, mod_ref, out_ref):
        hid = jnp.where(flag_ref[0] == 1, l_ref[...], s_ref[...]) + r_ref[...].astype(F32)
        normed, inv_std = norm_rows(tok_ref[...].astype(F32))
        scale = per_frame(hid.shape, mod_ref[0:1, width : 2 * width], mod_ref[1:2, width : 2 * width])
        out_ref[...] = rg_ref[...] + norm_back(hid * (1.0 + scale), normed, inv_std)

    return kernel_call(
        body,
        flags,
        [hid_long, hid_short, recv, tokens, resid_grad, mods],
        [shape_of((rows, width), F32)],
        pins=(0, 1, 3, 4, 5),
        flops=rows * width * 20,
        name="token_back",
    )[0]


def group_spec(pair, rows, wide, moves):
    index = pair[1]
    if index is None:
        return pl.BlockSpec((rows, wide), lambda i, f: (0, i if moves else 0))
    return pl.BlockSpec((None, rows, wide), lambda i, f: (index, 0, i if moves else 0))


def width_of(jobs):
    return sum(rights[0][0].shape[-1] for _, rights in jobs)


def split_weight_grads(flags, jobs, n_blk, cuts, head_rows, name):
    count = len(jobs[0][0])
    rows, depth = jobs[0][0][0][0].shape[-2:]
    pieces = [(job, *cut) for job, many in enumerate(cuts) for cut in many]
    tall = depth // n_blk
    wide = max(tall, LANES)
    per = wide // tall
    operands = [pair for lefts, rights in jobs for pair in [*lefts, *rights]]
    extra = 0
    if head_rows:
        head = head_rows[0].shape[1] // n_blk
        turns = head_rows[0].shape[2] // cuts[0][-1][1]
        extra = head * turns

    def body(flag_ref, *refs):
        outs = refs[len(operands) + len(head_rows) :]
        step = pl.program_id(0)
        results = []
        for job in range(len(jobs)):
            mine = refs[2 * count * job : 2 * count * (job + 1)]
            acc = dot_rows(mine[0][...], mine[count][...])
            for k in range(1, count):
                acc += dot_rows(mine[k][...], mine[count + k][...])
            results.append(acc.astype(BF))
        for member in range(per):
            place = relative_place(step * per + member, flag_ref[4], n_blk)
            if head_rows:
                part_ref, got_ref = refs[len(operands) : len(operands) + 2]
                at = pl.ds(pl.multiple_of((step * per + member) * head, head), head)
                both = (part_ref[flag_ref[2], at].astype(F32) + got_ref[at].astype(F32)).astype(BF)
            for out, (job, start, cols, order) in enumerate(pieces):
                sent, at = half_place(place, order)
                values = [results[job][member * tall : (member + 1) * tall, start : start + cols]]
                if head_rows and out == len(pieces) - 1:
                    values += [both[:, turn * cols : (turn + 1) * cols] for turn in range(turns)]

                def store(out_ref, values=values, at=at):
                    row = 0
                    for value in values:
                        out_ref[at, row : row + value.shape[0]] = value
                        row += value.shape[0]

                pl.when(sent == 1)(functools.partial(store, outs[2 * out]))
                pl.when(sent == 0)(functools.partial(store, outs[2 * out + 1]))

    specs = []
    for lefts, rights in jobs:
        specs += [group_spec(pair, rows, wide, True) for pair in lefts]
        specs += [group_spec(pair, rows, pair[0].shape[-1], False) for pair in rights]
    outs = []
    for out, (job, start, cols, order) in enumerate(pieces):
        outs += [shape_of((n_blk // 2, tall + (extra if out == len(pieces) - 1 else 0), cols), BF)] * 2
    return kernel_call(
        body,
        flags,
        [array for array, _ in operands] + list(head_rows),
        outs,
        specs=specs + [None] * len(head_rows),
        grid=(depth // wide,),
        vmem=24,
        pins=(0, 1, 2, 3, 5, 7) if head_rows else (),
        flops=2 * count * rows * depth * width_of(jobs),
        name=name,
    )


def head_weight_grads(flags, longs, shorts, grad_own, grad_oth, lay):
    rows, width = grad_own.shape
    pairs = lay.heads // 2

    def body(flag_ref, l_ref, s_ref, go_ref, gt_ref, out_ref):
        own_long = flag_ref[0] == 1
        grads = jnp.where(own_long, go_ref[...], gt_ref[...]), jnp.where(own_long, gt_ref[...], go_ref[...])
        for pair in range(pairs):
            acc = 0.0
            for ref, grad in zip((l_ref, s_ref), grads):
                left = join_pair(ref[2 * pair].astype(F32), ref[2 * pair + 1].astype(F32), rows).astype(BF)
                acc = acc + dot_rows(left, grad)
            out_ref[pair * LANES : (pair + 1) * LANES, :] = acc.astype(BF)

    return kernel_call(
        body,
        flags,
        [longs, shorts, grad_own, grad_oth],
        [shape_of((lay.heads * DH, width), BF)],
        pins=(0, 1),
        flops=4 * rows * width * lay.heads * DH,
        name="head_weight_grads",
    )[0]


def relative_place(target, here, n_blk):
    relative = target ^ here
    return relative ^ ((relative >> 1) & (10 & (n_blk - 1)))


def half_place(place, order):
    at = 0
    for bit in order[1:]:
        at = 2 * at + ((place >> bit) & 1)
    return (place >> order[0]) & 1, at


def hop_of(bit):
    return (1 << bit) if bit == 0 or bit % 2 == 1 else (1 << bit) | (1 << (bit - 1))


class CubeSum:
    def __init__(self, send, keep, n_blk, order):
        self.n_blk, self.order, self.at = n_blk, order, 0
        self.bits = n_blk.bit_length() - 1
        self.send, self.keep, self.value, self.got = send, keep, None, None

    def move(self, *starts):
        hop = hop_of(self.order[self.at])
        send = after(self.send, *starts) if starts else self.send
        self.got = lax.ppermute(send, "blk", [(i, i ^ hop) for i in range(self.n_blk)])

    def add(self):
        self.at += 1
        half = self.keep.shape[0] // 2
        if self.at == self.bits:
            self.value = (self.keep.astype(F32) + self.got.astype(F32))[0]
        else:
            low = [(self.keep[k].astype(F32) + self.got[k].astype(F32)).astype(BF) for k in (slice(half), slice(half, None))]
            self.keep, self.send = low

    def finish(self):
        while self.at < self.bits:
            self.move()
            self.add()
        return self.value


def lay_out_rows(flags, gathered, split, ff, name):
    n_uly, rows, total = gathered.shape
    cols = (total - split) // 3

    def body(flag_ref, in_ref, up_ref, attn_ref):
        for u in range(n_uly):
            for i in range(split // LANES):
                at = (i * n_uly + u) * LANES
                up_ref[:, at : at + LANES] = in_ref[u, :, i * LANES : (i + 1) * LANES].astype(F32)
            for j in range(3):
                at = (j * n_uly + u) * cols
                attn_ref[:, at : at + cols] = in_ref[u, :, split + j * cols : split + (j + 1) * cols].astype(F32)

    return kernel_call(
        body,
        flags,
        [gathered],
        [shape_of((rows, ff), F32), shape_of((rows, 3 * n_uly * cols), F32)],
        flops=rows * total,
        name=name,
    )


def modulation_grads(flags, long_rows, mine, got, row_out, name):
    half, width = mine.shape
    total = 2 * half
    quarter = total // 4

    def body(flag_ref, long_ref, mine_ref, got_ref, out_ref, sums_ref, part_ref, g_ref):
        g_ref[:half] = mine_ref[...]
        g_ref[half:] = got_ref[...]
        start = flag_ref[5]
        block = pl.multiple_of((start // LANES) * LANES, LANES)
        silu = g_ref[:, pl.ds(block, LANES)].astype(F32)
        parts = [silu[k * quarter : (k + 1) * quarter] for k in (1, 0, 3, 2)]
        mate = jnp.concatenate(parts, axis=0)
        own_long = long_ref[...] > 0.5

        def place_of(index):
            return index - PACK * ((index * 2731) >> 16)

        place = place_of(lax.broadcasted_iota(jnp.int32, (total, LANES), 0))

        def aligned(value, base):
            return jnp.where((place == base) | (place == base + 1), pltpu.roll(value, (base - 8) % total, 0), 0.0)

        def owner(base, is_long):
            return jnp.where(own_long == is_long, aligned(silu, base), aligned(mate, base))

        lefts = [
            owner(14, True) + owner(18, False),
            owner(16, True) + owner(20, False),
            aligned(silu, 0),
            aligned(silu, 2),
            aligned(silu, 4),
            aligned(silu, 6),
        ]
        for k, left in enumerate(lefts):
            part_ref[...] = dot_rows(left.astype(BF), g_ref[...])
            out_ref[:, k * width : (k + 1) * width] = part_ref[pl.ds(pl.multiple_of(start - block, row_out), row_out), :]
        row = lax.broadcasted_iota(jnp.int32, (32, quarter), 0)
        which = jnp.where(row == place_of(lax.broadcasted_iota(jnp.int32, (32, quarter), 1)), 1.0, 0.0).astype(BF)
        for u in range(4):
            sums_ref[u] = dot(which, g_ref[u * quarter : (u + 1) * quarter, :])

    return kernel_call(
        body,
        flags,
        [long_rows, mine, got],
        [shape_of((row_out, 6 * width), F32), shape_of((4, 32, width), F32)],
        scratch=[pltpu.VMEM((LANES, width), F32), pltpu.VMEM((total, width), BF)],
        vmem=max(20, 20 * total // 768),
        flops=total * width * LANES * 12,
        name=name,
    )


def after(value, *earlier):
    return lax.optimization_barrier((value,) + earlier)[0]


def rotary_static(frames):
    n_time, n_row = DH // 8, 3 * DH // 16
    cosine = np.zeros((frames * PATCH, LANES), np.float32)
    sine = np.zeros((frames * PATCH, LANES), np.float32)
    patch = np.arange(frames * PATCH) % PATCH
    for group, place in ((0, patch // GRID), (1, patch % GRID)):
        for j in range(n_row):
            freq = np.exp(np.float32(-math.log(10000.0)) * np.float32(j) / np.float32(n_row)).astype(np.float32)
            angle = (place.astype(np.float32) * freq).astype(np.float64)
            pair = n_time + group * n_row + j
            for head in (0, HALF):
                cosine[:, head + 2 * pair] = np.cos(angle)
                cosine[:, head + 2 * pair + 1] = np.cos(angle)
                sine[:, head + 2 * pair] = -np.sin(angle)
                sine[:, head + 2 * pair + 1] = np.sin(angle)
    return cosine, sine


def rotary_time(times):
    n_time = DH // 8
    lane = jnp.arange(LANES, dtype=jnp.int32)
    pair = (lane % HALF) // 2
    freq = jnp.exp(-math.log(10000.0) * pair.astype(F32) / float(n_time))
    angle = times.astype(F32)[:, None] * freq[None, :]
    live = (pair < n_time)[None, :]
    sign = jnp.where(lane % 2 == 0, -1.0, 1.0)[None, :]
    return jnp.where(live, jnp.cos(angle), 0.0), jnp.where(live, sign * jnp.sin(angle), 0.0)


class Layout:
    def __init__(self, rows, heads, parts):
        self.rows = rows
        self.heads = heads
        self.parts = parts
        self.top = round_up(-(-rows // 2), 16)
        self.vrow = round_up(rows, 16)


def on_device(
    tokens, cotangent, noise_embed, frame_clip, frame_index, mod_weight, mod_bias, attn_weight, attn_bias,
    proj_weight, proj_bias, up_weight, up_bias, down_weight, down_bias,
):
    n_uly = lax.axis_size("uly")
    n_blk = lax.axis_size("blk")
    blk = lax.axis_index("blk")
    uly = lax.axis_index("uly")
    rows, width = tokens.shape
    frames = noise_embed.shape[0]
    side, core = uly // 2, uly % 2
    heads = width // DH // 2
    parts = n_blk // heads
    lay = Layout(rows, heads, parts)
    dev = blk * n_uly + uly

    def swap_side(value):
        return lax.ppermute(value, "uly", [(i, i ^ 2) for i in range(n_uly)])

    def swap_core(value):
        return lax.ppermute(value, "uly", [(i, i ^ 1) for i in range(n_uly)])

    def spread(value):
        return lax.all_to_all(value, "blk", split_axis=0, concat_axis=0, tiled=True)

    long_first = frame_clip[::FB] == n_blk
    own_long_b = lax.dynamic_index_in_dim(long_first, blk, 0, False) == (side == 0)
    own_long = own_long_b.astype(jnp.int32)
    row_out = width // (n_blk * n_uly)
    flags = jnp.stack([own_long, side, core, blk // heads, blk, dev * row_out]).astype(jnp.int32)

    tok_oth = swap_side(tokens)
    silu = jax.nn.silu(noise_embed.astype(F32)).astype(BF)
    bias = mod_bias.astype(F32)
    first_mod = dot(silu, mod_weight[:, : 2 * width]) + bias[: 2 * width]
    first_mods = jnp.concatenate([first_mod, swap_side(first_mod)], axis=0)
    rest_mod = dot(after(silu, first_mod), mod_weight[:, 2 * width :]) + bias[2 * width :]

    block_time = frame_index.reshape(n_blk, FB)
    head_time, tail_time = block_time[:, : FB // 2], block_time[:, FB // 2 :]
    long_times = lax.dynamic_slice_in_dim(jnp.where(long_first[:, None], head_time, tail_time), core * frames, frames, 1)
    short_times = lax.dynamic_slice_in_dim(jnp.where(long_first[:, None], tail_time, head_time), core * frames, frames, 1)
    short_times = lax.dynamic_index_in_dim(short_times, blk, 0, False)
    time_cos, time_sin = rotary_time(jnp.concatenate([lax.dynamic_index_in_dim(long_times, blk, 0, False), short_times]))
    long_cos, long_sin = rotary_time(long_times.reshape(-1))
    short_cos, short_sin = time_cos[frames:, None], time_sin[frames:, None]
    long_cos, long_sin = long_cos[:, None], long_sin[:, None]
    tab_cos, tab_sin = (jnp.asarray(t) for t in rotary_static(frames))
    own_long_all = (long_first[None, :] == ((side ^ jnp.arange(2)) == 0)[:, None]).astype(F32)
    long_rows = jnp.broadcast_to(own_long_all[None, :, :, None, None], (2, 2, n_blk, PACK, LANES)).reshape(-1, LANES)
    first_mods, rest_mod, long_cos, long_sin, short_cos, short_sin, long_rows = lax.optimization_barrier(
        (first_mods, rest_mod, long_cos, long_sin, short_cos, short_sin, long_rows)
    )

    gate2 = rest_mod[:, 3 * width :]
    mid_mods = jnp.concatenate([rest_mod[:, :width], rest_mod[:, width : 2 * width], rest_mod[:, 2 * width : 3 * width]], axis=0)
    mid_mods = jnp.concatenate([mid_mods, jnp.zeros((2, width), F32)], axis=0)
    hidden1, qkv_long, qkv_short = tokens_to_qkv(
        flags, tokens, tok_oth, first_mods, attn_weight, attn_bias.astype(F32)[None], tab_cos, tab_sin, time_cos, time_sin, lay
    )
    sent = jnp.concatenate([qkv_long] * parts, axis=0) if parts > 1 else qkv_long
    long_own = spread(sent)
    short_oth = swap_core(qkv_short)
    out_short, ot_short, lse_short = attend(flags, qkv_short, short_oth, lay, False)
    mlp_grad, down_b = scale_cotangent(flags, after(cotangent, qkv_long), gate2)
    mlp_grad_oth = swap_side(mlp_grad)
    ahead_own = ahead_grads(flags, mlp_grad, down_weight, "ahead_own")
    long_own, out_short, mlp_grad, ahead_own = lax.optimization_barrier((long_own, out_short, mlp_grad, ahead_own))
    long_oth = swap_core(long_own)
    out_long_all, ot_long, lse_long = attend(flags, long_own, long_oth, lay, True)
    out_long_all, mlp_grad_oth = lax.optimization_barrier((out_long_all, mlp_grad_oth))

    def own_part(value):
        if parts == 1:
            return value
        return lax.dynamic_slice_in_dim(value, ((blk // 2) % parts) * heads, heads, 0)

    ahead_oth = ahead_grads(flags, mlp_grad_oth, down_weight, "ahead_other")
    out_long = own_part(spread(out_long_all))
    out_long, ahead_oth = lax.optimization_barrier((out_long, ahead_oth))
    out_recv = swap_side(jnp.where(own_long_b, out_short, out_long))
    branch, resid, hidden2 = project_and_norm(
        flags, out_long, out_short, out_recv, proj_weight, proj_bias.astype(F32)[None], tokens, mid_mods, lay
    )

    hidden2_oth = swap_side(hidden2)
    up_b = up_bias.astype(F32)[None]
    mine, send, bm, bt, hid_own = hidden_grads(flags, hidden2, ahead_own, up_weight, up_b, lay, F32, "hidden_own")
    hidden2_oth, hid_own = lax.optimization_barrier((hidden2_oth, hid_own))
    mine2, send2, bm2, bt2, hid_oth = hidden_grads(flags, hidden2_oth, ahead_oth, up_weight, up_b, lay, BF, "hidden_other")
    hid_recv = swap_side(hid_oth)

    got, got2 = swap_core(send), swap_core(send2)
    hid_c, hid_c2, mg_c, mg_c2 = (swap_core(v) for v in (hidden2, hidden2_oth, mlp_grad, mlp_grad_oth))
    plain = lambda *arrays: [(v, None) for v in arrays]
    blocks = [mine, mine2, got, got2]
    bits = list(range(n_blk.bit_length() - 1))
    orders = [bits, [1, 0] + bits[2:]]
    down_order, up_order = ([0, 2, 1], [1, 0, 2]) if len(bits) == 3 else (bits, bits)
    mlp_halves = split_weight_grads(
        flags,
        [
            ([(v, 0) for v in blocks], plain(mlp_grad, mlp_grad_oth, mg_c, mg_c2)),
            (plain(hidden2, hidden2_oth, hid_c, hid_c2), [(v, 1) for v in blocks]),
        ],
        n_blk, [[(0, width, down_order)], [(0, width, up_order)]], [], "mlp_grads",
    )
    hid_recv, *mlp_halves = lax.optimization_barrier((hid_recv, *mlp_halves))

    resid_grad, branch_grad, do_keep, do_send, mid_sums = branch_back(
        flags, hid_own, hid_recv, cotangent, resid, branch, mid_mods, proj_weight, lay
    )
    mlp_sums = [CubeSum(*mlp_halves[:2], n_blk, down_order), CubeSum(*mlp_halves[2:], n_blk, up_order)]
    for part in mlp_sums:
        part.move()
    do_recv = swap_side(do_send)
    mlp_own, mlp_oth = forward_rows(flags, mine, send, mine2, after(send2, do_send), down_weight)
    do_recv, mlp_own, mlp_oth = lax.optimization_barrier((do_recv, mlp_own, mlp_oth))
    do_long = jnp.where(own_long_b, do_keep, do_recv)
    if parts > 1:
        hot = (jnp.arange(parts) == (blk // 2) % parts)[:, None, None, None]
        do_sent = jnp.where(hot, do_long[None], 0).reshape((n_blk,) + do_long.shape[1:])
    else:
        do_sent = do_long
    do_all = spread(do_sent)
    dq_s, mine_s, theirs_s = attend_back(
        flags, qkv_short, short_oth, [do_keep, do_recv], ot_short, lse_short, tab_cos, tab_sin, short_cos, short_sin, lay, False
    )
    branch_grad_oth = swap_side(after(branch_grad, do_recv))
    mlp_recv = swap_side(after(mlp_oth, branch_grad_oth))
    do_all, dq_s, mine_s, theirs_s, branch_grad_oth, mlp_sums[0].got, mlp_sums[1].got = lax.optimization_barrier(
        (do_all, dq_s, mine_s, theirs_s, branch_grad_oth, mlp_sums[0].got, mlp_sums[1].got)
    )
    for part in mlp_sums:
        part.add()
    do_all, mlp_sums[0].send, mlp_sums[1].send = lax.optimization_barrier((do_all, mlp_sums[0].send, mlp_sums[1].send))
    for part in mlp_sums:
        part.move()

    dq_l, mine_l, theirs_l = attend_back(
        flags, long_own, long_oth, [do_all], ot_long, lse_long, tab_cos, tab_sin, long_cos, long_sin, lay, True
    )
    theirs_l, mlp_sums[0].got, mlp_sums[1].got = lax.optimization_barrier(
        (swap_core(theirs_l), mlp_sums[0].got, mlp_sums[1].got)
    )
    grads_sent = finish_keys(flags, dq_l, mine_l, theirs_l, tab_cos, tab_sin, long_cos, long_sin, lay, True)
    grads_all = spread(grads_sent)
    if parts > 1:
        grads_long = jnp.sum(grads_all.astype(F32).reshape((parts, heads) + grads_all.shape[1:]), axis=0).astype(BF)
    else:
        grads_long = grads_all

    theirs_s = swap_core(theirs_s)
    branch_grad_oth, dq_s, theirs_s, mlp_sums[0].got, mlp_sums[1].got, _ = lax.optimization_barrier(
        (branch_grad_oth, dq_s, theirs_s, mlp_sums[0].got, mlp_sums[1].got, grads_sent)
    )
    for part in mlp_sums:
        part.add()
    hidS, hidS_low, gmS, gtS, abS, sumS = qkv_back(
        flags, [dq_s, mine_s, theirs_s, tab_cos, tab_sin, short_cos, short_sin], tokens, tok_oth, attn_weight, lay, False
    )
    proj_part = head_weight_grads(flags, out_long, out_short, branch_grad, branch_grad_oth, lay).reshape(2, -1, width)
    proj_got = swap_core(jnp.where(core == 0, proj_part[1], proj_part[0]))
    h1_core = swap_core(hidden1)
    gtS_got = swap_core(gtS)
    grads_long, hidS_low, mlp_sums[0].send, mlp_sums[1].send = lax.optimization_barrier(
        (grads_long, hidS_low, mlp_sums[0].send, mlp_sums[1].send)
    )
    for part in mlp_sums:
        part.move()

    hidL, hidL_low, gmL, gtL, abL, sumL = qkv_back(flags, [grads_long], tokens, tok_oth, attn_weight, lay, True)
    gtL_got = swap_core(gtL)
    hid1_recv = swap_side(jnp.where(own_long_b, hidS_low, hidL_low))
    quarter = 3 * width // n_uly
    split = 2 * quarter // 3
    halves = split_weight_grads(
        flags,
        [([(hidden1, 0), (hidden1, 1), (h1_core, 0), (h1_core, 1)], plain(gmL, gmS, gtL_got, gtS_got))],
        n_blk, [[(0, split, orders[0]), (split, quarter - split, orders[1])]], [proj_part, proj_got], "attn_grads",
    )
    hid1_recv, mlp_recv, mlp_sums[0].got, mlp_sums[1].got, *halves = lax.optimization_barrier(
        (hid1_recv, mlp_recv, mlp_sums[0].got, mlp_sums[1].got, *halves)
    )
    attn_sums = [CubeSum(*halves[2 * k : 2 * k + 2], n_blk, order) for k, order in enumerate(orders)]
    for part in attn_sums:
        part.move()
    token_grad = token_back(flags, hidL, hidS, hid1_recv, tokens, resid_grad, first_mod, lay)
    output, gate2_sums = layer_output(flags, mlp_own, mlp_recv, down_bias.astype(F32)[None], resid, cotangent, gate2)
    gate2_sums, token_grad, *gots = lax.optimization_barrier((gate2_sums, token_grad, *[part.got for part in attn_sums]))
    pack = pack_rows(flags, n_blk, mid_sums, gate2_sums, silu, down_b, (bm, bm2, bt, bt2), sumL, sumS, abL, abS)
    many = spread(pack)
    for part, got in zip(attn_sums, gots):
        part.got = got
        part.add()
        part.move()
    many, *gots = lax.optimization_barrier((many, *[part.got for part in attn_sums]))
    both = swap_side(many)
    for part, got in zip(attn_sums, gots):
        part.got = got
        part.add()
        part.move()
    for part in mlp_sums:
        part.add()
    down_mine, up_mine = mlp_sums[0].finish(), mlp_sums[1].finish().astype(BF)
    both, down_mine, up_mine, *gots = lax.optimization_barrier((both, down_mine, up_mine, *[part.got for part in attn_sums]))
    for part, got in zip(attn_sums, gots):
        part.got = got
    both = jnp.stack([many, both])
    g_mod_weight, sums = modulation_grads(
        flags, long_rows, both.reshape(-1, width), swap_core(both).reshape(-1, width), row_out, "modulation_grads"
    )
    for part in attn_sums:
        part.add()
    attn_mine = [part.finish() for part in attn_sums]
    attn_rows = width // n_blk
    head = proj_part.shape[1] // n_blk
    proj_mine = jnp.concatenate(
        [attn_mine[1][attn_rows + k * head : attn_rows + (k + 1) * head] for k in range(width // (quarter - split))], axis=1
    )
    attn_mine = [part[:attn_rows].astype(BF) for part in attn_mine]

    quarters = jnp.concatenate([up_mine] + attn_mine, axis=1)
    quarters = lax.all_to_all(quarters.reshape(n_uly, row_out, -1), "uly", 0, 0, tiled=True)
    ff = up_weight.shape[1]

    g = ff // (n_blk * n_uly)

    def down_home(index):
        b, u = divmod(index, n_uly)
        start = ((b * g // LANES) * n_uly + u) * LANES + (b * g) % LANES
        return start // g

    down_map = [(i, down_home(i)) for i in range(n_blk * n_uly)]
    g_down_weight = down_mine.astype(F32)
    if any(a != b for a, b in down_map):
        g_down_weight = lax.ppermute(g_down_weight, ("blk", "uly"), down_map)
    proj_map = [(b * n_uly + u, u * n_blk + b) for b in range(n_blk) for u in range(n_uly)]
    g_proj_weight = lax.ppermute(proj_mine.astype(F32), ("blk", "uly"), proj_map)


    def cut(vector, size):
        return lax.dynamic_slice_in_dim(vector, dev * size, size, 0)

    total_dev = n_blk * n_uly
    whole_sum = jnp.sum(sums, axis=0)
    mod_line = jnp.concatenate([whole_sum[14:16] + whole_sum[18:20], whole_sum[16:18] + whole_sum[20:22], whole_sum[0:8]], axis=0)
    g_mod_bias = cut(mod_line.reshape(6, 2, width).sum(axis=1).reshape(-1), 6 * width // total_dev)
    g_down_bias = cut(whole_sum[10], width // total_dev)
    g_proj_bias = cut(whole_sum[11], width // total_dev)
    first = dev * g
    steps = (first // LANES) % n_uly ^ uly
    core_step, side_step = steps % 2, steps // 2
    up_mine_sum = sums[2 * core_step + side_step, 12] + sums[2 * (1 - core_step) + side_step, 13]
    g_up_bias = lax.dynamic_slice_in_dim(up_mine_sum, first // (LANES * n_uly) * LANES + first % LANES, g, 0)
    by_step = (sums[0:2, 22:24] + sums[2:4, 22:24]).reshape(2, 2 * width)[:, : 3 * width // 2]
    by_side = jnp.where(side == 0, by_step, by_step[::-1])
    g_attn_bias = cut(jnp.swapaxes(by_side.reshape(2, 3, width // 2), 0, 1).reshape(-1), 3 * width // total_dev)
    quarters, g_mod_bias, g_down_bias, g_proj_bias, g_up_bias, g_attn_bias, g_down_weight = lax.optimization_barrier(
        (quarters, g_mod_bias, g_down_bias, g_proj_bias, g_up_bias, g_attn_bias, g_down_weight)
    )
    g_up_weight, g_attn_weight = lay_out_rows(flags, quarters, ff // n_uly, ff, "lay_out_rows")
    return (
        output, token_grad, g_mod_weight, g_mod_bias, g_attn_weight, g_attn_bias,
        g_proj_weight, g_proj_bias, g_up_weight, g_up_bias, g_down_weight, g_down_bias,
    )


def solution(mesh):
    row = P(("blk", "uly"), None)
    flat = P(("blk", "uly"))
    in_specs = (row, row, row) + (P(),) * 12
    out_specs = (row, row, row, flat, row, flat, row, flat, row, flat, row, flat)
    return jax.shard_map(on_device, mesh=mesh, in_specs=in_specs, out_specs=out_specs, check_vma=False)
```

```python
import functools
import math

import jax
import jax.numpy as jnp
import numpy as np
from jax import lax
from jax.experimental import pallas as pl
from jax.experimental.pallas import tpu as pltpu
from jax.sharding import PartitionSpec as P

DH = 64
GRID = 10
FB = 8
PATCH = 100
HALF = 64
LANES = 128

GELU_C = 0.7978845608028654
GELU_K = 0.044715
NEG_BIG = -1e30
MIB = 1 << 20
UNROLL = 8
PACK = 24

BF = jnp.bfloat16
F32 = jnp.float32


def round_up(value, step):
    return -(-value // step) * step


def lane_low(shape):
    return lax.broadcasted_iota(jnp.int32, shape, len(shape) - 1) < HALF


def first_frame(shape):
    return lax.broadcasted_iota(jnp.int32, shape, 0) < PATCH


def swap_halves(value):
    return pltpu.roll(value, HALF, 1)


def swap_pairs(value):
    even = lax.broadcasted_iota(jnp.int32, value.shape, 1) % 2 == 0
    return jnp.where(even, pltpu.roll(value, LANES - 1, 1), pltpu.roll(value, 1, 1))


def per_frame(shape, first, second):
    return jnp.where(first_frame(shape), jnp.broadcast_to(first, shape), jnp.broadcast_to(second, shape))


def frame_sums(value):
    head = first_frame(value.shape)
    one = jnp.sum(jnp.where(head, value, 0.0), axis=0, keepdims=True)
    two = jnp.sum(jnp.where(head, 0.0, value), axis=0, keepdims=True)
    return one, two


def norm_rows(values):
    center = values - jnp.mean(values, axis=-1, keepdims=True)
    inv_std = lax.rsqrt(jnp.mean(center * center, axis=-1, keepdims=True) + 1e-06)
    return center * inv_std, inv_std


def norm_back(grad, normed, inv_std):
    return inv_std * (
        grad
        - jnp.mean(grad, axis=-1, keepdims=True)
        - normed * jnp.mean(grad * normed, axis=-1, keepdims=True)
    )


def dot(left, right):
    return jnp.dot(left, right, preferred_element_type=F32)


def dot_lanes(left, right):
    return lax.dot_general(left, right, (((1,), (1,)), ((), ())), preferred_element_type=F32)


def dot_rows(left, right):
    return lax.dot_general(left, right, (((0,), (0,)), ((), ())), preferred_element_type=F32)


def split_pair(value, rows_top):
    rows = value.shape[0]
    top = value[:rows_top]
    bottom = jnp.concatenate(
        [value[rows_top:], jnp.zeros((2 * rows_top - rows, LANES), value.dtype)], axis=0
    )
    low = lane_low(top.shape)
    return jnp.where(low, top, swap_halves(bottom)), jnp.where(low, swap_halves(top), bottom)


def join_pair(one, two, rows):
    rows_top = one.shape[0]
    low = lane_low(one.shape)
    top = jnp.where(low, one, swap_halves(two))
    bottom = jnp.where(low, swap_halves(one), two)
    return jnp.concatenate([top, bottom[: rows - rows_top]], axis=0)


def smem():
    return pl.BlockSpec(memory_space=pltpu.SMEM)


def whole(shape):
    return pl.BlockSpec(shape, lambda *_: (0,) * len(shape))


def kernel_call(body, flags, args, outs, *, specs=None, out_specs=None, grid=(1,), scratch=(), vmem=16, pins=(), out_pins=(), aliases=None, flops, name):
    specs = specs or [None] * len(args)
    out_specs = out_specs or [None] * len(outs)
    return pl.pallas_call(
        body,
        grid_spec=pltpu.PrefetchScalarGridSpec(
            num_scalar_prefetch=1,
            grid=grid,
            in_specs=[spec or whole(a.shape) for spec, a in zip(specs, args)],
            out_specs=[spec or whole(o.shape) for spec, o in zip(out_specs, outs)],
            scratch_shapes=list(scratch),
        ),
        out_shape=[pltpu.HBM(o.shape, o.dtype) if k in out_pins else o for k, o in enumerate(outs)],
        input_output_aliases=aliases or {},
        compiler_params=pltpu.CompilerParams(vmem_limit_bytes=vmem * MIB),
        cost_estimate=pl.CostEstimate(flops=flops // 4096, bytes_accessed=4096, transcendentals=0),
        name=name,
    )(flags, *[pltpu.with_memory_space_constraint(a, pltpu.HBM) if a.size >= MIB or k in pins else a for k, a in enumerate(args)])


def shape_of(dims, dtype):
    return jax.ShapeDtypeStruct(dims, dtype)


def tokens_to_qkv(flags, tok_own, tok_oth, mods, weight, bias, tab_cos, tab_sin, time_cos, time_sin, lay):
    rows, width = tok_own.shape
    cols = lay.heads * DH

    def body(flag_ref, own_ref, oth_ref, mod_ref, w_ref, b_ref, tc_ref, ts_ref, qc_ref, qs_ref, hid_ref, long_ref, short_ref, both_ref):
        step = pl.program_id(0)
        own_long = flag_ref[0]

        @pl.when(step == 0)
        def _():
            hidden = []
            for src, base in ((own_ref, 0), (oth_ref, 2)):
                normed, _ = norm_rows(src[...].astype(F32))
                shift = per_frame(normed.shape, mod_ref[base : base + 1, :width], mod_ref[base + 1 : base + 2, :width])
                scale = per_frame(
                    normed.shape, mod_ref[base : base + 1, width : 2 * width], mod_ref[base + 1 : base + 2, width : 2 * width]
                )
                hidden.append(normed * (1.0 + scale) + shift)
            swapped = own_long == 0
            first = jnp.where(swapped, hidden[1], hidden[0])
            second = jnp.where(swapped, hidden[0], hidden[1])
            hid_ref[0] = first.astype(BF)
            hid_ref[1] = second.astype(BF)
            both_ref[...] = jnp.concatenate([first, second], axis=0).astype(BF)

        result = dot(both_ref[...], w_ref[...]) + b_ref[...]
        for slot, out_ref in ((0, long_ref), (1, short_ref)):
            acc = result[slot * rows : (slot + 1) * rows]

            def rotated(pair):
                value = acc[:, pair * LANES : (pair + 1) * LANES]
                cosine = tc_ref[...] + per_frame(value.shape, qc_ref[2 * slot : 2 * slot + 1], qc_ref[2 * slot + 1 : 2 * slot + 2])
                sine = ts_ref[...] + per_frame(value.shape, qs_ref[2 * slot : 2 * slot + 1], qs_ref[2 * slot + 1 : 2 * slot + 2])
                return value * cosine + swap_pairs(value) * sine

            @pl.when(step == 0)
            def _():
                for pair in range(cols // LANES):
                    turned = rotated(pair)
                    out_ref[2 * pair, :rows, :HALF] = turned[:, :HALF].astype(BF)
                    out_ref[2 * pair + 1, :rows, :HALF] = swap_halves(turned)[:, :HALF].astype(BF)

            @pl.when(step == 1)
            def _():
                for pair in range(cols // LANES):
                    turned = rotated(pair)
                    out_ref[2 * pair, :rows, HALF:] = swap_halves(turned)[:, HALF:].astype(BF)
                    out_ref[2 * pair + 1, :rows, HALF:] = turned[:, HALF:].astype(BF)

            @pl.when(step == 2)
            def _():
                for pair in range(cols // LANES):
                    one, two = split_pair(acc[:, pair * LANES : (pair + 1) * LANES], lay.top)
                    out_ref[2 * pair, lay.vrow :, :] = one.astype(BF)
                    out_ref[2 * pair + 1, lay.vrow :, :] = two.astype(BF)

    packed = (lay.heads, lay.vrow + lay.top, LANES)
    return kernel_call(
        body,
        flags,
        [tok_own, tok_oth, mods, weight, bias, tab_cos, tab_sin, time_cos, time_sin],
        [shape_of((2, rows, width), BF), shape_of(packed, BF), shape_of(packed, BF)],
        specs=[
            None, None, None,
            pl.BlockSpec((width, cols), lambda j, f: (0, 2 * j + f[1])),
            pl.BlockSpec((1, cols), lambda j, f: (0, 2 * j + f[1])),
            None, None, None, None,
        ],
        scratch=[pltpu.VMEM((2 * rows, width), BF)],
        out_pins=(0,),
        grid=(3,),
        flops=12 * rows * width * cols,
        name="tokens_to_qkv",
    )


def unpack_values(ref, at, lay):
    part = ref[at, lay.vrow :, :].astype(F32)
    return jnp.concatenate([part, swap_halves(part)[: lay.rows - lay.top]], axis=0)


def hundreds(value):
    return (value * 1311) >> 17


def diag_mask(keys, queries, core):
    key = hundreds(lax.broadcasted_iota(jnp.int32, (keys, 1), 0)) ^ (2 * core)
    query = hundreds(lax.broadcasted_iota(jnp.int32, (1, queries), 1))
    query = ((query & 2) << 1) + (query & 1) + 2 * core
    return key <= query


def load_keys(own_ref, oth_ref, group, lay):
    low = lane_low((lay.rows, LANES))
    halves = [
        jnp.where(low, unpack_values(ref, group, lay), ref[group, : lay.rows, :].astype(F32))
        for ref in (own_ref, oth_ref)
    ]
    return jnp.concatenate(halves, axis=0)


def load_query(own_ref, at, lay):
    value = swap_halves(own_ref[at, : lay.rows, :].astype(F32)) * (1.0 / math.sqrt(DH))
    return jnp.where(lane_low(value.shape), 0.0, value)


def load_rows(load, groups):
    return jnp.concatenate([load(g) for g in groups], axis=0)


def fold_rows(value, op):
    return op(value.reshape(value.shape[0] // 8, 8, value.shape[1]), axis=0)


def unpack_rows(ref, at, lay):
    packed = ref[at].astype(F32)
    grad = jnp.concatenate([packed, swap_halves(packed)[: lay.rows - lay.top]], axis=0)
    return jnp.where(lane_low(grad.shape), grad, 0.0)


def attend(flags, own, oth, lay, long_clip):
    groups = own.shape[0]
    parts = lay.parts if long_clip else 1
    per = 2 if long_clip else 1
    count = groups // per
    keys, queries = 2 * lay.rows * per, lay.rows * per
    depth = count if long_clip else UNROLL

    def body(flag_ref, own_ref, oth_ref, o_ref, ot_ref, lse_ref, kv_ref, vt_ref, st_ref):
        core = flag_ref[2]
        part = flag_ref[3]

        def prepare(tile, slot):
            rows = jnp.concatenate([load_keys(own_ref, oth_ref, per * tile + k, lay) for k in range(per)], axis=0)
            kv_ref[slot] = rows.astype(BF)
            vt_ref[slot] = rows.T[:HALF].astype(BF)

        def block(at, slot):
            query = load_rows(lambda g: load_query(own_ref, g, lay), [per * at + k for k in range(per)]).astype(BF)

            def scores(kt, top):
                score = dot_lanes(kv_ref[kt], query)
                st_ref[kt] = score
                return jnp.maximum(top, fold_rows(score, jnp.max))

            top = jnp.full((8, queries), NEG_BIG, F32)
            if long_clip:
                top = lax.fori_loop(0, at, scores, top)
            score = dot_lanes(kv_ref[slot], query)
            score = jnp.where(diag_mask(keys, queries, core), score, NEG_BIG)
            st_ref[slot] = score
            top = jnp.max(jnp.maximum(top, fold_rows(score, jnp.max)), axis=0, keepdims=True)

            def mix(kt, carry):
                total, acc = carry
                expo = jnp.exp(st_ref[kt] - top)
                total = total + fold_rows(expo, jnp.sum)
                return total, acc + dot(vt_ref[kt], expo.astype(BF))

            zero = (jnp.zeros((8, queries), F32), jnp.zeros((HALF, queries), F32))
            if long_clip:
                total, acc = lax.fori_loop(0, at + 1, mix, zero)
            else:
                total, acc = mix(slot, zero)
            total = jnp.sum(total, axis=0, keepdims=True)
            acc = acc / total
            ot_ref[at] = acc
            lse_ref[at] = jnp.broadcast_to(top + jnp.log(total), (8, queries))
            out = jnp.concatenate([acc, jnp.zeros_like(acc)], axis=0).T
            for k in range(per):
                o_ref[per * at + k] = split_pair(out[k * lay.rows : (k + 1) * lay.rows], lay.top)[0].astype(BF)

        if long_clip:
            def prepare_loop(tile, _):
                prepare(tile, tile)
                return 0

            lax.fori_loop(0, count, prepare_loop, 0)
            if parts > 1:
                o_ref[...] = jnp.zeros_like(o_ref)

            def block_loop(step, _):
                at = step * parts + part if parts > 1 else step
                block(at, at)
                return 0

            lax.fori_loop(0, count // parts, block_loop, 0)
        else:
            def head_loop(step, _):
                for k in range(UNROLL):
                    prepare(UNROLL * step + k, k)
                for k in range(UNROLL):
                    block(UNROLL * step + k, k)
                return 0

            lax.fori_loop(0, count // UNROLL, head_loop, 0)

    pairs = count * (count + 1) // 2 if long_clip else count
    return kernel_call(
        body,
        flags,
        [own, oth],
        [
            shape_of((groups, lay.top, LANES), BF),
            shape_of((count, HALF, queries), F32),
            shape_of((count, 8, queries), F32),
        ],
        scratch=[
            pltpu.VMEM((depth, keys, LANES), BF),
            pltpu.VMEM((depth, HALF, keys), BF),
            pltpu.VMEM((depth, keys, queries), F32),
        ],
        out_pins=(1, 2),
        vmem=max(24, 3 * groups) if long_clip else 16,
        flops=pairs * 16 * keys * queries * DH // parts,
        name="attend_long" if long_clip else "attend_short",
    )


def attend_back(flags, own, oth, d_outs, ot, lse, tab_cos, tab_sin, time_cos, time_sin, lay, long_clip):
    groups = own.shape[0]
    parts = lay.parts if long_clip else 1
    per = 2 if long_clip else 1
    count = groups // per
    keys, queries = 2 * lay.rows * per, lay.rows * per
    depth = count if long_clip else UNROLL

    def body(flag_ref, own_ref, oth_ref, *refs):
        do_refs, refs = refs[: len(d_outs)], refs[len(d_outs) :]
        ot_ref, lse_ref, tc_ref, ts_ref, qc_ref, qs_ref, dq_ref, down_ref, doth_ref, kv_ref, kt_ref, acc_ref = refs
        own_long = flag_ref[0]
        core = flag_ref[2]
        part = flag_ref[3]

        def prepare(tile, slot):
            rows = jnp.concatenate([load_keys(own_ref, oth_ref, per * tile + k, lay) for k in range(per)], axis=0)
            kv_ref[slot] = rows.astype(BF)
            kt_ref[slot] = rows.T[HALF:].astype(BF)
            if long_clip:
                acc_ref[slot] = jnp.zeros((keys, LANES), F32)

        def block(at, slot):
            members = [per * at + k for k in range(per)]
            query = load_rows(lambda g: load_query(own_ref, g, lay), members).astype(BF)
            if long_clip:
                grad = load_rows(lambda g: unpack_rows(do_refs[0], g, lay), members)
            else:
                grad = load_rows(
                    lambda g: jnp.where(own_long == 1, unpack_rows(do_refs[1], g, lay), unpack_rows(do_refs[0], g, lay)), members
                )
            delta = jnp.sum(grad.T[:HALF] * ot_ref[at], axis=0, keepdims=True)
            grad = grad.astype(BF)
            lse_row = lse_ref[at][0:1]

            def tile_back(kt, acc, diag):
                tile = kv_ref[kt]
                prob = jnp.exp(dot_lanes(tile, query) - lse_row)
                if diag:
                    prob = jnp.where(diag_mask(keys, queries, core), prob, 0.0)
                score_grad = (prob * (dot_lanes(tile, grad) - delta)).astype(BF)
                both = dot(score_grad, query) + dot(prob.astype(BF), grad)
                if long_clip:
                    acc_ref[kt] += both
                else:
                    acc_ref[kt] = both
                return acc + dot(kt_ref[kt], score_grad)

            acc = tile_back(slot, jnp.zeros((HALF, queries), F32), True)
            if long_clip:
                acc = lax.fori_loop(0, at, lambda kt, a: tile_back(kt, a, False), acc)
            acc = acc * (1.0 / math.sqrt(DH))
            turned = jnp.concatenate([acc, jnp.zeros_like(acc)], axis=0).T
            for k, group in enumerate(members):
                dq = turned[k * lay.rows : (k + 1) * lay.rows]
                tab = group if long_clip else 0
                cosine = tc_ref[...] + per_frame(dq.shape, qc_ref[2 * tab], qc_ref[2 * tab + 1])
                sine = ts_ref[...] + per_frame(dq.shape, qs_ref[2 * tab], qs_ref[2 * tab + 1])
                dq_ref[group] = (dq * cosine - swap_pairs(dq) * sine).astype(BF)

        def flush(tile, slot):
            for k in range(per):
                down_ref[per * tile + k] = acc_ref[slot, 2 * k * lay.rows : (2 * k + 1) * lay.rows].astype(BF)
                doth_ref[per * tile + k] = acc_ref[slot, (2 * k + 1) * lay.rows : (2 * k + 2) * lay.rows].astype(BF)

        if long_clip:
            def prepare_loop(tile, _):
                prepare(tile, tile)
                return 0

            lax.fori_loop(0, count, prepare_loop, 0)
            if parts > 1:
                dq_ref[...] = jnp.zeros_like(dq_ref)

            def block_loop(step, _):
                at = step * parts + part if parts > 1 else step
                block(at, at)
                return 0

            lax.fori_loop(0, count // parts, block_loop, 0)

            def flush_loop(tile, _):
                flush(tile, tile)
                return 0

            lax.fori_loop(0, count, flush_loop, 0)
        else:
            def head_loop(step, _):
                for k in range(UNROLL):
                    prepare(UNROLL * step + k, k)
                for k in range(UNROLL):
                    block(UNROLL * step + k, k)
                for k in range(UNROLL):
                    flush(UNROLL * step + k, k)
                return 0

            lax.fori_loop(0, count // UNROLL, head_loop, 0)

    pairs = count * (count + 1) // 2 if long_clip else count
    return kernel_call(
        body,
        flags,
        [own, oth, *d_outs, ot, lse, tab_cos, tab_sin, time_cos, time_sin],
        [
            shape_of((groups, lay.rows, LANES), BF),
            shape_of((groups, lay.rows, LANES), BF),
            shape_of((groups, lay.rows, LANES), BF),
        ],
        scratch=[
            pltpu.VMEM((depth, keys, LANES), BF),
            pltpu.VMEM((depth, HALF, keys), BF),
            pltpu.VMEM((depth, keys, LANES), F32),
        ],
        out_pins=(0, 1),
        vmem=max(24, 3 * groups) if long_clip else 20,
        pins=(0, 1) + tuple(range(2 + len(d_outs), 8 + len(d_outs))),
        flops=pairs * 40 * keys * queries * DH // parts,
        name="attend_back_long" if long_clip else "attend_back_short",
    )


def finish_keys(flags, dq, mine, theirs, tab_cos, tab_sin, time_cos, time_sin, lay, long_clip):
    groups = dq.shape[0]

    def body(flag_ref, dq_ref, a_ref, b_ref, tc_ref, ts_ref, qc_ref, qs_ref, out_ref):
        def one(group, _):
            both = a_ref[group].astype(F32) + b_ref[group].astype(F32)
            tab = group if long_clip else 0
            cosine = tc_ref[...] + per_frame(both.shape, qc_ref[2 * tab], qc_ref[2 * tab + 1])
            sine = ts_ref[...] + per_frame(both.shape, qs_ref[2 * tab], qs_ref[2 * tab + 1])
            keys = both * cosine - swap_pairs(both) * sine
            out_ref[group, : lay.rows, :] = jnp.where(lane_low(keys.shape), dq_ref[group].astype(F32), keys).astype(BF)
            out_ref[group, lay.vrow :, :] = split_pair(both, lay.top)[0].astype(BF)
            return 0

        lax.fori_loop(0, groups, one, 0)

    return kernel_call(
        body,
        flags,
        [dq, mine, theirs, tab_cos, tab_sin, time_cos, time_sin],
        [shape_of((groups, lay.vrow + lay.top, LANES), BF)],
        pins=(0, 1),
        vmem=max(16, groups),
        flops=groups * lay.rows * LANES * 10,
        name="finish_keys",
    )[0]


def project_and_norm(flags, long_out, short_out, recv, weight, bias, tokens, mods, lay):
    rows, width = tokens.shape
    half = lay.heads * DH

    def body(flag_ref, long_ref, short_ref, recv_ref, w_ref, b_ref, tok_ref, mod_ref, branch_ref, resid_ref, hid_ref, att_ref):
        own_long = flag_ref[0]
        side = flag_ref[1]
        for pair in range(lay.heads // 2):
            kept = [
                jnp.where(own_long == 1, long_ref[2 * pair + k].astype(F32), short_ref[2 * pair + k].astype(F32)) for k in (0, 1)
            ]
            got = [recv_ref[2 * pair + k].astype(F32) for k in (0, 1)]
            lanes = slice(pair * LANES, (pair + 1) * LANES)
            att_ref[side, :, lanes] = join_pair(kept[0], kept[1], rows).astype(BF)
            att_ref[1 - side, :, lanes] = join_pair(got[0], got[1], rows).astype(BF)
        branch = dot(att_ref[0], w_ref[:half]) + dot(att_ref[1], w_ref[half:]) + b_ref[...]
        branch_ref[...] = branch
        gate = per_frame(branch.shape, mod_ref[0:1], mod_ref[1:2])
        resid = tok_ref[...].astype(F32) + gate * branch
        resid_ref[...] = resid
        normed, _ = norm_rows(resid)
        shift = per_frame(branch.shape, mod_ref[2:3], mod_ref[3:4])
        scale = per_frame(branch.shape, mod_ref[4:5], mod_ref[5:6])
        hid_ref[...] = (normed * (1.0 + scale) + shift).astype(BF)

    full = shape_of((rows, width), F32)
    return kernel_call(
        body,
        flags,
        [long_out, short_out, recv, weight, bias, tokens, mods],
        [full, full, shape_of((rows, width), BF)],
        scratch=[pltpu.VMEM((2, rows, half), BF)],
        out_pins=(0, 1),
        vmem=24,
        flops=2 * rows * width * width,
        name="project_and_norm",
    )


def hidden_blocks(width, wide, chunks, weight_rows):
    def pick(k):
        def at(i, f):
            block = 2 * (chunks * i + k) + f[1]
            return (block, 0) if weight_rows else (0, block)
        return at

    return [pl.BlockSpec((wide, width) if weight_rows else (width, wide), pick(k)) for k in range(chunks)]


def ahead_grads(flags, mlp_grad, down_weight, name):
    rows, width = mlp_grad.shape
    ff = down_weight.shape[0]
    wide, chunks = 2 * LANES, 2

    def body(flag_ref, mg_ref, *refs):
        out_ref = refs[-1]
        for k in range(chunks):
            out_ref[:, k * wide : (k + 1) * wide] = dot_lanes(mg_ref[...], refs[k][...])

    return kernel_call(
        body,
        flags,
        [mlp_grad] + [down_weight] * chunks,
        [shape_of((rows, ff // 2), F32)],
        specs=[None] + hidden_blocks(width, wide, chunks, True),
        out_specs=[pl.BlockSpec((rows, chunks * wide), lambda i, f: (0, i))],
        out_pins=(0,),
        grid=(ff // (2 * wide * chunks),),
        flops=rows * width * ff,
        name=name,
    )[0]


def hidden_grads(flags, hidden, ahead, up_weight, up_bias, lay, out_dtype, name):
    rows, width = hidden.shape
    ff = up_weight.shape[1]
    wide, chunks = 2 * LANES, 2
    steps = ff // (2 * wide * chunks)
    quarter = ff // 4

    def body(flag_ref, hid_ref, ahead_ref, *refs):
        weights, outs = refs[: 2 * chunks], refs[2 * chunks :]
        mine_ref, send_ref, bm_ref, bt_ref, hg_ref, hacc = outs
        step = pl.program_id(0)
        first = flag_ref[2] == 0
        back = 0.0
        for k in range(chunks):
            up_ref, ub_ref = weights[k], weights[chunks + k]
            pre = dot(hid_ref[...], up_ref[...]) + ub_ref[...]
            tanh = jnp.tanh(GELU_C * (pre + GELU_K * pre * pre * pre))
            act = (0.5 * pre * (1.0 + tanh)).astype(BF)
            slope = 0.5 * (1.0 + tanh) + 0.5 * pre * (1.0 - tanh * tanh) * GELU_C * (1.0 + 3.0 * GELU_K * pre * pre)
            pre_low = (ahead_ref[:, k * wide : (k + 1) * wide] * slope).astype(BF)
            back = back + dot_lanes(pre_low, up_ref[...])
            sums = jnp.sum(pre_low.astype(F32), axis=0, keepdims=True)
            lanes = slice(k * LANES, (k + 1) * LANES)
            for at, value in ((0, act), (1, pre_low)):
                mine_ref[at, :, lanes] = jnp.where(first, value[:, :LANES], value[:, LANES:])
                send_ref[at, :, lanes] = jnp.where(first, value[:, LANES:], value[:, :LANES])
            bm_ref[:, lanes] = jnp.broadcast_to(jnp.where(first, sums[:, :LANES], sums[:, LANES:]), (8, LANES))
            bt_ref[:, lanes] = jnp.broadcast_to(jnp.where(first, sums[:, LANES:], sums[:, :LANES]), (8, LANES))

        @pl.when(step == 0)
        def _():
            hacc[...] = back

        @pl.when(step > 0)
        def _():
            hacc[...] += back

        @pl.when(step == steps - 1)
        def _():
            hg_ref[...] = hacc[...].astype(hg_ref.dtype)

    chunk = pl.BlockSpec((2, rows, chunks * LANES), lambda i, f: (0, 0, i))
    bchunk = pl.BlockSpec((8, chunks * LANES), lambda i, f: (0, i))
    return kernel_call(
        body,
        flags,
        [hidden, ahead] + [up_weight] * chunks + [up_bias] * chunks,
        [shape_of((2, rows, quarter), BF)] * 2 + [shape_of((8, quarter), F32)] * 2 + [shape_of((rows, width), out_dtype)],
        specs=[None, pl.BlockSpec((rows, chunks * wide), lambda i, f: (0, i))]
        + hidden_blocks(width, wide, chunks, False)
        + hidden_blocks(1, wide, chunks, False),
        out_specs=[chunk, chunk, bchunk, bchunk, None],
        grid=(steps,),
        scratch=[pltpu.VMEM((rows, width), F32)],
        pins=(1,),
        flops=2 * rows * width * ff,
        name=name,
    )


def forward_rows(flags, mine, send, mine2, send2, down_weight):
    _, rows, quarter = mine.shape
    ff, width = down_weight.shape
    wide, chunks = 2 * LANES, 2
    steps = ff // (2 * wide * chunks)

    def body(flag_ref, m_ref, s_ref, m2_ref, s2_ref, *refs):
        own_ref, oth_ref, acc_ref = refs[chunks:]
        first = flag_ref[2] == 0
        step = pl.program_id(0)
        for at, (a_ref, b_ref) in enumerate(((m_ref, s_ref), (m2_ref, s2_ref))):
            total = 0.0
            for k in range(chunks):
                lanes = slice(k * LANES, (k + 1) * LANES)
                a, b = a_ref[:, lanes], b_ref[:, lanes]
                act = jnp.concatenate([jnp.where(first, a, b), jnp.where(first, b, a)], axis=1)
                total = total + dot(act, refs[k][...])

            @pl.when(step == 0)
            def _(total=total, at=at):
                acc_ref[at] = total

            @pl.when(step > 0)
            def _(total=total, at=at):
                acc_ref[at] += total

        @pl.when(step == steps - 1)
        def _():
            own_ref[...] = acc_ref[0]
            oth_ref[...] = acc_ref[1].astype(BF)

    chunk = pl.BlockSpec((None, rows, chunks * LANES), lambda i, f: (0, 0, i))
    return kernel_call(
        body,
        flags,
        [mine, send, mine2, send2] + [down_weight] * chunks,
        [shape_of((rows, width), F32), shape_of((rows, width), BF)],
        specs=[chunk] * 4 + hidden_blocks(width, wide, chunks, True),
        scratch=[pltpu.VMEM((2, rows, width), F32)],
        out_pins=(0,),
        grid=(steps,),
        flops=2 * rows * width * ff,
        name="forward_rows",
    )


def scale_cotangent(flags, cotangent, gates):
    rows, width = cotangent.shape

    def body(flag_ref, dy_ref, g_ref, out_ref, sums_ref):
        low = (per_frame((rows, width), g_ref[0:1], g_ref[1:2]) * dy_ref[...].astype(F32)).astype(BF)
        out_ref[...] = low
        sums_ref[...] = jnp.broadcast_to(jnp.sum(low.astype(F32), axis=0, keepdims=True), sums_ref.shape)

    return kernel_call(
        body,
        flags,
        [cotangent, gates],
        [shape_of((rows, width), BF), shape_of((8, width), F32)],
        pins=(0,),
        flops=rows * width,
        name="scale_cotangent",
    )


def layer_output(flags, mlp_own, mlp_recv, bias, resid, cotangent, gates):
    rows, width = resid.shape

    def body(flag_ref, a_ref, b_ref, bias_ref, r_ref, dy_ref, g_ref, out_ref, sums_ref):
        mlp = a_ref[...] + b_ref[...].astype(F32) + bias_ref[...]
        out_ref[...] = (r_ref[...] + per_frame((rows, width), g_ref[0:1], g_ref[1:2]) * mlp).astype(BF)
        sums_ref[0:1], sums_ref[1:2] = frame_sums(dy_ref[...].astype(F32) * mlp)
        sums_ref[2:8] = jnp.zeros((6, width), F32)

    return kernel_call(
        body,
        flags,
        [mlp_own, mlp_recv, bias, resid, cotangent, gates],
        [shape_of((rows, width), BF), shape_of((8, width), F32)],
        pins=(0, 3, 4),
        flops=rows * width * 4,
        name="layer_output",
    )


def pack_rows(flags, n_blk, mid, gate2, silu, down_b, up_sums, sum_long, sum_short, bias_long, bias_short):
    width = mid.shape[1]
    cols = bias_long.shape[1]

    def body(flag_ref, mid_ref, g_ref, s_ref, d_ref, m1, m2, t1, t2, sl, ss, bl, bs, out_ref):
        bias = bl[0:1] + bs[0:1]
        bias = jnp.concatenate([bias, jnp.zeros((1, 2 * width - cols), F32)], axis=1)
        rows = jnp.concatenate(
            [mid_ref[0:6], g_ref[0:2], s_ref[...].astype(F32), d_ref[0:1], mid_ref[6:7], m1[0:1] + m2[0:1], t1[0:1] + t2[0:1],
             sl[0:4], ss[0:4], bias[:, :width], bias[:, width:]],
            axis=0,
        ).astype(BF)
        for k in range(n_blk):
            out_ref[k] = rows

    return kernel_call(
        body,
        flags,
        [mid, gate2, silu, down_b, *up_sums, sum_long, sum_short, bias_long, bias_short],
        [shape_of((n_blk, PACK, width), BF)],
        flops=width * PACK,
        name="pack_rows",
    )[0]


def branch_back(flags, hid_own, hid_recv, cotangent, resid, branch, mods, weight, lay):
    rows, width = resid.shape
    half = lay.heads * DH

    def body(flag_ref, a_ref, b_ref, dy_ref, r_ref, br_ref, mod_ref, w_ref, rg_ref, bg_ref, keep_ref, send_ref, sums_ref):
        side = flag_ref[1]
        hid = a_ref[...] + b_ref[...].astype(F32)
        norm, inv_std = norm_rows(r_ref[...])
        scale = per_frame(hid.shape, mod_ref[4:5], mod_ref[5:6])
        resid = dy_ref[...].astype(F32) + norm_back(hid * (1.0 + scale), norm, inv_std)
        rg_ref[...] = resid
        gate = per_frame(hid.shape, mod_ref[0:1], mod_ref[1:2])
        low = (gate * resid).astype(BF)
        bg_ref[...] = low
        for out_ref, which in ((keep_ref, side), (send_ref, 1 - side)):
            grad = dot_lanes(low, w_ref[pl.ds(pl.multiple_of(which * half, half), half), :])
            for pair in range(lay.heads // 2):
                one, two = split_pair(grad[:, pair * LANES : (pair + 1) * LANES], lay.top)
                out_ref[2 * pair] = one.astype(BF)
                out_ref[2 * pair + 1] = two.astype(BF)
        sums_ref[0:1], sums_ref[1:2] = frame_sums(resid * br_ref[...])
        sums_ref[2:3], sums_ref[3:4] = frame_sums(hid)
        sums_ref[4:5], sums_ref[5:6] = frame_sums(hid * norm)
        sums_ref[6:7] = jnp.sum(low.astype(F32), axis=0, keepdims=True)
        sums_ref[7:8] = jnp.zeros((1, width), F32)

    packed = shape_of((lay.heads, lay.top, LANES), BF)
    return kernel_call(
        body,
        flags,
        [hid_own, hid_recv, cotangent, resid, branch, mods, weight],
        [shape_of((rows, width), F32), shape_of((rows, width), BF), packed, packed, shape_of((8, width), F32)],
        pins=(0, 2, 3, 4, 5),
        out_pins=(0,),
        vmem=24,
        flops=2 * rows * width * width,
        name="branch_back",
    )


def qkv_back(flags, grads, tok_own, tok_oth, weight, lay, is_long):
    rows, width = tok_own.shape
    cols = lay.heads * DH
    half = cols // 2

    def body(flag_ref, *refs):
        g_refs, refs = refs[: len(grads)], refs[len(grads) :]
        own_ref, oth_ref, w_ref, hid_ref, low_ref, gm_ref, gt_ref, bias_ref, sums_ref, q_ref, acc_ref = refs
        step = pl.program_id(0)
        core = flag_ref[2]

        @pl.when(step == 0)
        def _():
            if not is_long:
                dq_ref, a_ref, b_ref, tc_ref, ts_ref, qc_ref, qs_ref = g_refs
                table = (rows, LANES)
                cosine = tc_ref[...] + per_frame(table, qc_ref[0], qc_ref[1])
                sine = ts_ref[...] + per_frame(table, qs_ref[0], qs_ref[1])
            for pair in range(lay.heads // 2):
                lanes = slice(pair * LANES, (pair + 1) * LANES)
                low = lane_low((rows, LANES))
                if is_long:
                    g_ref = g_refs[0]
                    one, two = (g_ref[2 * pair + k, :rows, :].astype(F32) for k in (0, 1))
                    query, key = jnp.where(low, one, swap_halves(two)), jnp.where(low, swap_halves(one), two)
                    value = join_pair(*(g_ref[2 * pair + k, lay.vrow :, :].astype(F32) for k in (0, 1)), rows)
                else:
                    one, two = (dq_ref[2 * pair + k].astype(F32) for k in (0, 1))
                    query = jnp.where(low, one, swap_halves(two))
                    one, two = (a_ref[2 * pair + k].astype(F32) + b_ref[2 * pair + k].astype(F32) for k in (0, 1))
                    value = jnp.where(low, one, swap_halves(two))
                    one, two = (v * cosine - swap_pairs(v) * sine for v in (one, two))
                    key = jnp.where(low, swap_halves(one), two)
                q_ref[0, :, lanes] = query.astype(BF)
                q_ref[1, :, lanes] = key.astype(BF)
                q_ref[2, :, lanes] = value.astype(BF)

        value = q_ref[step]
        part = dot_lanes(value, w_ref[...])

        @pl.when(step == 0)
        def _():
            acc_ref[...] = part

        @pl.when(step > 0)
        def _():
            acc_ref[...] += part

        first = core == 0
        gm_ref[...] = jnp.where(first, value[:, :half], value[:, half:])
        gt_ref[...] = jnp.where(first, value[:, half:], value[:, :half])
        bias_ref[...] = jnp.broadcast_to(jnp.sum(value.astype(F32), axis=0, keepdims=True), bias_ref.shape)

        @pl.when(step == 2)
        def _():
            hid = acc_ref[...]
            hid_ref[...] = hid
            low_ref[...] = hid.astype(BF)
            mine = (flag_ref[0] == 1) if is_long else (flag_ref[0] == 0)
            normed, _ = norm_rows(jnp.where(mine, own_ref[...].astype(F32), oth_ref[...].astype(F32)))
            sums_ref[0:1], sums_ref[1:2] = frame_sums(hid)
            sums_ref[2:3], sums_ref[3:4] = frame_sums(hid * normed)
            sums_ref[4:8] = jnp.zeros((4, width), F32)

    return kernel_call(
        body,
        flags,
        [*grads, tok_own, tok_oth, weight],
        [
            shape_of((rows, width), F32),
            shape_of((rows, width), BF),
            shape_of((rows, 3 * half), BF),
            shape_of((rows, 3 * half), BF),
            shape_of((8, 3 * cols), F32),
            shape_of((8, width), F32),
        ],
        specs=[None] * (len(grads) + 2) + [pl.BlockSpec((width, cols), lambda j, f: (0, 2 * j + f[1]))],
        out_specs=[
            None, None,
            pl.BlockSpec((rows, half), lambda j, f: (0, j)),
            pl.BlockSpec((rows, half), lambda j, f: (0, j)),
            pl.BlockSpec((8, cols), lambda j, f: (0, j)),
            None,
        ],
        pins=(len(grads), len(grads) + 1) + (() if is_long else (0, 1)),
        out_pins=(0,),
        grid=(3,),
        scratch=[pltpu.VMEM((3, rows, cols), BF), pltpu.VMEM((rows, width), F32)],
        flops=6 * rows * width * cols,
        name="qkv_back_long" if is_long else "qkv_back_short",
    )


def token_back(flags, hid_long, hid_short, recv, tokens, resid_grad, mods, lay):
    rows, width = tokens.shape

    def body(flag_ref, l_ref, s_ref, r_ref, tok_ref, rg_ref, mod_ref, out_ref):
        hid = jnp.where(flag_ref[0] == 1, l_ref[...], s_ref[...]) + r_ref[...].astype(F32)
        normed, inv_std = norm_rows(tok_ref[...].astype(F32))
        scale = per_frame(hid.shape, mod_ref[0:1, width : 2 * width], mod_ref[1:2, width : 2 * width])
        out_ref[...] = rg_ref[...] + norm_back(hid * (1.0 + scale), normed, inv_std)

    return kernel_call(
        body,
        flags,
        [hid_long, hid_short, recv, tokens, resid_grad, mods],
        [shape_of((rows, width), F32)],
        pins=(0, 1, 3, 4, 5),
        flops=rows * width * 20,
        name="token_back",
    )[0]


def group_spec(pair, rows, wide, moves):
    index = pair[1]
    if index is None:
        return pl.BlockSpec((rows, wide), lambda i, f: (0, i if moves else 0))
    return pl.BlockSpec((None, rows, wide), lambda i, f: (index, 0, i if moves else 0))


def width_of(jobs):
    return sum(rights[0][0].shape[-1] for _, rights in jobs)


def split_weight_grads(flags, jobs, n_blk, cuts, head_rows, name):
    count = len(jobs[0][0])
    rows, depth = jobs[0][0][0][0].shape[-2:]
    pieces = [(job, *cut) for job, many in enumerate(cuts) for cut in many]
    tall = depth // n_blk
    wide = max(tall, LANES)
    per = wide // tall
    operands = [pair for lefts, rights in jobs for pair in [*lefts, *rights]]
    extra = 0
    if head_rows:
        head = head_rows[0].shape[1] // n_blk
        turns = head_rows[0].shape[2] // cuts[0][-1][1]
        extra = head * turns

    def body(flag_ref, *refs):
        outs = refs[len(operands) + len(head_rows) :]
        step = pl.program_id(0)
        results = []
        for job in range(len(jobs)):
            mine = refs[2 * count * job : 2 * count * (job + 1)]
            acc = dot_rows(mine[0][...], mine[count][...])
            for k in range(1, count):
                acc += dot_rows(mine[k][...], mine[count + k][...])
            results.append(acc.astype(BF))
        for member in range(per):
            place = relative_place(step * per + member, flag_ref[4], n_blk)
            if head_rows:
                part_ref, got_ref = refs[len(operands) : len(operands) + 2]
                at = pl.ds(pl.multiple_of((step * per + member) * head, head), head)
                both = (part_ref[flag_ref[2], at].astype(F32) + got_ref[at].astype(F32)).astype(BF)
            for out, (job, start, cols, order) in enumerate(pieces):
                sent, at = half_place(place, order)
                values = [results[job][member * tall : (member + 1) * tall, start : start + cols]]
                if head_rows and out == len(pieces) - 1:
                    values += [both[:, turn * cols : (turn + 1) * cols] for turn in range(turns)]

                def store(out_ref, values=values, at=at):
                    row = 0
                    for value in values:
                        out_ref[at, row : row + value.shape[0]] = value
                        row += value.shape[0]

                pl.when(sent == 1)(functools.partial(store, outs[2 * out]))
                pl.when(sent == 0)(functools.partial(store, outs[2 * out + 1]))

    specs = []
    for lefts, rights in jobs:
        specs += [group_spec(pair, rows, wide, True) for pair in lefts]
        specs += [group_spec(pair, rows, pair[0].shape[-1], False) for pair in rights]
    outs = []
    for out, (job, start, cols, order) in enumerate(pieces):
        outs += [shape_of((n_blk // 2, tall + (extra if out == len(pieces) - 1 else 0), cols), BF)] * 2
    return kernel_call(
        body,
        flags,
        [array for array, _ in operands] + list(head_rows),
        outs,
        specs=specs + [None] * len(head_rows),
        grid=(depth // wide,),
        vmem=24,
        pins=(0, 1, 2, 3, 5, 7) if head_rows else (),
        flops=2 * count * rows * depth * width_of(jobs),
        name=name,
    )


def head_weight_grads(flags, longs, shorts, grad_own, grad_oth, lay):
    rows, width = grad_own.shape
    pairs = lay.heads // 2

    def body(flag_ref, l_ref, s_ref, go_ref, gt_ref, out_ref):
        own_long = flag_ref[0] == 1
        grads = jnp.where(own_long, go_ref[...], gt_ref[...]), jnp.where(own_long, gt_ref[...], go_ref[...])
        for pair in range(pairs):
            acc = 0.0
            for ref, grad in zip((l_ref, s_ref), grads):
                left = join_pair(ref[2 * pair].astype(F32), ref[2 * pair + 1].astype(F32), rows).astype(BF)
                acc = acc + dot_rows(left, grad)
            out_ref[pair * LANES : (pair + 1) * LANES, :] = acc.astype(BF)

    return kernel_call(
        body,
        flags,
        [longs, shorts, grad_own, grad_oth],
        [shape_of((lay.heads * DH, width), BF)],
        pins=(0, 1),
        flops=4 * rows * width * lay.heads * DH,
        name="head_weight_grads",
    )[0]


def relative_place(target, here, n_blk):
    relative = target ^ here
    return relative ^ ((relative >> 1) & (10 & (n_blk - 1)))


def half_place(place, order):
    at = 0
    for bit in order[1:]:
        at = 2 * at + ((place >> bit) & 1)
    return (place >> order[0]) & 1, at


def hop_of(bit):
    return (1 << bit) if bit == 0 or bit % 2 == 1 else (1 << bit) | (1 << (bit - 1))


class CubeSum:
    def __init__(self, send, keep, n_blk, order):
        self.n_blk, self.order, self.at = n_blk, order, 0
        self.bits = n_blk.bit_length() - 1
        self.send, self.keep, self.value, self.got = send, keep, None, None

    def move(self, *starts):
        hop = hop_of(self.order[self.at])
        send = after(self.send, *starts) if starts else self.send
        self.got = lax.ppermute(send, "blk", [(i, i ^ hop) for i in range(self.n_blk)])

    def add(self):
        self.at += 1
        half = self.keep.shape[0] // 2
        if self.at == self.bits:
            self.value = (self.keep.astype(F32) + self.got.astype(F32))[0]
        else:
            low = [(self.keep[k].astype(F32) + self.got[k].astype(F32)).astype(BF) for k in (slice(half), slice(half, None))]
            self.keep, self.send = low

    def finish(self):
        while self.at < self.bits:
            self.move()
            self.add()
        return self.value


def lay_out_rows(flags, gathered, split, ff, name):
    n_uly, rows, total = gathered.shape
    cols = (total - split) // 3

    def body(flag_ref, in_ref, up_ref, attn_ref):
        for u in range(n_uly):
            for i in range(split // LANES):
                at = (i * n_uly + u) * LANES
                up_ref[:, at : at + LANES] = in_ref[u, :, i * LANES : (i + 1) * LANES].astype(F32)
            for j in range(3):
                at = (j * n_uly + u) * cols
                attn_ref[:, at : at + cols] = in_ref[u, :, split + j * cols : split + (j + 1) * cols].astype(F32)

    return kernel_call(
        body,
        flags,
        [gathered],
        [shape_of((rows, ff), F32), shape_of((rows, 3 * n_uly * cols), F32)],
        flops=rows * total,
        name=name,
    )


def modulation_grads(flags, long_rows, mine, got, row_out, name):
    half, width = mine.shape
    total = 2 * half
    quarter = total // 4

    def body(flag_ref, long_ref, mine_ref, got_ref, out_ref, sums_ref, part_ref, g_ref):
        g_ref[:half] = mine_ref[...]
        g_ref[half:] = got_ref[...]
        start = flag_ref[5]
        block = pl.multiple_of((start // LANES) * LANES, LANES)
        silu = g_ref[:, pl.ds(block, LANES)].astype(F32)
        parts = [silu[k * quarter : (k + 1) * quarter] for k in (1, 0, 3, 2)]
        mate = jnp.concatenate(parts, axis=0)
        own_long = long_ref[...] > 0.5

        def place_of(index):
            return index - PACK * ((index * 2731) >> 16)

        place = place_of(lax.broadcasted_iota(jnp.int32, (total, LANES), 0))

        def aligned(value, base):
            return jnp.where((place == base) | (place == base + 1), pltpu.roll(value, (base - 8) % total, 0), 0.0)

        def owner(base, is_long):
            return jnp.where(own_long == is_long, aligned(silu, base), aligned(mate, base))

        lefts = [
            owner(14, True) + owner(18, False),
            owner(16, True) + owner(20, False),
            aligned(silu, 0),
            aligned(silu, 2),
            aligned(silu, 4),
            aligned(silu, 6),
        ]
        for k, left in enumerate(lefts):
            part_ref[...] = dot_rows(left.astype(BF), g_ref[...])
            out_ref[:, k * width : (k + 1) * width] = part_ref[pl.ds(pl.multiple_of(start - block, row_out), row_out), :]
        row = lax.broadcasted_iota(jnp.int32, (32, quarter), 0)
        which = jnp.where(row == place_of(lax.broadcasted_iota(jnp.int32, (32, quarter), 1)), 1.0, 0.0).astype(BF)
        for u in range(4):
            sums_ref[u] = dot(which, g_ref[u * quarter : (u + 1) * quarter, :])

    return kernel_call(
        body,
        flags,
        [long_rows, mine, got],
        [shape_of((row_out, 6 * width), F32), shape_of((4, 32, width), F32)],
        scratch=[pltpu.VMEM((LANES, width), F32), pltpu.VMEM((total, width), BF)],
        vmem=max(20, 20 * total // 768),
        flops=total * width * LANES * 12,
        name=name,
    )


def after(value, *earlier):
    return lax.optimization_barrier((value,) + earlier)[0]


def rotary_static(frames):
    n_time, n_row = DH // 8, 3 * DH // 16
    cosine = np.zeros((frames * PATCH, LANES), np.float32)
    sine = np.zeros((frames * PATCH, LANES), np.float32)
    patch = np.arange(frames * PATCH) % PATCH
    for group, place in ((0, patch // GRID), (1, patch % GRID)):
        for j in range(n_row):
            freq = np.exp(np.float32(-math.log(10000.0)) * np.float32(j) / np.float32(n_row)).astype(np.float32)
            angle = (place.astype(np.float32) * freq).astype(np.float64)
            pair = n_time + group * n_row + j
            for head in (0, HALF):
                cosine[:, head + 2 * pair] = np.cos(angle)
                cosine[:, head + 2 * pair + 1] = np.cos(angle)
                sine[:, head + 2 * pair] = -np.sin(angle)
                sine[:, head + 2 * pair + 1] = np.sin(angle)
    return cosine, sine


def rotary_time(times):
    n_time = DH // 8
    lane = jnp.arange(LANES, dtype=jnp.int32)
    pair = (lane % HALF) // 2
    freq = jnp.exp(-math.log(10000.0) * pair.astype(F32) / float(n_time))
    angle = times.astype(F32)[:, None] * freq[None, :]
    live = (pair < n_time)[None, :]
    sign = jnp.where(lane % 2 == 0, -1.0, 1.0)[None, :]
    return jnp.where(live, jnp.cos(angle), 0.0), jnp.where(live, sign * jnp.sin(angle), 0.0)


class Layout:
    def __init__(self, rows, heads, parts):
        self.rows = rows
        self.heads = heads
        self.parts = parts
        self.top = round_up(-(-rows // 2), 16)
        self.vrow = round_up(rows, 16)


def on_device(
    tokens, cotangent, noise_embed, frame_clip, frame_index, mod_weight, mod_bias, attn_weight, attn_bias,
    proj_weight, proj_bias, up_weight, up_bias, down_weight, down_bias,
):
    n_uly = lax.axis_size("uly")
    n_blk = lax.axis_size("blk")
    blk = lax.axis_index("blk")
    uly = lax.axis_index("uly")
    rows, width = tokens.shape
    frames = noise_embed.shape[0]
    side, core = uly // 2, uly % 2
    heads = width // DH // 2
    parts = n_blk // heads
    lay = Layout(rows, heads, parts)
    dev = blk * n_uly + uly

    def swap_side(value):
        return lax.ppermute(value, "uly", [(i, i ^ 2) for i in range(n_uly)])

    def swap_core(value):
        return lax.ppermute(value, "uly", [(i, i ^ 1) for i in range(n_uly)])

    def spread(value):
        return lax.all_to_all(value, "blk", split_axis=0, concat_axis=0, tiled=True)

    long_first = frame_clip[::FB] == n_blk
    own_long_b = lax.dynamic_index_in_dim(long_first, blk, 0, False) == (side == 0)
    own_long = own_long_b.astype(jnp.int32)
    row_out = width // (n_blk * n_uly)
    flags = jnp.stack([own_long, side, core, blk // heads, blk, dev * row_out]).astype(jnp.int32)

    tok_oth = swap_side(tokens)
    silu = jax.nn.silu(noise_embed.astype(F32)).astype(BF)
    bias = mod_bias.astype(F32)
    first_mod = dot(silu, mod_weight[:, : 2 * width]) + bias[: 2 * width]
    first_mods = jnp.concatenate([first_mod, swap_side(first_mod)], axis=0)
    rest_mod = dot(after(silu, first_mod), mod_weight[:, 2 * width :]) + bias[2 * width :]

    block_time = frame_index.reshape(n_blk, FB)
    head_time, tail_time = block_time[:, : FB // 2], block_time[:, FB // 2 :]
    long_times = lax.dynamic_slice_in_dim(jnp.where(long_first[:, None], head_time, tail_time), core * frames, frames, 1)
    short_times = lax.dynamic_slice_in_dim(jnp.where(long_first[:, None], tail_time, head_time), core * frames, frames, 1)
    short_times = lax.dynamic_index_in_dim(short_times, blk, 0, False)
    time_cos, time_sin = rotary_time(jnp.concatenate([lax.dynamic_index_in_dim(long_times, blk, 0, False), short_times]))
    long_cos, long_sin = rotary_time(long_times.reshape(-1))
    short_cos, short_sin = time_cos[frames:, None], time_sin[frames:, None]
    long_cos, long_sin = long_cos[:, None], long_sin[:, None]
    tab_cos, tab_sin = (jnp.asarray(t) for t in rotary_static(frames))
    own_long_all = (long_first[None, :] == ((side ^ jnp.arange(2)) == 0)[:, None]).astype(F32)
    long_rows = jnp.broadcast_to(own_long_all[None, :, :, None, None], (2, 2, n_blk, PACK, LANES)).reshape(-1, LANES)
    first_mods, rest_mod, long_cos, long_sin, short_cos, short_sin, long_rows = lax.optimization_barrier(
        (first_mods, rest_mod, long_cos, long_sin, short_cos, short_sin, long_rows)
    )

    gate2 = rest_mod[:, 3 * width :]
    mid_mods = jnp.concatenate([rest_mod[:, :width], rest_mod[:, width : 2 * width], rest_mod[:, 2 * width : 3 * width]], axis=0)
    mid_mods = jnp.concatenate([mid_mods, jnp.zeros((2, width), F32)], axis=0)
    hidden1, qkv_long, qkv_short = tokens_to_qkv(
        flags, tokens, tok_oth, first_mods, attn_weight, attn_bias.astype(F32)[None], tab_cos, tab_sin, time_cos, time_sin, lay
    )
    sent = jnp.concatenate([qkv_long] * parts, axis=0) if parts > 1 else qkv_long
    long_own = spread(sent)
    short_oth = swap_core(qkv_short)
    out_short, ot_short, lse_short = attend(flags, qkv_short, short_oth, lay, False)
    mlp_grad, down_b = scale_cotangent(flags, after(cotangent, qkv_long), gate2)
    mlp_grad_oth = swap_side(mlp_grad)
    ahead_own = ahead_grads(flags, mlp_grad, down_weight, "ahead_own")
    long_own, out_short, mlp_grad, ahead_own = lax.optimization_barrier((long_own, out_short, mlp_grad, ahead_own))
    long_oth = swap_core(long_own)
    out_long_all, ot_long, lse_long = attend(flags, long_own, long_oth, lay, True)
    out_long_all, mlp_grad_oth = lax.optimization_barrier((out_long_all, mlp_grad_oth))

    def own_part(value):
        if parts == 1:
            return value
        return lax.dynamic_slice_in_dim(value, ((blk // 2) % parts) * heads, heads, 0)

    ahead_oth = ahead_grads(flags, mlp_grad_oth, down_weight, "ahead_other")
    out_long = own_part(spread(out_long_all))
    out_long, ahead_oth = lax.optimization_barrier((out_long, ahead_oth))
    out_recv = swap_side(jnp.where(own_long_b, out_short, out_long))
    branch, resid, hidden2 = project_and_norm(
        flags, out_long, out_short, out_recv, proj_weight, proj_bias.astype(F32)[None], tokens, mid_mods, lay
    )

    hidden2_oth = swap_side(hidden2)
    up_b = up_bias.astype(F32)[None]
    mine, send, bm, bt, hid_own = hidden_grads(flags, hidden2, ahead_own, up_weight, up_b, lay, F32, "hidden_own")
    hidden2_oth, hid_own = lax.optimization_barrier((hidden2_oth, hid_own))
    mine2, send2, bm2, bt2, hid_oth = hidden_grads(flags, hidden2_oth, ahead_oth, up_weight, up_b, lay, BF, "hidden_other")
    hid_recv = swap_side(hid_oth)

    got, got2 = swap_core(send), swap_core(send2)
    hid_c, hid_c2, mg_c, mg_c2 = (swap_core(v) for v in (hidden2, hidden2_oth, mlp_grad, mlp_grad_oth))
    plain = lambda *arrays: [(v, None) for v in arrays]
    blocks = [mine, mine2, got, got2]
    bits = list(range(n_blk.bit_length() - 1))
    orders = [bits, [1, 0] + bits[2:]]
    down_order, up_order = ([0, 1, 2], [1, 2, 0]) if len(bits) == 3 else (bits, bits)
    mlp_halves = split_weight_grads(
        flags,
        [
            ([(v, 0) for v in blocks], plain(mlp_grad, mlp_grad_oth, mg_c, mg_c2)),
            (plain(hidden2, hidden2_oth, hid_c, hid_c2), [(v, 1) for v in blocks]),
        ],
        n_blk, [[(0, width, down_order)], [(0, width, up_order)]], [], "mlp_grads",
    )
    hid_recv, *mlp_halves = lax.optimization_barrier((hid_recv, *mlp_halves))

    resid_grad, branch_grad, do_keep, do_send, mid_sums = branch_back(
        flags, hid_own, hid_recv, cotangent, resid, branch, mid_mods, proj_weight, lay
    )
    mlp_sums = [CubeSum(*mlp_halves[:2], n_blk, down_order), CubeSum(*mlp_halves[2:], n_blk, up_order)]
    for part in mlp_sums:
        part.move()
    do_recv = swap_side(do_send)
    mlp_own, mlp_oth = forward_rows(flags, mine, send, mine2, after(send2, do_send), down_weight)
    do_recv, mlp_own, mlp_oth = lax.optimization_barrier((do_recv, mlp_own, mlp_oth))
    do_long = jnp.where(own_long_b, do_keep, do_recv)
    if parts > 1:
        hot = (jnp.arange(parts) == (blk // 2) % parts)[:, None, None, None]
        do_sent = jnp.where(hot, do_long[None], 0).reshape((n_blk,) + do_long.shape[1:])
    else:
        do_sent = do_long
    do_all = spread(do_sent)
    dq_s, mine_s, theirs_s = attend_back(
        flags, qkv_short, short_oth, [do_keep, do_recv], ot_short, lse_short, tab_cos, tab_sin, short_cos, short_sin, lay, False
    )
    branch_grad_oth = swap_side(after(branch_grad, do_recv))
    mlp_recv = swap_side(after(mlp_oth, branch_grad_oth))
    do_all, dq_s, mine_s, theirs_s, branch_grad_oth, mlp_sums[0].got, mlp_sums[1].got = lax.optimization_barrier(
        (do_all, dq_s, mine_s, theirs_s, branch_grad_oth, mlp_sums[0].got, mlp_sums[1].got)
    )
    for part in mlp_sums:
        part.add()
    do_all, mlp_sums[0].send, mlp_sums[1].send = lax.optimization_barrier((do_all, mlp_sums[0].send, mlp_sums[1].send))
    for part in mlp_sums:
        part.move()

    dq_l, mine_l, theirs_l = attend_back(
        flags, long_own, long_oth, [do_all], ot_long, lse_long, tab_cos, tab_sin, long_cos, long_sin, lay, True
    )
    theirs_l, mlp_sums[0].got, mlp_sums[1].got = lax.optimization_barrier(
        (swap_core(theirs_l), mlp_sums[0].got, mlp_sums[1].got)
    )
    grads_sent = finish_keys(flags, dq_l, mine_l, theirs_l, tab_cos, tab_sin, long_cos, long_sin, lay, True)
    grads_all = spread(grads_sent)
    if parts > 1:
        grads_long = jnp.sum(grads_all.astype(F32).reshape((parts, heads) + grads_all.shape[1:]), axis=0).astype(BF)
    else:
        grads_long = grads_all

    theirs_s = swap_core(theirs_s)
    branch_grad_oth, dq_s, theirs_s, mlp_sums[0].got, mlp_sums[1].got, _ = lax.optimization_barrier(
        (branch_grad_oth, dq_s, theirs_s, mlp_sums[0].got, mlp_sums[1].got, grads_sent)
    )
    for part in mlp_sums:
        part.add()
    hidS, hidS_low, gmS, gtS, abS, sumS = qkv_back(
        flags, [dq_s, mine_s, theirs_s, tab_cos, tab_sin, short_cos, short_sin], tokens, tok_oth, attn_weight, lay, False
    )
    proj_part = head_weight_grads(flags, out_long, out_short, branch_grad, branch_grad_oth, lay).reshape(2, -1, width)
    proj_got = swap_core(jnp.where(core == 0, proj_part[1], proj_part[0]))
    h1_core = swap_core(hidden1)
    gtS_got = swap_core(gtS)
    grads_long, hidS_low, mlp_sums[0].send, mlp_sums[1].send = lax.optimization_barrier(
        (grads_long, hidS_low, mlp_sums[0].send, mlp_sums[1].send)
    )
    for part in mlp_sums:
        part.move()

    hidL, hidL_low, gmL, gtL, abL, sumL = qkv_back(flags, [grads_long], tokens, tok_oth, attn_weight, lay, True)
    gtL_got = swap_core(gtL)
    hid1_recv = swap_side(jnp.where(own_long_b, hidS_low, hidL_low))
    quarter = 3 * width // n_uly
    split = 2 * quarter // 3
    halves = split_weight_grads(
        flags,
        [([(hidden1, 0), (hidden1, 1), (h1_core, 0), (h1_core, 1)], plain(gmL, gmS, gtL_got, gtS_got))],
        n_blk, [[(0, split, orders[0]), (split, quarter - split, orders[1])]], [proj_part, proj_got], "attn_grads",
    )
    hid1_recv, mlp_recv, mlp_sums[0].got, mlp_sums[1].got, *halves = lax.optimization_barrier(
        (hid1_recv, mlp_recv, mlp_sums[0].got, mlp_sums[1].got, *halves)
    )
    attn_sums = [CubeSum(*halves[2 * k : 2 * k + 2], n_blk, order) for k, order in enumerate(orders)]
    for part in attn_sums:
        part.move()
    token_grad = token_back(flags, hidL, hidS, hid1_recv, tokens, resid_grad, first_mod, lay)
    output, gate2_sums = layer_output(flags, mlp_own, mlp_recv, down_bias.astype(F32)[None], resid, cotangent, gate2)
    gate2_sums, token_grad, *gots = lax.optimization_barrier((gate2_sums, token_grad, *[part.got for part in attn_sums]))
    pack = pack_rows(flags, n_blk, mid_sums, gate2_sums, silu, down_b, (bm, bm2, bt, bt2), sumL, sumS, abL, abS)
    many = spread(pack)
    for part, got in zip(attn_sums, gots):
        part.got = got
        part.add()
        part.move()
    many, *gots = lax.optimization_barrier((many, *[part.got for part in attn_sums]))
    both = swap_side(many)
    for part, got in zip(attn_sums, gots):
        part.got = got
        part.add()
        part.move()
    for part in mlp_sums:
        part.add()
    down_mine, up_mine = mlp_sums[0].finish(), mlp_sums[1].finish().astype(BF)
    both, down_mine, up_mine, *gots = lax.optimization_barrier((both, down_mine, up_mine, *[part.got for part in attn_sums]))
    for part, got in zip(attn_sums, gots):
        part.got = got
    both = jnp.stack([many, both])
    g_mod_weight, sums = modulation_grads(
        flags, long_rows, both.reshape(-1, width), swap_core(both).reshape(-1, width), row_out, "modulation_grads"
    )
    for part in attn_sums:
        part.add()
    attn_mine = [part.finish() for part in attn_sums]
    attn_rows = width // n_blk
    head = proj_part.shape[1] // n_blk
    proj_mine = jnp.concatenate(
        [attn_mine[1][attn_rows + k * head : attn_rows + (k + 1) * head] for k in range(width // (quarter - split))], axis=1
    )
    attn_mine = [part[:attn_rows].astype(BF) for part in attn_mine]

    quarters = jnp.concatenate([up_mine] + attn_mine, axis=1)
    quarters = lax.all_to_all(quarters.reshape(n_uly, row_out, -1), "uly", 0, 0, tiled=True)
    ff = up_weight.shape[1]

    g = ff // (n_blk * n_uly)

    def down_home(index):
        b, u = divmod(index, n_uly)
        start = ((b * g // LANES) * n_uly + u) * LANES + (b * g) % LANES
        return start // g

    down_map = [(i, down_home(i)) for i in range(n_blk * n_uly)]
    g_down_weight = down_mine.astype(F32)
    if any(a != b for a, b in down_map):
        g_down_weight = lax.ppermute(g_down_weight, ("blk", "uly"), down_map)
    proj_map = [(b * n_uly + u, u * n_blk + b) for b in range(n_blk) for u in range(n_uly)]
    g_proj_weight = lax.ppermute(proj_mine.astype(F32), ("blk", "uly"), proj_map)


    def cut(vector, size):
        return lax.dynamic_slice_in_dim(vector, dev * size, size, 0)

    total_dev = n_blk * n_uly
    whole_sum = jnp.sum(sums, axis=0)
    mod_line = jnp.concatenate([whole_sum[14:16] + whole_sum[18:20], whole_sum[16:18] + whole_sum[20:22], whole_sum[0:8]], axis=0)
    g_mod_bias = cut(mod_line.reshape(6, 2, width).sum(axis=1).reshape(-1), 6 * width // total_dev)
    g_down_bias = cut(whole_sum[10], width // total_dev)
    g_proj_bias = cut(whole_sum[11], width // total_dev)
    first = dev * g
    steps = (first // LANES) % n_uly ^ uly
    core_step, side_step = steps % 2, steps // 2
    up_mine_sum = sums[2 * core_step + side_step, 12] + sums[2 * (1 - core_step) + side_step, 13]
    g_up_bias = lax.dynamic_slice_in_dim(up_mine_sum, first // (LANES * n_uly) * LANES + first % LANES, g, 0)
    by_step = (sums[0:2, 22:24] + sums[2:4, 22:24]).reshape(2, 2 * width)[:, : 3 * width // 2]
    by_side = jnp.where(side == 0, by_step, by_step[::-1])
    g_attn_bias = cut(jnp.swapaxes(by_side.reshape(2, 3, width // 2), 0, 1).reshape(-1), 3 * width // total_dev)
    quarters, g_mod_bias, g_down_bias, g_proj_bias, g_up_bias, g_attn_bias, g_down_weight = lax.optimization_barrier(
        (quarters, g_mod_bias, g_down_bias, g_proj_bias, g_up_bias, g_attn_bias, g_down_weight)
    )
    g_up_weight, g_attn_weight = lay_out_rows(flags, quarters, ff // n_uly, ff, "lay_out_rows")
    return (
        output, token_grad, g_mod_weight, g_mod_bias, g_attn_weight, g_attn_bias,
        g_proj_weight, g_proj_bias, g_up_weight, g_up_bias, g_down_weight, g_down_bias,
    )


def solution(mesh):
    row = P(("blk", "uly"), None)
    flat = P(("blk", "uly"))
    in_specs = (row, row, row) + (P(),) * 12
    out_specs = (row, row, row, flat, row, flat, row, flat, row, flat, row, flat)
    return jax.shard_map(on_device, mesh=mesh, in_specs=in_specs, out_specs=out_specs, check_vma=False)
```
